32 devices in a mesh: row: 4 (over y, x), col: 4 (over z), layer: 2 (over core).
Axes of the slice: x: 2, y: 2, z: 4, core: 2. Of those that a mesh axis runs over, the one named last changes fastest.
Arguments:
- x_blocks: bfloat16 [4, 4, 28, 128, 128], P('col', 'row'), may hold values from -1.75 to 1.75
- slot_rows: int32 [4, 4, 28], replicated, may hold values from 0 to 27, as said below
- slot_cols: int32 [4, 4, 28], replicated, may hold values from 0 to 27, as said below
Outputs:
- c_blocks: bfloat16 [4, 4, 28, 128, 128], P('col', 'row', 'layer')
The draws below stay inside these ranges and needn't reach their ends.
Inputs may be any that keep to these rules, and one draw needn't show every extreme that they name: In every tile the pairs (slot_rows, slot_cols) are distinct; exactly 7 local rows hold 2 stored blocks, 14 local rows hold one, the others none. slot_cols[a, b, s] is slot_rows[a, b, s] or slot_rows[a, b, s] + 1, modulo 28; a row with two stored blocks has both.
All inputs are finite; a program needn't handle non-finite values.
Results may differ from the reference program's by a relative error of at most 0.001.
Values may be sent and summed in bfloat16 or wider, within the bound.
No kernel may reach another device: no remote copies, remote signals or barrier semaphores. Data moves between devices by JAX's collectives and lax.ppermute only.
A program may use at most 64 MiB of HBM per device.

```python
import jax
import jax.numpy as jnp
from jax import lax

BLK = 128
TB = 28
MB = 2
SLOTS = 28
HALF = 2
N_ROW = 4
N_COL = 4


def tile_pattern(key):
    first_key, second_key, third_key = jax.random.split(key, 3)
    ordering = jax.random.permutation(first_key, TB).astype(jnp.int32)
    doubles = ordering[:TB // 4]
    singles = ordering[TB // 4:3 * TB // 4]
    rows_all = jnp.concatenate([doubles, doubles, singles])
    single_offsets = jax.random.randint(second_key, (TB // 2,), 0, 2).astype(jnp.int32)
    offsets = jnp.concatenate([jnp.zeros((TB // 4,), jnp.int32), jnp.ones((TB // 4,), jnp.int32), single_offsets])
    cols_all = (rows_all + offsets) % TB
    shuffle = jax.random.permutation(third_key, TB)
    return (rows_all[shuffle], cols_all[shuffle])


def both_patterns(key):
    base_key = jax.random.fold_in(key, 7)
    tile_keys = jax.random.split(base_key, N_COL * N_ROW)
    rows_all, cols_all = jax.vmap(tile_pattern)(tile_keys)
    return (rows_all.reshape(N_COL, N_ROW, TB), cols_all.reshape(N_COL, N_ROW, TB))


def draw_slot_rows(key, part):
    return both_patterns(key)[0]


def draw_slot_cols(key, part):
    return both_patterns(key)[1]


def steps_of(rng, shape, cuts, smallest, high):
    level, own = 1.0, jax.random.fold_in(rng, 6)
    for dim, blocks in cuts:
        draws = jnp.exp(jax.random.uniform(jax.random.fold_in(own, dim), (blocks,), jnp.float32, smallest / len(cuts), high / len(cuts)))
        level = level * jnp.repeat(draws, shape[dim] // blocks).reshape([-1 if axis == dim else 1 for axis in range(len(shape))])
    return level


def centred(stream_key, shape, width, most, pieces=(), kind=jnp.bfloat16):
    array = width * jax.random.normal(stream_key, shape, jnp.float32)
    if pieces:
        array = array * steps_of(stream_key, shape, pieces, -0.22, 0.18)
    return jnp.clip(array, -most, most).astype(kind)


def setup_inputs(seed: int = 0) -> dict:
    streams_of = jax.random.split(jax.random.key(seed), 4)
    return {
        "x_blocks": centred(streams_of[0], (N_COL, N_ROW, SLOTS, BLK, BLK), (BLK ** -0.25), 1.75, ((0, 4), (1, 4))),
        "slot_rows": draw_slot_rows(jax.random.fold_in(streams_of[3], 71), 0),
        "slot_cols": draw_slot_cols(jax.random.fold_in(streams_of[3], 71), 0),
    }


def candidates(a_cols, b_rows):
    matches = (a_cols[:, None] == b_rows[None, :]).astype(jnp.int32)
    ranking = jnp.cumsum(matches, axis=1) * matches
    chosen_slots = []
    present = []
    for position in range(MB):
        chosen = (ranking == position + 1).astype(jnp.int32)
        present.append(jnp.max(chosen, axis=1) > 0)
        chosen_slots.append(jnp.argmax(chosen, axis=1).astype(jnp.int32))
    return chosen_slots, present


def tile_terms(a_blocks, a_rows, a_cols, b_blocks, b_rows, b_cols, out_rows, out_cols):
    slot_count = a_blocks.shape[0]
    chosen_slots, present = candidates(a_cols, b_rows)
    out_keys = out_rows * TB + out_cols
    products = []
    targets = []
    for position in range(MB):
        picked = chosen_slots[position]
        pair_keys = a_rows * TB + b_cols[picked]
        equal = (pair_keys[:, None] == out_keys[None, :]).astype(jnp.int32)
        landed = (jnp.max(equal, axis=1) > 0) & present[position]
        target = jnp.where(landed, jnp.argmax(equal, axis=1).astype(jnp.int32), slot_count)
        products.append(jnp.einsum("sij,sjk->sik", a_blocks.astype(jnp.float32), b_blocks[picked].astype(jnp.float32)))
        targets.append(target.astype(jnp.int32))
    summed = jax.ops.segment_sum(jnp.concatenate(products), jnp.concatenate(targets), num_segments=slot_count + 1)
    return summed[:slot_count]


def reference(x_blocks, slot_rows, slot_cols):
    grid_size = N_COL
    slot_count = x_blocks.shape[2]
    width_block = x_blocks.shape[3]

    def one_tile(tile_index):
        row_class = tile_index // grid_size
        col_class = tile_index % grid_size
        accumulated = jnp.zeros((slot_count, width_block, width_block), jnp.float32)
        for shift_value in range(-HALF, HALF):
            middle = (row_class + shift_value) % grid_size
            accumulated = accumulated + tile_terms(
                x_blocks[row_class, middle], slot_rows[row_class, middle], slot_cols[row_class, middle],
                x_blocks[middle, col_class], slot_rows[middle, col_class], slot_cols[middle, col_class],
                slot_rows[row_class, col_class], slot_cols[row_class, col_class])
        return accumulated.astype(jnp.bfloat16)

    result = lax.map(one_tile, jnp.arange(grid_size * grid_size, dtype=jnp.int32))
    return result.reshape(grid_size, grid_size, slot_count, width_block, width_block)
```

```python
import functools

import jax
import jax.numpy as jnp
from jax import lax
from jax.experimental import pallas as pl
from jax.experimental.pallas import tpu as pltpu
from jax.sharding import PartitionSpec as P

TB = 28
GROUP = 4
CHUNKS = 2


class Plan:
    def __init__(self, mesh):
        self.grid = mesh.shape["row"]
        self.half = min(6, self.grid) // 2
        self.whole = 2 * self.half == self.grid
        self.stages = self.grid - 1 if self.whole else self.half

    def shift(self, a, l):
        if self.whole:
            return l - a
        mid = self.grid // 2
        k = (l - a + mid) % self.grid - mid
        return k if -self.half <= k < self.half else None

    def hop_pairs(self, stage):
        pairs = []
        for source in range(self.grid):
            for layer, step in ((0, 1), (1, -1)):
                target = source + step
                origin = target - step * stage
                if self.whole and not (0 <= target < self.grid and 0 <= origin < self.grid):
                    continue
                target %= self.grid
                if self.shift(target, origin % self.grid) == -step * stage:
                    pairs.append((source * 2 + layer, target * 2 + layer))
        return pairs

    def row_pairs(self, by):
        pairs = []
        for r in range(self.grid):
            for a in range(self.grid):
                k = self.shift(a, r)
                if k is not None:
                    layer = int(k > 0)
                    target = (r + by) % self.grid
                    pairs.append(
                        tuple((p * self.grid + a) * 2 + layer for p in (r, target))
                    )
        return pairs

    def taken(self, a, layer, stage):
        l = jnp.where(layer == 0, a - stage, a + stage)
        if self.whole:
            valid = (l >= 0) & (l < self.grid)
        else:
            valid = jnp.where(layer == 0, stage <= self.half, stage < self.half)
        if stage == 0:
            valid = valid & (layer == 0)
        l = jnp.where(l < 0, l + self.grid, l)
        return jnp.where(l >= self.grid, l - self.grid, l), valid


def list_pairs(rows, cols, a, l, b, valid, pos, pairs, stage):
    slots = rows.shape[2]

    def clear(i, carry):
        pos[i] = 0
        return carry

    lax.fori_loop(0, 4 * TB, clear, 0, unroll=8)

    def place(s, carry):
        ra = rows[a, l, s]
        pos[2 * ra + (cols[a, l, s] != ra).astype(jnp.int32)] = s + 1
        rb = rows[l, b, s]
        pos[2 * TB + 2 * rb + (cols[l, b, s] != rb).astype(jnp.int32)] = s + 1
        return carry

    lax.fori_loop(0, slots, place, 0, unroll=4)

    def collect(u, count):
        r = rows[a, b, u]
        d = (cols[a, b, u] != r).astype(jnp.int32)
        left, right = pos[2 * r], pos[2 * TB + 2 * r + d]
        pairs[stage, count] = ((left - 1) * 64 + (right - 1)) * 64 + u
        count = count + ((left > 0) & (right > 0)).astype(jnp.int32)
        after = jnp.where(r + 1 == TB, 0, r + 1)
        left, right = pos[2 * r + 1], pos[2 * TB + 2 * after]
        pairs[stage, count] = ((left - 1) * 64 + (right - 1)) * 64 + u
        return count + ((left > 0) & (right > 0) & (d == 1)).astype(jnp.int32)

    count = lax.fori_loop(0, slots, collect, jnp.int32(0), unroll=2)
    count = jnp.where(valid, count, 0)
    for extra in range(GROUP - 1):
        pairs[stage, count + extra] = slots
    return count


def add_products(count, pairs, stage, left, right, acc):
    def step(i, carry):
        codes = [pairs[stage, i * GROUP + j] for j in range(GROUP)]
        products = [
            jnp.dot(
                left[stage, code // 4096],
                right[stage, (code // 64) % 64],
                preferred_element_type=jnp.float32,
            )
            for code in codes
        ]
        for code, product in zip(codes, products):
            acc[code % 64] += product
        return carry

    lax.fori_loop(0, (count + GROUP - 1) // GROUP, step, 0)


def load_tiles(plan, stages, a, b, layer, lefts, rights, left, right, sem):
    waits = []
    for i, stage in enumerate(stages):
        l, _ = plan.taken(a, layer, stage)
        by = b - l
        by = jnp.where(by < 0, by + plan.grid, by)
        for n, ref in enumerate(lefts):

            @pl.when(by == n)
            def _(ref=ref):
                pltpu.make_async_copy(ref, left.at[i], sem.at[i, 0]).start()

        copies = [pltpu.make_async_copy(lefts[0], left.at[i], sem.at[i, 0])]
        at = 0
        for j, ref in enumerate(rights[i]):
            copy = pltpu.make_async_copy(
                ref, right.at[i, pl.ds(at, ref.shape[0])], sem.at[i, 1 + j]
            )
            copy.start()
            copies.append(copy)
            at += ref.shape[0]
        waits.append(copies)
    return waits


def early_kernel(plan, parts, rows, cols, *refs):
    stages = range(plan.stages)
    lefts = refs[: plan.grid]
    refs = refs[plan.grid :]
    rights = []
    for n in parts:
        rights.append(refs[:n])
        refs = refs[n:]
    out, left, right, acc, pos, pairs, sem, out_sem = refs
    a, b, layer = (lax.axis_index(n) for n in ("col", "row", "layer"))
    waits = load_tiles(plan, stages, a, b, layer, lefts, rights, left, right, sem)
    acc[...] = jnp.zeros_like(acc)
    for i, stage in enumerate(stages):
        l, valid = plan.taken(a, layer, stage)
        count = list_pairs(rows, cols, a, l, b, valid, pos, pairs, i)
        for copy in waits[i]:
            copy.wait()
        add_products(count, pairs, i, left, right, acc)
    copy = pltpu.make_async_copy(acc.at[pl.ds(0, out.shape[0])], out, out_sem)
    copy.start()
    copy.wait()


def last_kernel(plan, parts, rows, cols, total, *refs):
    lefts, rights = refs[: plan.grid], refs[plan.grid : plan.grid + parts]
    mine, other, left, right, acc, pos, pairs, sem, io_sem = refs[plan.grid + parts :]
    a, b, layer = (lax.axis_index(n) for n in ("col", "row", "layer"))
    held = pltpu.make_async_copy(total, acc.at[pl.ds(0, total.shape[0])], io_sem.at[0])
    held.start()
    waits = load_tiles(
        plan, [plan.stages], a, b, layer, lefts, [rights], left, right, sem
    )
    l, valid = plan.taken(a, layer, plan.stages)
    count = list_pairs(rows, cols, a, l, b, valid, pos, pairs, 0)
    held.wait()
    for copy in waits[0]:
        copy.wait()
    add_products(count, pairs, 0, left, right, acc)
    share = mine.shape[0]
    sent = pltpu.make_async_copy(
        acc.at[pl.ds((1 - layer) * share, share)], other, io_sem.at[0]
    )
    kept = pltpu.make_async_copy(
        acc.at[pl.ds(layer * share, share)], mine, io_sem.at[1]
    )
    sent.start()
    kept.start()
    sent.wait()
    kept.wait()


def scratch(tile, stages, parts):
    slots, size = tile.shape[0], tile.shape[1]
    return [
        pltpu.VMEM((stages, *tile.shape), tile.dtype),
        pltpu.VMEM((stages, *tile.shape), tile.dtype),
        pltpu.VMEM((slots + 1, size, size), jnp.float32),
        pltpu.SMEM((4 * TB,), jnp.int32),
        pltpu.SMEM((stages, 2 * slots + GROUP), jnp.int32),
        pltpu.SemaphoreType.DMA((stages, 1 + parts)),
    ]


def on_device(plan, x_blocks, slot_rows, slot_cols):
    own = x_blocks[0, 0]
    slots, size = own.shape[0], own.shape[1]
    share = slots // 2
    bounds = [slots * i // CHUNKS for i in range(CHUNKS + 1)]
    held = [own[i:j] for i, j in zip(bounds[:-1], bounds[1:])]
    rights = [[own]]
    for stage in range(1, plan.stages + 1):
        pairs = plan.hop_pairs(stage)
        held = [lax.ppermute(part, ("col", "layer"), pairs) for part in held]
        rights.append(held)
    lefts = [own] + [
        lax.ppermute(own, ("row", "col", "layer"), plan.row_pairs(by))
        for by in range(1, plan.grid)
    ]
    anywhere = pl.BlockSpec(memory_space=pl.ANY)
    scalars = pl.BlockSpec(memory_space=pltpu.SMEM)
    parts = [len(r) for r in rights[:-1]]
    early = [part for stage in rights[:-1] for part in stage]
    tile_bytes = own.size * 2
    total = pl.pallas_call(
        functools.partial(early_kernel, plan, parts),
        out_shape=jax.ShapeDtypeStruct((slots, size, size), jnp.float32),
        in_specs=[scalars] * 2 + [anywhere] * (plan.grid + len(early)),
        out_specs=anywhere,
        scratch_shapes=scratch(own, plan.stages, CHUNKS)
        + [pltpu.SemaphoreType.DMA],
        cost_estimate=pl.CostEstimate(
            flops=2 * size**3 * slots * plan.stages,
            bytes_accessed=(2 * plan.stages + 2) * tile_bytes,
            transcendentals=0,
        ),
        name="early_products",
    )(slot_rows, slot_cols, *lefts, *early)
    half = jax.ShapeDtypeStruct((share, size, size), jnp.float32)
    mine, other = pl.pallas_call(
        functools.partial(last_kernel, plan, CHUNKS),
        out_shape=(half, half),
        in_specs=[scalars] * 2 + [anywhere] * (1 + plan.grid + CHUNKS),
        out_specs=(anywhere, anywhere),
        scratch_shapes=scratch(own, 1, CHUNKS) + [pltpu.SemaphoreType.DMA((2,))],
        cost_estimate=pl.CostEstimate(
            flops=2 * size**3 * slots,
            bytes_accessed=6 * tile_bytes,
            transcendentals=0,
        ),
        name="last_products",
    )(slot_rows, slot_cols, total, *lefts, *rights[-1])
    received = lax.ppermute(other, "layer", [(0, 1), (1, 0)])
    return (mine + received).astype(jnp.bfloat16)[None, None]


def solution(mesh):
    in_specs = (P("col", "row", None, None, None), P(), P())
    out_specs = P("col", "row", "layer", None, None)
    return jax.shard_map(
        functools.partial(on_device, Plan(mesh)),
        mesh=mesh,
        in_specs=in_specs,
        out_specs=out_specs,
        check_vma=False,
    )
```

```python
import functools

import jax
import jax.numpy as jnp
from jax import lax
from jax.experimental import pallas as pl
from jax.experimental.pallas import tpu as pltpu
from jax.sharding import PartitionSpec as P

TB = 28
GROUP = 4
CHUNKS = 2


class Plan:
    def __init__(self, mesh):
        self.grid = mesh.shape["row"]
        self.half = min(6, self.grid) // 2
        self.whole = 2 * self.half == self.grid
        self.stages = self.grid - 1 if self.whole else self.half

    def shift(self, a, l):
        if self.whole:
            return l - a
        mid = self.grid // 2
        k = (l - a + mid) % self.grid - mid
        return k if -self.half <= k < self.half else None

    def hop_pairs(self, stage):
        pairs = []
        for source in range(self.grid):
            for layer, step in ((0, 1), (1, -1)):
                target = source + step
                origin = target - step * stage
                if self.whole and not (0 <= target < self.grid and 0 <= origin < self.grid):
                    continue
                target %= self.grid
                if self.shift(target, origin % self.grid) == -step * stage:
                    pairs.append((source * 2 + layer, target * 2 + layer))
        return pairs

    def row_pairs(self, by):
        pairs = []
        for r in range(self.grid):
            for a in range(self.grid):
                k = self.shift(a, r)
                if k is not None:
                    layer = int(k > 0)
                    target = r ^ by
                    pairs.append(
                        tuple((p * self.grid + a) * 2 + layer for p in (r, target))
                    )
        return pairs

    def taken(self, a, layer, stage):
        l = jnp.where(layer == 0, a - stage, a + stage)
        if self.whole:
            valid = (l >= 0) & (l < self.grid)
        else:
            valid = jnp.where(layer == 0, stage <= self.half, stage < self.half)
        if stage == 0:
            valid = valid & (layer == 0)
        l = jnp.where(l < 0, l + self.grid, l)
        return jnp.where(l >= self.grid, l - self.grid, l), valid


def place():
    return tuple(lax.axis_index(n) for n in ("col", "row", "layer"))


def list_kernel(plan, rows, cols, pairs, pos):
    slots = rows.shape[2]
    a, b, layer = place()

    def clear(i, carry):
        pos[i] = 0
        return carry

    lax.fori_loop(0, 4 * TB, clear, 0, unroll=8)
    for stage in range(plan.stages + 1):
        l, valid = plan.taken(a, layer, stage)
        mark = 64 * (stage + 1) + 1

        def enter(s, carry):
            ra = rows[a, l, s]
            pos[2 * ra + (cols[a, l, s] != ra).astype(jnp.int32)] = mark + s
            rb = rows[l, b, s]
            pos[2 * TB + 2 * rb + (cols[l, b, s] != rb).astype(jnp.int32)] = mark + s
            return carry

        def collect(u, count):
            r = rows[a, b, u]
            d = (cols[a, b, u] != r).astype(jnp.int32)
            left, right = pos[2 * r] - mark, pos[2 * TB + 2 * r + d] - mark
            pairs[stage, count] = (left * 64 + right) * 64 + u
            count = count + ((left >= 0) & (right >= 0)).astype(jnp.int32)
            after = jnp.where(r + 1 == TB, 0, r + 1)
            left, right = pos[2 * r + 1] - mark, pos[2 * TB + 2 * after] - mark
            pairs[stage, count] = (left * 64 + right) * 64 + u
            return count + ((left >= 0) & (right >= 0) & (d == 1)).astype(jnp.int32)

        lax.fori_loop(0, slots, enter, 0, unroll=4)
        count = lax.fori_loop(0, slots, collect, jnp.int32(0), unroll=4)
        for extra in range(GROUP - 1):
            pairs[stage, count + extra] = slots
        pairs[stage, pairs.shape[1] - 1] = jnp.where(valid, count, 0)


def add_products(count, pairs, stage, left, right, job, acc):
    def step(i, carry):
        codes = [pairs[stage, i * GROUP + j] for j in range(GROUP)]
        products = [
            jnp.dot(
                left[job, code // 4096],
                right[job, (code // 64) % 64],
                preferred_element_type=jnp.float32,
            )
            for code in codes
        ]
        for code, product in zip(codes, products):
            acc[code % 64] += product
        return carry

    lax.fori_loop(0, (count + GROUP - 1) // GROUP, step, 0)


def fetch(copies, buffer, sem):
    at = 0
    for j, ref in enumerate(copies):
        pltpu.make_async_copy(
            ref, buffer.at[pl.ds(at, ref.shape[0])], sem.at[j]
        ).start()
        at += ref.shape[0]


def fetched(copies, buffer, sem):
    at = 0
    for j, ref in enumerate(copies):
        pltpu.make_async_copy(
            ref, buffer.at[pl.ds(at, ref.shape[0])], sem.at[j]
        ).wait()
        at += ref.shape[0]


def fetch_left(lefts, by, buffer, sem):
    for n, ref in lefts.items():

        @pl.when(by == n)
        def _(ref=ref):
            pltpu.make_async_copy(ref, buffer, sem).start()


def early_kernel(plan, parts, pairs, *refs):
    far = plan.grid - 1
    lefts = dict(enumerate(refs[:far]))
    refs = refs[far:]
    rights = []
    for n in parts:
        rights.append(refs[:n])
        refs = refs[n:]
    out, left, right, acc, left_sem, right_sem, out_sem = refs
    a, b, layer = place()
    last = pairs.shape[1] - 1
    jobs = []
    for stage in range(plan.stages):
        l, _ = plan.taken(a, layer, stage)
        by = b ^ l
        count = jnp.where(by == far, 0, pairs[stage, last])
        jobs.append((stage, by, count))

        @pl.when(count > 0)
        def _(stage=stage, by=by):
            fetch(rights[stage], right.at[stage], right_sem.at[stage])
            fetch_left(lefts, by, left.at[stage], left_sem.at[stage])

    acc[...] = jnp.zeros_like(acc)
    for stage, by, count in jobs:

        @pl.when(count > 0)
        def _(stage=stage, count=count):
            pltpu.make_async_copy(
                lefts[0], left.at[stage], left_sem.at[stage]
            ).wait()
            fetched(rights[stage], right.at[stage], right_sem.at[stage])
            add_products(count, pairs, stage, left, right, stage, acc)

    copy = pltpu.make_async_copy(acc.at[pl.ds(0, out.shape[0])], out, out_sem)
    copy.start()
    copy.wait()


def last_kernel(plan, parts, pairs, total, *refs):
    far = plan.grid - 1
    lefts = dict(enumerate(refs[: plan.grid]))
    refs = refs[plan.grid :]
    rights = []
    for n in parts:
        rights.append(refs[:n])
        refs = refs[n:]
    mine, other, left, right, acc, left_sem, right_sem, io_sem = refs
    a, b, layer = place()
    last = pairs.shape[1] - 1
    held = pltpu.make_async_copy(total, acc.at[pl.ds(0, total.shape[0])], io_sem.at[0])
    held.start()
    end = plan.stages
    jobs = []
    for stage in range(end + 1):
        l, _ = plan.taken(a, layer, stage)
        by = b ^ l
        count = pairs[stage, last]
        if stage < end:
            count = jnp.where(by == far, count, 0)
        jobs.append((stage, by, count))
        slot = int(stage == end)

        @pl.when(count > 0)
        def _(stage=stage, by=by, slot=slot):
            fetch(rights[stage], right.at[slot], right_sem.at[stage])
            if stage < end:
                pltpu.make_async_copy(
                    lefts[far], left.at[slot], left_sem.at[slot]
                ).start()
            else:
                fetch_left(lefts, by, left.at[slot], left_sem.at[slot])

    held.wait()
    for stage, by, count in jobs:
        slot = int(stage == end)

        @pl.when(count > 0)
        def _(stage=stage, count=count, slot=slot):
            pltpu.make_async_copy(lefts[far], left.at[slot], left_sem.at[slot]).wait()
            fetched(rights[stage], right.at[slot], right_sem.at[stage])
            add_products(count, pairs, stage, left, right, slot, acc)

    share = mine.shape[0]
    sent = pltpu.make_async_copy(
        acc.at[pl.ds((1 - layer) * share, share)], other, io_sem.at[0]
    )
    kept = pltpu.make_async_copy(
        acc.at[pl.ds(layer * share, share)], mine, io_sem.at[1]
    )
    sent.start()
    kept.start()
    sent.wait()
    kept.wait()


def scratch(tile, jobs, stages, parts):
    slots, size = tile.shape[0], tile.shape[1]
    return [
        pltpu.VMEM((jobs, *tile.shape), tile.dtype),
        pltpu.VMEM((jobs, *tile.shape), tile.dtype),
        pltpu.VMEM((slots + 1, size, size), jnp.float32),
        pltpu.SemaphoreType.DMA((jobs,)),
        pltpu.SemaphoreType.DMA((stages, parts)),
    ]


def on_device(plan, x_blocks, slot_rows, slot_cols):
    own = x_blocks[0, 0]
    slots, size = own.shape[0], own.shape[1]
    share = slots // 2
    bounds = [slots * i // CHUNKS for i in range(CHUNKS + 1)]
    held = [own[i:j] for i, j in zip(bounds[:-1], bounds[1:])]
    rights = [[own]]
    for stage in range(1, plan.stages + 1):
        pairs = plan.hop_pairs(stage)
        held = [lax.ppermute(part, ("col", "layer"), pairs) for part in held]
        rights.append(held)
    lefts = [own] + [
        lax.ppermute(own, ("row", "col", "layer"), plan.row_pairs(by))
        for by in range(1, plan.grid)
    ]
    anywhere = pl.BlockSpec(memory_space=pl.ANY)
    scalars = pl.BlockSpec(memory_space=pltpu.SMEM)
    lists = pl.pallas_call(
        functools.partial(list_kernel, plan),
        out_shape=jax.ShapeDtypeStruct(
            (plan.stages + 1, 2 * slots + GROUP + 1), jnp.int32
        ),
        in_specs=[scalars] * 2,
        out_specs=scalars,
        scratch_shapes=[pltpu.SMEM((4 * TB,), jnp.int32)],
        cost_estimate=pl.CostEstimate(
            flops=0, bytes_accessed=4 * own.size, transcendentals=0
        ),
        name="list_products",
    )(slot_rows, slot_cols)
    parts = [len(r) for r in rights]
    tile_bytes = own.size * 2
    total = pl.pallas_call(
        functools.partial(early_kernel, plan, parts[:-1]),
        out_shape=jax.ShapeDtypeStruct((slots, size, size), jnp.float32),
        in_specs=[scalars] + [anywhere] * (plan.grid - 1 + sum(parts[:-1])),
        out_specs=anywhere,
        scratch_shapes=scratch(own, plan.stages, plan.stages, CHUNKS)
        + [pltpu.SemaphoreType.DMA],
        cost_estimate=pl.CostEstimate(
            flops=2 * size**3 * slots * plan.stages,
            bytes_accessed=(2 * plan.stages + 2) * tile_bytes,
            transcendentals=0,
        ),
        name="early_products",
    )(lists, *lefts[:-1], *[part for stage in rights[:-1] for part in stage])
    half = jax.ShapeDtypeStruct((share, size, size), jnp.float32)
    mine, other = pl.pallas_call(
        functools.partial(last_kernel, plan, parts),
        out_shape=(half, half),
        in_specs=[scalars] + [anywhere] * (1 + plan.grid + sum(parts)),
        out_specs=(anywhere, anywhere),
        scratch_shapes=scratch(own, 2, plan.stages + 1, CHUNKS)
        + [pltpu.SemaphoreType.DMA((2,))],
        cost_estimate=pl.CostEstimate(
            flops=2 * size**3 * slots,
            bytes_accessed=6 * tile_bytes,
            transcendentals=0,
        ),
        name="last_products",
    )(lists, total, *lefts, *[part for stage in rights for part in stage])
    received = lax.ppermute(other, "layer", [(0, 1), (1, 0)])
    return (mine + received).astype(jnp.bfloat16)[None, None]


def solution(mesh):
    in_specs = (P("col", "row", None, None, None), P(), P())
    out_specs = P("col", "row", "layer", None, None)
    return jax.shard_map(
        functools.partial(on_device, Plan(mesh)),
        mesh=mesh,
        in_specs=in_specs,
        out_specs=out_specs,
        check_vma=False,
    )
```

```python
import functools

import jax
import jax.numpy as jnp
from jax import lax
from jax.experimental import pallas as pl
from jax.experimental.pallas import tpu as pltpu
from jax.sharding import PartitionSpec as P

TB = 28
GROUP = 4
LANES = 128
GRANT = 16 << 20
CHUNKS = 2


class Plan:
    def __init__(self, mesh):
        self.grid = mesh.shape["row"]
        self.half = min(6, self.grid) // 2
        self.whole = 2 * self.half == self.grid
        self.stages = self.grid - 1 if self.whole else self.half

    def shift(self, a, l):
        if self.whole:
            return l - a
        mid = self.grid // 2
        k = (l - a + mid) % self.grid - mid
        return k if -self.half <= k < self.half else None

    def hop_pairs(self, stage):
        pairs = []
        for source in range(self.grid):
            for layer, step in ((0, 1), (1, -1)):
                target = source + step
                origin = target - step * stage
                if self.whole and not (0 <= target < self.grid and 0 <= origin < self.grid):
                    continue
                target %= self.grid
                if self.shift(target, origin % self.grid) == -step * stage:
                    pairs.append((source * 2 + layer, target * 2 + layer))
        return pairs

    def row_pairs(self, by):
        pairs = []
        for r in range(self.grid):
            for a in range(self.grid):
                k = self.shift(a, r)
                if k is not None:
                    layer = int(k > 0)
                    target = r ^ by
                    pairs.append(
                        tuple((p * self.grid + a) * 2 + layer for p in (r, target))
                    )
        return pairs

    def taken(self, a, layer, stage):
        l = jnp.where(layer == 0, a - stage, a + stage)
        if self.whole:
            valid = (l >= 0) & (l < self.grid)
        else:
            valid = jnp.where(layer == 0, stage <= self.half, stage < self.half)
        if stage == 0:
            valid = valid & (layer == 0)
        l = jnp.where(l < 0, l + self.grid, l)
        return jnp.where(l >= self.grid, l - self.grid, l), valid


def place():
    return tuple(lax.axis_index(n) for n in ("col", "row", "layer"))


def list_kernel(plan, rows, cols, pairs, keys, codes):
    slots = rows.shape[2]
    stages = plan.stages + 1
    a, b, layer = place()
    lane = lax.broadcasted_iota(jnp.int32, (1, LANES), 1)
    down = lax.broadcasted_iota(jnp.int32, (LANES, LANES), 0)
    across = lax.broadcasted_iota(jnp.int32, (LANES, LANES), 1)

    def key_of(i, j):
        r, c = rows[i, pl.ds(j, 1), :], cols[i, pl.ds(j, 1), :]
        return 2 * r + (c != r).astype(jnp.int32)

    keys[...] = jnp.full_like(keys, -1)
    taken = []
    for stage in range(stages):
        l, valid = plan.taken(a, layer, stage)
        taken.append(valid)
        l = jnp.clip(l, 0, plan.grid - 1)
        keys[pl.ds(stage, 1), 0:slots] = key_of(a, l)
        keys[pl.ds(stages + stage, 1), 0:slots] = key_of(l, b)
    keys[pl.ds(2 * stages, 1), 0:slots] = key_of(a, b)
    out = keys[pl.ds(2 * stages, 1), :]
    out = jnp.where(lane < LANES // 2, out, pltpu.roll(out, LANES // 2, 1))
    slot = lane % (LANES // 2)
    r, d = out // 2, out % 2
    after = jnp.where(r + 1 == TB, 0, r + 1)
    second = lane >= LANES // 2
    left_key = jnp.where(second, 2 * r + 1, 2 * r)
    right_key = jnp.where(second, jnp.where(d == 1, 2 * after, -2), out)
    wanted = slot < slots
    left_key = jnp.where(wanted, left_key, -2)
    right_key = jnp.where(wanted, right_key, -2)
    columns = keys[...].T

    def find(column, key):
        hit = columns[:, column : column + 1] == key
        return jnp.sum(jnp.where(hit, down + 1, 0), axis=0, keepdims=True)

    codes[...] = jnp.zeros_like(codes)
    for stage in range(stages):
        left, right = find(stage, left_key), find(stages + stage, right_key)
        good = (left > 0) & (right > 0) & taken[stage]
        code = ((left - 1) * 64 + (right - 1)) * 64 + slot
        codes[pl.ds(stage, 1), :] = jnp.where(good, code + 1, 0)
    found = codes[...] > 0
    ahead = jnp.dot(
        found.astype(jnp.float32),
        (down < across).astype(jnp.float32),
        preferred_element_type=jnp.float32,
    ).astype(jnp.int32)
    order = jnp.where(found, ahead, -1).T
    entries = codes[...].T
    for stage in range(stages):
        hit = order[:, stage : stage + 1] == across
        entry = jnp.where(hit, entries[:, stage : stage + 1], 0)
        entry = jnp.sum(entry, axis=0, keepdims=True)
        count = jnp.sum(
            found[stage : stage + 1].astype(jnp.int32), axis=1, keepdims=True
        )
        entry = jnp.where(lane < count, entry - 1, slots)
        pairs[pl.ds(stage, 1), :] = jnp.where(lane == LANES - 1, count, entry)


def add_products(count, pairs, stage, left, right, job, acc):
    def step(i, carry):
        codes = [pairs[stage, i * GROUP + j] for j in range(GROUP)]
        products = [
            jnp.dot(
                left[job, code // 4096],
                right[job, (code // 64) % 64],
                preferred_element_type=jnp.float32,
            )
            for code in codes
        ]
        for code, product in zip(codes, products):
            acc[code % 64] += product
        return carry

    lax.fori_loop(0, (count + GROUP - 1) // GROUP, step, 0)


def fetch(copies, buffer, sem):
    at = 0
    for j, ref in enumerate(copies):
        pltpu.make_async_copy(
            ref, buffer.at[pl.ds(at, ref.shape[0])], sem.at[j]
        ).start()
        at += ref.shape[0]


def fetched(copies, buffer, sem):
    at = 0
    for j, ref in enumerate(copies):
        pltpu.make_async_copy(
            ref, buffer.at[pl.ds(at, ref.shape[0])], sem.at[j]
        ).wait()
        at += ref.shape[0]


def fetch_left(lefts, by, buffer, sem):
    for n, ref in lefts.items():

        @pl.when(by == n)
        def _(ref=ref):
            pltpu.make_async_copy(ref, buffer, sem).start()


def early_kernel(plan, parts, pairs, *refs):
    far = plan.grid - 1
    lefts = dict(enumerate(refs[:far]))
    refs = refs[far:]
    rights = []
    for n in parts:
        rights.append(refs[:n])
        refs = refs[n:]
    acc, left, right, left_sem, right_sem = refs
    a, b, layer = place()
    last = pairs.shape[1] - 1
    jobs = []
    for stage in range(plan.stages):
        l, _ = plan.taken(a, layer, stage)
        by = b ^ l
        count = jnp.where(by == far, 0, pairs[stage, last])
        jobs.append((stage, by, count))

        @pl.when(count > 0)
        def _(stage=stage, by=by):
            fetch(rights[stage], right.at[stage], right_sem.at[stage])
            fetch_left(lefts, by, left.at[stage], left_sem.at[stage])

    acc[...] = jnp.zeros_like(acc)
    for stage, by, count in jobs:

        @pl.when(count > 0)
        def _(stage=stage, count=count):
            pltpu.make_async_copy(
                lefts[0], left.at[stage], left_sem.at[stage]
            ).wait()
            fetched(rights[stage], right.at[stage], right_sem.at[stage])
            add_products(count, pairs, stage, left, right, stage, acc)


def last_kernel(plan, parts, pairs, total, *refs):
    far = plan.grid - 1
    lefts = dict(enumerate(refs[: plan.grid]))
    refs = refs[plan.grid :]
    rights = []
    for n in parts:
        rights.append(refs[:n])
        refs = refs[n:]
    acc, mine, other, left, right, left_sem, right_sem = refs
    a, b, layer = place()
    last = pairs.shape[1] - 1
    end = plan.stages
    jobs = []
    for stage in range(end + 1):
        l, _ = plan.taken(a, layer, stage)
        by = b ^ l
        count = pairs[stage, last]
        if stage < end:
            count = jnp.where(by == far, count, 0)
        jobs.append((stage, by, count))
        slot = int(stage == end)

        @pl.when(count > 0)
        def _(stage=stage, by=by, slot=slot):
            fetch(rights[stage], right.at[slot], right_sem.at[stage])
            if stage < end:
                pltpu.make_async_copy(
                    lefts[far], left.at[slot], left_sem.at[slot]
                ).start()
            else:
                fetch_left(lefts, by, left.at[slot], left_sem.at[slot])

    del total
    for stage, by, count in jobs:
        slot = int(stage == end)

        @pl.when(count > 0)
        def _(stage=stage, count=count, slot=slot):
            pltpu.make_async_copy(lefts[far], left.at[slot], left_sem.at[slot]).wait()
            fetched(rights[stage], right.at[slot], right_sem.at[stage])
            add_products(count, pairs, stage, left, right, slot, acc)

    share = mine.shape[0]
    mine[...] = acc[pl.ds(layer * share, share)]
    other[...] = acc[pl.ds((1 - layer) * share, share)]


def scratch(tile, jobs, stages, parts):
    return [
        pltpu.VMEM((jobs, *tile.shape), tile.dtype),
        pltpu.VMEM((jobs, *tile.shape), tile.dtype),
        pltpu.SemaphoreType.DMA((jobs,)),
        pltpu.SemaphoreType.DMA((stages, parts)),
    ]


def on_device(plan, x_blocks, slot_rows, slot_cols):
    own = x_blocks[0, 0]
    slots, size = own.shape[0], own.shape[1]
    share = slots // 2
    bounds = [slots * i // CHUNKS for i in range(CHUNKS + 1)]
    held = [own[i:j] for i, j in zip(bounds[:-1], bounds[1:])]
    anywhere = pl.BlockSpec(memory_space=pl.ANY)
    scalars = pl.BlockSpec(memory_space=pltpu.SMEM)
    vmem = pl.BlockSpec(memory_space=pltpu.VMEM)
    lists = pl.pallas_call(
        functools.partial(list_kernel, plan),
        out_shape=jax.ShapeDtypeStruct((plan.stages + 1, LANES), jnp.int32),
        in_specs=[vmem] * 2,
        out_specs=vmem,
        scratch_shapes=[pltpu.VMEM((LANES, LANES), jnp.int32)] * 2,
        compiler_params=pltpu.CompilerParams(vmem_limit_bytes=GRANT),
        cost_estimate=pl.CostEstimate(
            flops=0, bytes_accessed=4 * own.size, transcendentals=0
        ),
        name="list_products",
    )(slot_rows, slot_cols)
    rights = [[own]]
    for stage in range(1, plan.stages + 1):
        pairs = plan.hop_pairs(stage)
        if stage == 2:
            held[0], lists = lax.optimization_barrier((held[0], lists))
        held = [lax.ppermute(part, ("col", "layer"), pairs) for part in held]
        rights.append(held)
    lefts = [own] + [
        lax.ppermute(own, ("row", "col", "layer"), plan.row_pairs(by))
        for by in range(1, plan.grid)
    ]
    parts = [len(r) for r in rights]
    tile_bytes = own.size * 2
    running = jax.ShapeDtypeStruct((slots + 1, size, size), jnp.float32)
    total = pl.pallas_call(
        functools.partial(early_kernel, plan, parts[:-1]),
        out_shape=running,
        in_specs=[scalars] + [anywhere] * (plan.grid - 1 + sum(parts[:-1])),
        out_specs=vmem,
        scratch_shapes=scratch(own, plan.stages, plan.stages, CHUNKS),
        compiler_params=pltpu.CompilerParams(vmem_limit_bytes=GRANT),
        cost_estimate=pl.CostEstimate(
            flops=2 * size**3 * slots * plan.stages,
            bytes_accessed=(2 * plan.stages + 2) * tile_bytes,
            transcendentals=0,
        ),
        name="early_products",
    )(lists, *lefts[:-1], *[part for stage in rights[:-1] for part in stage])
    half = jax.ShapeDtypeStruct((share, size, size), jnp.float32)
    _, mine, other = pl.pallas_call(
        functools.partial(last_kernel, plan, parts),
        out_shape=(running, half, half),
        in_specs=[scalars, vmem] + [anywhere] * (plan.grid + sum(parts)),
        out_specs=(vmem, vmem, vmem),
        input_output_aliases={1: 0},
        scratch_shapes=scratch(own, 2, plan.stages + 1, CHUNKS),
        compiler_params=pltpu.CompilerParams(vmem_limit_bytes=GRANT),
        cost_estimate=pl.CostEstimate(
            flops=2 * size**3 * slots,
            bytes_accessed=6 * tile_bytes,
            transcendentals=0,
        ),
        name="last_products",
    )(lists, total, *lefts, *[part for stage in rights for part in stage])
    received = lax.ppermute(other, "layer", [(0, 1), (1, 0)])
    return (mine + received).astype(jnp.bfloat16)[None, None]


def solution(mesh):
    in_specs = (P("col", "row", None, None, None), P(), P())
    out_specs = P("col", "row", "layer", None, None)
    return jax.shard_map(
        functools.partial(on_device, Plan(mesh)),
        mesh=mesh,
        in_specs=in_specs,
        out_specs=out_specs,
        check_vma=False,
    )
```

```python
import functools

import jax
import jax.numpy as jnp
from jax import lax
from jax.experimental import pallas as pl
from jax.experimental.pallas import tpu as pltpu
from jax.sharding import PartitionSpec as P

TB = 28
GROUP = 4
LANES = 128
GRANT = 16 << 20
CHUNKS = 2
JOIN = 3


class Plan:
    def __init__(self, mesh):
        self.grid = mesh.shape["row"]
        self.half = min(6, self.grid) // 2
        self.whole = 2 * self.half == self.grid
        self.stages = self.grid - 1 if self.whole else self.half

    def shift(self, a, l):
        if self.whole:
            return l - a
        mid = self.grid // 2
        k = (l - a + mid) % self.grid - mid
        return k if -self.half <= k < self.half else None

    def hop_pairs(self, stage):
        pairs = []
        for source in range(self.grid):
            for layer, step in ((0, 1), (1, -1)):
                target = source + step
                origin = target - step * stage
                if self.whole and not (0 <= target < self.grid and 0 <= origin < self.grid):
                    continue
                target %= self.grid
                if self.shift(target, origin % self.grid) == -step * stage:
                    pairs.append((source * 2 + layer, target * 2 + layer))
        return pairs

    def row_pairs(self, by, held=0):
        pairs = []
        for r in range(self.grid):
            for a in range(self.grid):
                k = self.shift(a, r)
                if k is not None:
                    layer = int(k > 0)
                    pairs.append(
                        tuple(
                            (p * self.grid + a) * 2 + layer
                            for p in (r ^ held, r ^ held ^ by)
                        )
                    )
        return pairs

    def taken(self, a, layer, stage):
        l = jnp.where(layer == 0, a - stage, a + stage)
        if self.whole:
            valid = (l >= 0) & (l < self.grid)
        else:
            valid = jnp.where(layer == 0, stage <= self.half, stage < self.half)
        if stage == 0:
            valid = valid & (layer == 0)
        l = jnp.where(l < 0, l + self.grid, l)
        return jnp.where(l >= self.grid, l - self.grid, l), valid


def place():
    return tuple(lax.axis_index(n) for n in ("col", "row", "layer"))


def list_kernel(plan, bounds, rows, cols, pairs, keys, codes):
    slots = rows.shape[2]
    stages = plan.stages + 1
    a, b, layer = place()
    lane = lax.broadcasted_iota(jnp.int32, (1, LANES), 1)
    down = lax.broadcasted_iota(jnp.int32, (LANES, LANES), 0)
    across = lax.broadcasted_iota(jnp.int32, (LANES, LANES), 1)

    def key_of(i, j):
        r, c = rows[i, pl.ds(j, 1), :], cols[i, pl.ds(j, 1), :]
        return 2 * r + (c != r).astype(jnp.int32)

    keys[...] = jnp.full_like(keys, -1)
    taken = []
    for stage in range(stages):
        l, valid = plan.taken(a, layer, stage)
        taken.append(valid)
        l = jnp.clip(l, 0, plan.grid - 1)
        keys[pl.ds(stage, 1), 0:slots] = key_of(a, l)
        keys[pl.ds(stages + stage, 1), 0:slots] = key_of(l, b)
    keys[pl.ds(2 * stages, 1), 0:slots] = key_of(a, b)
    out = keys[pl.ds(2 * stages, 1), :]
    out = jnp.where(lane < LANES // 2, out, pltpu.roll(out, LANES // 2, 1))
    slot = lane % (LANES // 2)
    r, d = out // 2, out % 2
    after = jnp.where(r + 1 == TB, 0, r + 1)
    second = lane >= LANES // 2
    left_key = jnp.where(second, 2 * r + 1, 2 * r)
    right_key = jnp.where(second, jnp.where(d == 1, 2 * after, -2), out)
    wanted = slot < slots
    left_key = jnp.where(wanted, left_key, -2)
    right_key = jnp.where(wanted, right_key, -2)
    columns = keys[...].T

    def find(column, key):
        hit = columns[:, column : column + 1] == key
        return jnp.sum(jnp.where(hit, down + 1, 0), axis=0, keepdims=True)

    codes[...] = jnp.zeros_like(codes)
    for stage in range(stages):
        left, right = find(stage, left_key), find(stages + stage, right_key)
        good = (left > 0) & (right > 0) & taken[stage]
        code = jnp.where(good, ((left - 1) * 64 + (right - 1)) * 64 + slot + 1, 0)
        if stage < plan.stages:
            codes[pl.ds(stage, 1), :] = code
        else:
            for j, (low, high) in enumerate(zip(bounds[:-1], bounds[1:])):
                here = (right > low) & (right <= high)
                codes[pl.ds(stage + j, 1), :] = jnp.where(here, code, 0)
    found = codes[...] > 0
    ahead = jnp.dot(
        found.astype(jnp.float32),
        (down < across).astype(jnp.float32),
        preferred_element_type=jnp.float32,
    ).astype(jnp.int32)
    order = jnp.where(found, ahead, -1).T
    entries = codes[...].T
    for stage in range(pairs.shape[0]):
        hit = order[:, stage : stage + 1] == across
        entry = jnp.where(hit, entries[:, stage : stage + 1], 0)
        entry = jnp.sum(entry, axis=0, keepdims=True)
        count = jnp.sum(
            found[stage : stage + 1].astype(jnp.int32), axis=1, keepdims=True
        )
        entry = jnp.where(lane < count, entry - 1, slots)
        pairs[pl.ds(stage, 1), :] = jnp.where(lane == LANES - 1, count, entry)


def add_products(count, pairs, row, left, right, acc, low=0):
    def step(i, carry):
        codes = [pairs[row, i * GROUP + j] for j in range(GROUP)]
        products = [
            jnp.dot(
                left[code // 4096],
                right[jnp.maximum((code // 64) % 64 - low, 0)],
                preferred_element_type=jnp.float32,
            )
            for code in codes
        ]
        for code, product in zip(codes, products):
            acc[code % 64] += product
        return carry

    lax.fori_loop(0, (count + GROUP - 1) // GROUP, step, 0)


def fetch(copies, buffer, sem):
    at = 0
    for j, ref in enumerate(copies):
        pltpu.make_async_copy(
            ref, buffer.at[pl.ds(at, ref.shape[0])], sem.at[j]
        ).start()
        at += ref.shape[0]


def fetched(copies, buffer, sem):
    at = 0
    for j, ref in enumerate(copies):
        pltpu.make_async_copy(
            ref, buffer.at[pl.ds(at, ref.shape[0])], sem.at[j]
        ).wait()
        at += ref.shape[0]


def fetch_left(lefts, by, buffer, sem):
    for n, ref in lefts.items():

        @pl.when(by == n)
        def _(ref=ref):
            pltpu.make_async_copy(ref, buffer, sem).start()


def early_kernel(plan, parts, pairs, *refs):
    far = plan.grid - 1
    lefts = dict(enumerate(refs[:far]))
    refs = refs[far:]
    rights = []
    for n in parts:
        rights.append(refs[:n])
        refs = refs[n:]
    acc, left, right, left_sem, right_sem = refs
    a, b, layer = place()
    last = pairs.shape[1] - 1
    jobs = []
    for stage in range(plan.stages):
        l, _ = plan.taken(a, layer, stage)
        by = b ^ l
        count = jnp.where(by == far, 0, pairs[stage, last])
        jobs.append((stage, by, count))

        @pl.when(count > 0)
        def _(stage=stage, by=by):
            fetch(rights[stage], right.at[stage], right_sem.at[stage])
            fetch_left(lefts, by, left.at[stage], left_sem.at[stage])

    acc[...] = jnp.zeros_like(acc)
    for stage, by, count in jobs:

        @pl.when(count > 0)
        def _(stage=stage, count=count):
            pltpu.make_async_copy(
                lefts[0], left.at[stage], left_sem.at[stage]
            ).wait()
            fetched(rights[stage], right.at[stage], right_sem.at[stage])
            add_products(
                count, pairs, stage, left.at[stage], right.at[stage], acc
            )


def middle_kernel(plan, parts, pairs, total, *refs):
    del total
    lefts = dict(enumerate(refs[: plan.grid - 1]))
    refs = refs[plan.grid - 1 :]
    far_parts, refs = refs[:2], refs[2:]
    rights = []
    for n in parts[:-1]:
        rights.append(refs[:n])
        refs = refs[n:]
    first, acc, left_last, left, right, left_sem, right_sem = refs
    far, end, last = plan.grid - 1, plan.stages, pairs.shape[1] - 1
    a, b, layer = place()
    l, _ = plan.taken(a, layer, end)
    end_by = b ^ l

    @pl.when(end_by == far)
    def _():
        fetch(far_parts, left_last, left_sem.at[1])

    fetch_left(lefts, end_by, left_last, left_sem.at[1, 0])
    for stage in range(end):
        l, _ = plan.taken(a, layer, stage)
        count = jnp.where(b ^ l == far, pairs[stage, last], 0)

        @pl.when(count > 0)
        def _(stage=stage, count=count):
            fetch(rights[stage], right, right_sem)
            fetch(far_parts, left, left_sem.at[0])
            fetched(rights[stage], right, right_sem)
            fetched(far_parts, left, left_sem.at[0])
            add_products(count, pairs, stage, left, right, acc)

    @pl.when(end_by == far)
    def _():
        fetched(far_parts, left_last, left_sem.at[1])

    @pl.when((end_by >= 0) & (end_by < far))
    def _():
        pltpu.make_async_copy(lefts[0], left_last, left_sem.at[1, 0]).wait()

    add_products(pairs[end, last], pairs, end, left_last, first, acc)


def last_kernel(plan, bounds, pairs, total, left_last, *refs):
    del total
    refs, (acc, mine, other) = refs[:-3], refs[-3:]
    last = pairs.shape[1] - 1
    for j, part in enumerate(refs):
        row = plan.stages + 1 + j
        add_products(pairs[row, last], pairs, row, left_last, part, acc, bounds[1 + j])
    layer = lax.axis_index("layer")
    share = mine.shape[0]
    mine[...] = acc[pl.ds(layer * share, share)]
    other[...] = acc[pl.ds((1 - layer) * share, share)]


def on_device(plan, x_blocks, slot_rows, slot_cols):
    own = x_blocks[0, 0]
    slots, size = own.shape[0], own.shape[1]
    share = slots // 2
    bounds = [slots * i // CHUNKS for i in range(CHUNKS + 1)]
    held = [own[i:j] for i, j in zip(bounds[:-1], bounds[1:])]
    anywhere = pl.BlockSpec(memory_space=pl.ANY)
    scalars = pl.BlockSpec(memory_space=pltpu.SMEM)
    vmem = pl.BlockSpec(memory_space=pltpu.VMEM)
    compiler_params = pltpu.CompilerParams(vmem_limit_bytes=GRANT)
    tile_bytes = own.size * 2

    def cost(products, tiles):
        return pl.CostEstimate(
            flops=2 * size**3 * products,
            bytes_accessed=tiles * tile_bytes,
            transcendentals=0,
        )

    lists = pl.pallas_call(
        functools.partial(list_kernel, plan, bounds),
        out_shape=jax.ShapeDtypeStruct((plan.stages + CHUNKS, LANES), jnp.int32),
        in_specs=[vmem] * 2,
        out_specs=vmem,
        scratch_shapes=[pltpu.VMEM((LANES, LANES), jnp.int32)] * 2,
        compiler_params=compiler_params,
        cost_estimate=cost(0, 2),
        name="list_products",
    )(slot_rows, slot_cols)
    rights = [[own]]
    for stage in range(1, plan.stages + 1):
        pairs = plan.hop_pairs(stage)
        if stage == JOIN:
            held[0], lists = lax.optimization_barrier((held[0], lists))
        held = [lax.ppermute(part, ("col", "layer"), pairs) for part in held]
        rights.append(held)
    everywhere = ("row", "col", "layer")
    far = plan.grid - 1
    lefts = [own] + [
        lax.ppermute(own, everywhere, plan.row_pairs(by)) for by in range(1, far)
    ]
    far_parts = [
        lax.ppermute(part, everywhere, plan.row_pairs(far ^ by, by))
        for by, part in ((1, lefts[1][:share]), (2, lefts[2][share:]))
    ]
    parts = [len(r) for r in rights]
    running = jax.ShapeDtypeStruct((slots + 1, size, size), jnp.float32)
    before = [part for stage in rights[:-1] for part in stage]
    total = pl.pallas_call(
        functools.partial(early_kernel, plan, parts[:-1]),
        out_shape=running,
        in_specs=[scalars] + [anywhere] * (len(lefts) + len(before)),
        out_specs=vmem,
        scratch_shapes=[
            pltpu.VMEM((plan.stages, *own.shape), own.dtype),
            pltpu.VMEM((plan.stages, *own.shape), own.dtype),
            pltpu.SemaphoreType.DMA((plan.stages,)),
            pltpu.SemaphoreType.DMA((plan.stages, CHUNKS)),
        ],
        compiler_params=compiler_params,
        cost_estimate=cost(slots * plan.stages, 2 * plan.stages),
        name="early_products",
    )(lists, *lefts, *before)
    first, *rest = rights[-1]
    total, left_last = pl.pallas_call(
        functools.partial(middle_kernel, plan, parts),
        out_shape=(running, jax.ShapeDtypeStruct(own.shape, own.dtype)),
        in_specs=[scalars, vmem]
        + [anywhere] * (len(lefts) + len(far_parts) + len(before))
        + [vmem],
        out_specs=(vmem, vmem),
        input_output_aliases={1: 0},
        scratch_shapes=[
            pltpu.VMEM(own.shape, own.dtype),
            pltpu.VMEM(own.shape, own.dtype),
            pltpu.SemaphoreType.DMA((2, 2)),
            pltpu.SemaphoreType.DMA((CHUNKS,)),
        ],
        compiler_params=compiler_params,
        cost_estimate=cost(slots, 4),
        name="middle_products",
    )(lists, total, *lefts, *far_parts, *before, first)
    half = jax.ShapeDtypeStruct((share, size, size), jnp.float32)
    _, mine, other = pl.pallas_call(
        functools.partial(last_kernel, plan, bounds),
        out_shape=(running, half, half),
        in_specs=[scalars] + [vmem] * (2 + len(rest)),
        out_specs=(vmem, vmem, vmem),
        input_output_aliases={1: 0},
        compiler_params=compiler_params,
        cost_estimate=cost(slots // 2, 4),
        name="last_products",
    )(lists, total, left_last, *rest)
    received = lax.ppermute(other, "layer", [(0, 1), (1, 0)])
    return (mine + received).astype(jnp.bfloat16)[None, None]


def solution(mesh):
    in_specs = (P("col", "row", None, None, None), P(), P())
    out_specs = P("col", "row", "layer", None, None)
    return jax.shard_map(
        functools.partial(on_device, Plan(mesh)),
        mesh=mesh,
        in_specs=in_specs,
        out_specs=out_specs,
        check_vma=False,
    )
```

```python
import functools

import jax
import jax.numpy as jnp
from jax import lax
from jax.experimental import pallas as pl
from jax.experimental.pallas import tpu as pltpu
from jax.sharding import PartitionSpec as P

TB = 28
GROUP = 4
LANES = 128
GRANT = 16 << 20
CHUNKS = 2
JOIN = 3


class Plan:
    def __init__(self, mesh):
        self.grid = mesh.shape["row"]
        self.half = min(6, self.grid) // 2
        self.whole = 2 * self.half == self.grid
        self.stages = self.grid - 1 if self.whole else self.half

    def shift(self, a, l):
        if self.whole:
            return l - a
        mid = self.grid // 2
        k = (l - a + mid) % self.grid - mid
        return k if -self.half <= k < self.half else None

    def hop_pairs(self, stage):
        pairs = []
        for source in range(self.grid):
            for layer, step in ((0, 1), (1, -1)):
                target = source + step
                origin = target - step * stage
                if self.whole and not (0 <= target < self.grid and 0 <= origin < self.grid):
                    continue
                target %= self.grid
                if self.shift(target, origin % self.grid) == -step * stage:
                    pairs.append((source * 2 + layer, target * 2 + layer))
        return pairs

    def row_pairs(self, by, held=0):
        pairs = []
        for r in range(self.grid):
            for a in range(self.grid):
                k = self.shift(a, r)
                if k is not None:
                    layer = int(k > 0)
                    pairs.append(
                        tuple(
                            (p * self.grid + a) * 2 + layer
                            for p in (r ^ held, r ^ held ^ by)
                        )
                    )
        return pairs

    def taken(self, a, layer, stage):
        l = jnp.where(layer == 0, a - stage, a + stage)
        if self.whole:
            valid = (l >= 0) & (l < self.grid)
        else:
            valid = jnp.where(layer == 0, stage <= self.half, stage < self.half)
        if stage == 0:
            valid = valid & (layer == 0)
        l = jnp.where(l < 0, l + self.grid, l)
        return jnp.where(l >= self.grid, l - self.grid, l), valid


def place():
    return tuple(lax.axis_index(n) for n in ("col", "row", "layer"))


def list_kernel(plan, bounds, rows_in, cols_in, pairs, rows, cols, keys, codes, sem):
    slots = rows.shape[2]
    stages = plan.stages + 1
    inputs = [
        pltpu.make_async_copy(rows_in, rows, sem.at[0]),
        pltpu.make_async_copy(cols_in, cols, sem.at[1]),
    ]
    for copy in inputs:
        copy.start()
    a, b, layer = place()
    lane = lax.broadcasted_iota(jnp.int32, (1, LANES), 1)
    down = lax.broadcasted_iota(jnp.int32, (LANES, LANES), 0)
    across = lax.broadcasted_iota(jnp.int32, (LANES, LANES), 1)

    def key_of(i, j):
        r, c = rows[i, pl.ds(j, 1), :], cols[i, pl.ds(j, 1), :]
        return 2 * r + (c != r).astype(jnp.int32)

    keys[...] = jnp.full_like(keys, -1)
    for copy in inputs:
        copy.wait()
    taken = []
    for stage in range(stages):
        l, valid = plan.taken(a, layer, stage)
        taken.append(valid)
        l = jnp.clip(l, 0, plan.grid - 1)
        keys[pl.ds(stage, 1), 0:slots] = key_of(a, l)
        keys[pl.ds(stages + stage, 1), 0:slots] = key_of(l, b)
    keys[pl.ds(2 * stages, 1), 0:slots] = key_of(a, b)
    out = keys[pl.ds(2 * stages, 1), :]
    out = jnp.where(lane < LANES // 2, out, pltpu.roll(out, LANES // 2, 1))
    slot = lane % (LANES // 2)
    r, d = out // 2, out % 2
    after = jnp.where(r + 1 == TB, 0, r + 1)
    second = lane >= LANES // 2
    left_key = jnp.where(second, 2 * r + 1, 2 * r)
    right_key = jnp.where(second, jnp.where(d == 1, 2 * after, -2), out)
    wanted = slot < slots
    left_key = jnp.where(wanted, left_key, -2)
    right_key = jnp.where(wanted, right_key, -2)
    columns = keys[...].T

    def find(column, key):
        hit = columns[:, column : column + 1] == key
        return jnp.sum(jnp.where(hit, down + 1, 0), axis=0, keepdims=True)

    codes[...] = jnp.zeros_like(codes)
    for stage in range(stages):
        left, right = find(stage, left_key), find(stages + stage, right_key)
        good = (left > 0) & (right > 0) & taken[stage]
        code = jnp.where(good, ((left - 1) * 64 + (right - 1)) * 64 + slot + 1, 0)
        if stage < plan.stages:
            codes[pl.ds(stage, 1), :] = code
        else:
            for j, (low, high) in enumerate(zip(bounds[:-1], bounds[1:])):
                here = (right > low) & (right <= high)
                codes[pl.ds(stage + j, 1), :] = jnp.where(here, code, 0)
    found = codes[...] > 0
    ahead = jnp.dot(
        found.astype(jnp.float32),
        (down < across).astype(jnp.float32),
        preferred_element_type=jnp.float32,
    ).astype(jnp.int32)
    order = jnp.where(found, ahead, -1).T
    entries = codes[...].T
    for stage in range(pairs.shape[0]):
        hit = order[:, stage : stage + 1] == across
        entry = jnp.where(hit, entries[:, stage : stage + 1], 0)
        entry = jnp.sum(entry, axis=0, keepdims=True)
        count = jnp.sum(
            found[stage : stage + 1].astype(jnp.int32), axis=1, keepdims=True
        )
        entry = jnp.where(lane < count, entry - 1, slots)
        pairs[pl.ds(stage, 1), :] = jnp.where(lane == LANES - 1, count, entry)


def add_products(count, pairs, row, left, right, acc, low=0):
    def step(i, carry):
        codes = [pairs[row, i * GROUP + j] for j in range(GROUP)]
        products = [
            jnp.dot(
                left[code // 4096],
                right[jnp.maximum((code // 64) % 64 - low, 0)],
                preferred_element_type=jnp.float32,
            )
            for code in codes
        ]
        for code, product in zip(codes, products):
            acc[code % 64] += product
        return carry

    lax.fori_loop(0, (count + GROUP - 1) // GROUP, step, 0)


def fetch(copies, buffer, sem):
    at = 0
    for j, ref in enumerate(copies):
        pltpu.make_async_copy(
            ref, buffer.at[pl.ds(at, ref.shape[0])], sem.at[j]
        ).start()
        at += ref.shape[0]


def fetched(copies, buffer, sem):
    at = 0
    for j, ref in enumerate(copies):
        pltpu.make_async_copy(
            ref, buffer.at[pl.ds(at, ref.shape[0])], sem.at[j]
        ).wait()
        at += ref.shape[0]


def fetch_left(lefts, by, buffer, sem):
    for n, ref in lefts.items():

        @pl.when(by == n)
        def _(ref=ref):
            pltpu.make_async_copy(ref, buffer, sem).start()


def early_kernel(plan, parts, pairs, *refs):
    far = plan.grid - 1
    lefts = dict(enumerate(refs[:far]))
    refs = refs[far:]
    rights = []
    for n in parts:
        rights.append(refs[:n])
        refs = refs[n:]
    acc, left, right, left_sem, right_sem = refs
    a, b, layer = place()
    last = pairs.shape[1] - 1
    jobs = []
    for stage in range(plan.stages):
        l, _ = plan.taken(a, layer, stage)
        by = b ^ l
        count = jnp.where(by == far, 0, pairs[stage, last])
        jobs.append((stage, by, count))

        @pl.when(count > 0)
        def _(stage=stage, by=by):
            fetch(rights[stage], right.at[stage], right_sem.at[stage])
            fetch_left(lefts, by, left.at[stage], left_sem.at[stage])

    acc[...] = jnp.zeros_like(acc)
    for stage, by, count in jobs:

        @pl.when(count > 0)
        def _(stage=stage, count=count):
            pltpu.make_async_copy(
                lefts[0], left.at[stage], left_sem.at[stage]
            ).wait()
            fetched(rights[stage], right.at[stage], right_sem.at[stage])
            add_products(
                count, pairs, stage, left.at[stage], right.at[stage], acc
            )


def middle_kernel(plan, parts, pairs, total, *refs):
    del total
    lefts = dict(enumerate(refs[: plan.grid - 1]))
    refs = refs[plan.grid - 1 :]
    far_parts, refs = refs[:2], refs[2:]
    rights = []
    for n in parts[:-1]:
        rights.append(refs[:n])
        refs = refs[n:]
    first, acc, left_last, left, right, left_sem, right_sem = refs
    far, end, last = plan.grid - 1, plan.stages, pairs.shape[1] - 1
    a, b, layer = place()
    l, _ = plan.taken(a, layer, end)
    end_by = b ^ l

    @pl.when(end_by == far)
    def _():
        fetch(far_parts, left_last, left_sem.at[1])

    fetch_left(lefts, end_by, left_last, left_sem.at[1, 0])
    for stage in range(end):
        l, _ = plan.taken(a, layer, stage)
        count = jnp.where(b ^ l == far, pairs[stage, last], 0)

        @pl.when(count > 0)
        def _(stage=stage, count=count):
            fetch(rights[stage], right, right_sem)
            fetch(far_parts, left, left_sem.at[0])
            fetched(rights[stage], right, right_sem)
            fetched(far_parts, left, left_sem.at[0])
            add_products(count, pairs, stage, left, right, acc)

    @pl.when(end_by == far)
    def _():
        fetched(far_parts, left_last, left_sem.at[1])

    @pl.when((end_by >= 0) & (end_by < far))
    def _():
        pltpu.make_async_copy(lefts[0], left_last, left_sem.at[1, 0]).wait()

    add_products(pairs[end, last], pairs, end, left_last, first, acc)


def last_kernel(plan, bounds, pairs, total, left_last, *refs):
    del total
    refs, (acc, mine, other) = refs[:-3], refs[-3:]
    last = pairs.shape[1] - 1
    for j, part in enumerate(refs):
        row = plan.stages + 1 + j
        add_products(pairs[row, last], pairs, row, left_last, part, acc, bounds[1 + j])
    layer = lax.axis_index("layer")
    share = mine.shape[0]
    mine[...] = acc[pl.ds(layer * share, share)]
    other[...] = acc[pl.ds((1 - layer) * share, share)]


def on_device(plan, x_blocks, slot_rows, slot_cols):
    own = x_blocks[0, 0]
    slots, size = own.shape[0], own.shape[1]
    share = slots // 2
    bounds = [slots * i // CHUNKS for i in range(CHUNKS + 1)]
    held = [
        (lax.optimization_barrier(own) if i else own)[i:j]
        for i, j in zip(bounds[:-1], bounds[1:])
    ]
    anywhere = pl.BlockSpec(memory_space=pl.ANY)
    scalars = pl.BlockSpec(memory_space=pltpu.SMEM)
    vmem = pl.BlockSpec(memory_space=pltpu.VMEM)
    compiler_params = pltpu.CompilerParams(vmem_limit_bytes=GRANT)
    tile_bytes = own.size * 2

    def cost(products, tiles):
        return pl.CostEstimate(
            flops=2 * size**3 * products,
            bytes_accessed=tiles * tile_bytes,
            transcendentals=0,
        )

    lists = pl.pallas_call(
        functools.partial(list_kernel, plan, bounds),
        out_shape=jax.ShapeDtypeStruct((plan.stages + CHUNKS, LANES), jnp.int32),
        in_specs=[anywhere] * 2,
        out_specs=vmem,
        scratch_shapes=[pltpu.VMEM(slot_rows.shape, jnp.int32)] * 2
        + [pltpu.VMEM((LANES, LANES), jnp.int32)] * 2
        + [pltpu.SemaphoreType.DMA((2,))],
        compiler_params=compiler_params,
        cost_estimate=cost(0, 2),
        name="list_products",
    )(slot_rows, slot_cols)
    rights = [[own]]
    for stage in range(1, plan.stages + 1):
        pairs = plan.hop_pairs(stage)
        if stage == JOIN:
            held[0], lists = lax.optimization_barrier((held[0], lists))
        arrived = []
        for part in held:
            arrived.append(lax.ppermute(part, ("col", "layer"), pairs))
        rights.append(arrived)
        held = list(arrived)
    everywhere = ("row", "col", "layer")
    far = plan.grid - 1
    lefts = [own]
    for by in range(1, far):
        lefts.append(lax.ppermute(own, everywhere, plan.row_pairs(by)))
    far_parts = []
    for by, part in ((1, lefts[1][:share]), (2, lefts[2][share:])):
        far_parts.append(lax.ppermute(part, everywhere, plan.row_pairs(far ^ by, by)))
    parts = [len(r) for r in rights]
    running = jax.ShapeDtypeStruct((slots + 1, size, size), jnp.float32)
    before = [part for stage in rights[:-1] for part in stage]
    total = pl.pallas_call(
        functools.partial(early_kernel, plan, parts[:-1]),
        out_shape=running,
        in_specs=[scalars] + [anywhere] * (len(lefts) + len(before)),
        out_specs=vmem,
        scratch_shapes=[
            pltpu.VMEM((plan.stages, *own.shape), own.dtype),
            pltpu.VMEM((plan.stages, *own.shape), own.dtype),
            pltpu.SemaphoreType.DMA((plan.stages,)),
            pltpu.SemaphoreType.DMA((plan.stages, CHUNKS)),
        ],
        compiler_params=compiler_params,
        cost_estimate=cost(slots * plan.stages, 2 * plan.stages),
        name="early_products",
    )(lists, *lefts, *before)
    first, *rest = rights[-1]
    total, left_last = pl.pallas_call(
        functools.partial(middle_kernel, plan, parts),
        out_shape=(running, jax.ShapeDtypeStruct(own.shape, own.dtype)),
        in_specs=[scalars, vmem]
        + [anywhere] * (len(lefts) + len(far_parts) + len(before))
        + [vmem],
        out_specs=(vmem, vmem),
        input_output_aliases={1: 0},
        scratch_shapes=[
            pltpu.VMEM(own.shape, own.dtype),
            pltpu.VMEM(own.shape, own.dtype),
            pltpu.SemaphoreType.DMA((2, 2)),
            pltpu.SemaphoreType.DMA((CHUNKS,)),
        ],
        compiler_params=compiler_params,
        cost_estimate=cost(slots, 4),
        name="middle_products",
    )(lists, total, *lefts, *far_parts, *before, first)
    half = jax.ShapeDtypeStruct((share, size, size), jnp.float32)
    _, mine, other = pl.pallas_call(
        functools.partial(last_kernel, plan, bounds),
        out_shape=(running, half, half),
        in_specs=[scalars] + [vmem] * (2 + len(rest)),
        out_specs=(vmem, vmem, vmem),
        input_output_aliases={1: 0},
        compiler_params=compiler_params,
        cost_estimate=cost(slots // 2, 4),
        name="last_products",
    )(lists, total, left_last, *rest)
    received = lax.ppermute(other, "layer", [(0, 1), (1, 0)])
    return (mine + received).astype(jnp.bfloat16)[None, None]


def solution(mesh):
    plan = Plan(mesh)

    def body(*args):
        return on_device(plan, *args)

    in_specs = (P("col", "row", None, None, None), P(), P())
    out_specs = P("col", "row", "layer", None, None)
    return jax.shard_map(
        body, mesh=mesh, in_specs=in_specs, out_specs=out_specs, check_vma=False
    )
```

```python
import functools

import jax
import jax.numpy as jnp
from jax import lax
from jax.experimental import pallas as pl
from jax.experimental.pallas import tpu as pltpu
from jax.sharding import PartitionSpec as P

TB = 28
GROUP = 8
LANES = 128
GRANT = 16 << 20
CHUNKS = 2


class Plan:
    def __init__(self, mesh):
        self.grid = mesh.shape["row"]
        self.half = min(6, self.grid) // 2
        self.whole = 2 * self.half == self.grid
        self.stages = self.grid - 1 if self.whole else self.half

    def shift(self, a, l):
        if self.whole:
            return l - a
        mid = self.grid // 2
        k = (l - a + mid) % self.grid - mid
        return k if -self.half <= k < self.half else None

    def hop_pairs(self, stage):
        pairs = []
        for source in range(self.grid):
            for layer, step in ((0, 1), (1, -1)):
                target = source + step
                origin = target - step * stage
                if self.whole and not (0 <= target < self.grid and 0 <= origin < self.grid):
                    continue
                target %= self.grid
                if self.shift(target, origin % self.grid) == -step * stage:
                    pairs.append((source * 2 + layer, target * 2 + layer))
        return pairs

    def row_pairs(self, by):
        pairs = []
        for r in range(self.grid):
            for a in range(self.grid):
                k = self.shift(a, r)
                if k is not None:
                    layer = int(k > 0)
                    pairs.append(
                        tuple((p * self.grid + a) * 2 + layer for p in (r, r ^ by))
                    )
        return pairs

    def taken(self, a, layer, stage):
        l = jnp.where(layer == 0, a - stage, a + stage)
        if self.whole:
            valid = (l >= 0) & (l < self.grid)
        else:
            valid = jnp.where(layer == 0, stage <= self.half, stage < self.half)
        if stage == 0:
            valid = valid & (layer == 0)
        l = jnp.where(l < 0, l + self.grid, l)
        return jnp.where(l >= self.grid, l - self.grid, l), valid


def place():
    return tuple(lax.axis_index(n) for n in ("col", "row", "layer"))


def list_kernel(plan, bounds, rows_in, cols_in, pairs, rows, cols, keys, codes, sem):
    slots = rows.shape[2]
    stages = plan.stages + 1
    inputs = [
        pltpu.make_async_copy(rows_in, rows, sem.at[0]),
        pltpu.make_async_copy(cols_in, cols, sem.at[1]),
    ]
    for copy in inputs:
        copy.start()
    a, b, layer = place()
    lane = lax.broadcasted_iota(jnp.int32, (1, LANES), 1)
    down = lax.broadcasted_iota(jnp.int32, (LANES, LANES), 0)
    across = lax.broadcasted_iota(jnp.int32, (LANES, LANES), 1)

    def key_of(i, j):
        r, c = rows[i, pl.ds(j, 1), :], cols[i, pl.ds(j, 1), :]
        return 2 * r + (c != r).astype(jnp.int32)

    keys[...] = jnp.full_like(keys, -1)
    for copy in inputs:
        copy.wait()
    taken = []
    for stage in range(stages):
        l, valid = plan.taken(a, layer, stage)
        taken.append(valid)
        l = jnp.clip(l, 0, plan.grid - 1)
        keys[pl.ds(stage, 1), 0:slots] = key_of(a, l)
        keys[pl.ds(stages + stage, 1), 0:slots] = key_of(l, b)
    keys[pl.ds(2 * stages, 1), 0:slots] = key_of(a, b)
    out = keys[pl.ds(2 * stages, 1), :]
    out = jnp.where(lane < LANES // 2, out, pltpu.roll(out, LANES // 2, 1))
    slot = lane % (LANES // 2)
    r, d = out // 2, out % 2
    after = jnp.where(r + 1 == TB, 0, r + 1)
    second = lane >= LANES // 2
    left_key = jnp.where(second, 2 * r + 1, 2 * r)
    right_key = jnp.where(second, jnp.where(d == 1, 2 * after, -2), out)
    wanted = slot < slots
    left_key = jnp.where(wanted, left_key, -2)
    right_key = jnp.where(wanted, right_key, -2)
    columns = keys[...].T

    def find(column, key):
        hit = columns[:, column : column + 1] == key
        return jnp.sum(jnp.where(hit, down + 1, 0), axis=0, keepdims=True)

    codes[...] = jnp.zeros_like(codes)
    for stage in range(stages):
        left, right = find(stage, left_key), find(stages + stage, right_key)
        good = (left > 0) & (right > 0) & taken[stage]
        code = jnp.where(good, ((left - 1) * 64 + (right - 1)) * 64 + slot + 1, 0)
        if stage < plan.stages:
            codes[pl.ds(stage, 1), :] = code
        else:
            for j, (low, high) in enumerate(zip(bounds[:-1], bounds[1:])):
                here = (right > low) & (right <= high)
                codes[pl.ds(stage + j, 1), :] = jnp.where(here, code, 0)
    found = codes[...] > 0
    ahead = jnp.dot(
        found.astype(jnp.float32),
        (down < across).astype(jnp.float32),
        preferred_element_type=jnp.float32,
    ).astype(jnp.int32)
    order = jnp.where(found, ahead, -1).T
    entries = codes[...].T
    for stage in range(pairs.shape[0]):
        hit = order[:, stage : stage + 1] == across
        entry = jnp.where(hit, entries[:, stage : stage + 1], 0)
        entry = jnp.sum(entry, axis=0, keepdims=True)
        count = jnp.sum(
            found[stage : stage + 1].astype(jnp.int32), axis=1, keepdims=True
        )
        entry = jnp.where(lane < count, entry - 1, slots)
        pairs[pl.ds(stage, 1), :] = jnp.where(lane == LANES - 1, count, entry)


def add_products(count, pairs, row, left, right, acc, low=0):
    def step(i, carry):
        codes = [pairs[row, i * GROUP + j] for j in range(GROUP)]
        products = [
            jnp.dot(
                left[code // 4096],
                right[jnp.maximum((code // 64) % 64 - low, 0)],
                preferred_element_type=jnp.float32,
            )
            for code in codes
        ]
        for code, product in zip(codes, products):
            acc[code % 64] += product
        return carry

    lax.fori_loop(0, (count + GROUP - 1) // GROUP, step, 0)


def fetch(copies, buffer, sem):
    at = 0
    for j, ref in enumerate(copies):
        pltpu.make_async_copy(
            ref, buffer.at[pl.ds(at, ref.shape[0])], sem.at[j]
        ).start()
        at += ref.shape[0]


def fetched(copies, buffer, sem):
    at = 0
    for j, ref in enumerate(copies):
        pltpu.make_async_copy(
            ref, buffer.at[pl.ds(at, ref.shape[0])], sem.at[j]
        ).wait()
        at += ref.shape[0]


def fetch_left(lefts, by, buffer, sem):
    for n, ref in lefts.items():

        @pl.when(by == n)
        def _(ref=ref):
            pltpu.make_async_copy(ref, buffer, sem).start()


def early_kernel(plan, parts, pairs, *refs):
    far = plan.grid - 1
    lefts = dict(enumerate(refs[:far]))
    refs = refs[far:]
    rights = []
    for n in parts:
        rights.append(refs[:n])
        refs = refs[n:]
    acc, left, right, left_sem, right_sem = refs
    a, b, layer = place()
    last = pairs.shape[1] - 1
    jobs = []
    for stage in range(plan.stages):
        l, _ = plan.taken(a, layer, stage)
        by = b ^ l
        count = jnp.where(by == far, 0, pairs[stage, last])
        jobs.append((stage, by, count))

        @pl.when(count > 0)
        def _(stage=stage, by=by):
            fetch(rights[stage], right.at[stage], right_sem.at[stage])
            fetch_left(lefts, by, left.at[stage], left_sem.at[stage])

    acc[...] = jnp.zeros_like(acc)
    for stage, by, count in jobs:

        @pl.when(count > 0)
        def _(stage=stage, count=count):
            pltpu.make_async_copy(
                lefts[0], left.at[stage], left_sem.at[stage]
            ).wait()
            fetched(rights[stage], right.at[stage], right_sem.at[stage])
            add_products(
                count, pairs, stage, left.at[stage], right.at[stage], acc
            )


def middle_kernel(plan, parts, pairs, total, *refs):
    del total
    lefts = dict(enumerate(refs[: plan.grid]))
    refs = refs[plan.grid :]
    rights = []
    for n in parts[:-1]:
        rights.append(refs[:n])
        refs = refs[n:]
    first, acc, left_last, right, left_sem, right_sem = refs
    far, end, last = plan.grid - 1, plan.stages, pairs.shape[1] - 1
    a, b, layer = place()
    l, _ = plan.taken(a, layer, end)
    fetch_left(lefts, b ^ l, left_last, left_sem)
    counts = []
    for stage in range(end):
        l, _ = plan.taken(a, layer, stage)
        count = jnp.where(b ^ l == far, pairs[stage, last], 0)
        counts.append(count)

        @pl.when(count > 0)
        def _(stage=stage):
            fetch(rights[stage], right, right_sem)

    pltpu.make_async_copy(lefts[0], left_last, left_sem).wait()
    add_products(pairs[end, last], pairs, end, left_last, first, acc)
    for stage, count in enumerate(counts):

        @pl.when(count > 0)
        def _(stage=stage, count=count):
            fetched(rights[stage], right, right_sem)
            add_products(count, pairs, stage, lefts[far], right, acc)


def last_kernel(plan, bounds, pairs, total, left_last, *refs):
    del total
    refs, (acc, mine, other) = refs[:-3], refs[-3:]
    last = pairs.shape[1] - 1
    for j, part in enumerate(refs):
        row = plan.stages + 1 + j
        add_products(pairs[row, last], pairs, row, left_last, part, acc, bounds[1 + j])
    layer = lax.axis_index("layer")
    share = mine.shape[0]
    mine[...] = acc[pl.ds(layer * share, share)]
    other[...] = acc[pl.ds((1 - layer) * share, share)]


def on_device(plan, x_blocks, slot_rows, slot_cols):
    own = x_blocks[0, 0]
    slots, size = own.shape[0], own.shape[1]
    share = slots // 2
    bounds = [slots * i // CHUNKS for i in range(CHUNKS + 1)]
    held = [
        (lax.optimization_barrier(own) if i else own)[i:j]
        for i, j in zip(bounds[:-1], bounds[1:])
    ]
    anywhere = pl.BlockSpec(memory_space=pl.ANY)
    scalars = pl.BlockSpec(memory_space=pltpu.SMEM)
    vmem = pl.BlockSpec(memory_space=pltpu.VMEM)
    compiler_params = pltpu.CompilerParams(vmem_limit_bytes=GRANT)
    tile_bytes = own.size * 2

    def cost(products, tiles):
        return pl.CostEstimate(
            flops=2 * size**3 * products,
            bytes_accessed=tiles * tile_bytes,
            transcendentals=0,
        )

    lists = pl.pallas_call(
        functools.partial(list_kernel, plan, bounds),
        out_shape=jax.ShapeDtypeStruct((plan.stages + CHUNKS, LANES), jnp.int32),
        in_specs=[pl.BlockSpec(memory_space=pltpu.HBM)] * 2,
        out_specs=vmem,
        scratch_shapes=[pltpu.VMEM(slot_rows.shape, jnp.int32)] * 2
        + [pltpu.VMEM((LANES, LANES), jnp.int32)] * 2
        + [pltpu.SemaphoreType.DMA((2,))],
        compiler_params=compiler_params,
        cost_estimate=cost(0, 2),
        name="list_products",
    )(slot_rows, slot_cols)
    rights = [[own]]
    for stage in range(1, plan.stages + 1):
        pairs = plan.hop_pairs(stage)
        arrived = []
        for part in held:
            arrived.append(lax.ppermute(part, ("col", "layer"), pairs))
        rights.append(arrived)
        held = list(arrived)
    everywhere = ("row", "col", "layer")
    lefts = [own]
    for by in range(1, plan.grid):
        lefts.append(lax.ppermute(own, everywhere, plan.row_pairs(by)))
    *near, far = lefts
    parts = [len(r) for r in rights]
    running = jax.ShapeDtypeStruct((slots + 1, size, size), jnp.float32)
    before = [part for stage in rights[:-1] for part in stage]
    total = pl.pallas_call(
        functools.partial(early_kernel, plan, parts[:-1]),
        out_shape=running,
        in_specs=[scalars] + [anywhere] * (len(near) + len(before)),
        out_specs=vmem,
        scratch_shapes=[
            pltpu.VMEM((plan.stages, *own.shape), own.dtype),
            pltpu.VMEM((plan.stages, *own.shape), own.dtype),
            pltpu.SemaphoreType.DMA((plan.stages,)),
            pltpu.SemaphoreType.DMA((plan.stages, CHUNKS)),
        ],
        compiler_params=compiler_params,
        cost_estimate=cost(slots * plan.stages, 2 * plan.stages),
        name="early_products",
    )(lists, *near, *before)
    first, *rest = rights[-1]
    total, left_last = pl.pallas_call(
        functools.partial(middle_kernel, plan, parts),
        out_shape=(running, jax.ShapeDtypeStruct(own.shape, own.dtype)),
        in_specs=[scalars, vmem]
        + [anywhere] * len(near)
        + [vmem]
        + [anywhere] * len(before)
        + [vmem],
        out_specs=(vmem, vmem),
        input_output_aliases={1: 0},
        scratch_shapes=[
            pltpu.VMEM(own.shape, own.dtype),
            pltpu.SemaphoreType.DMA,
            pltpu.SemaphoreType.DMA((CHUNKS,)),
        ],
        compiler_params=compiler_params,
        cost_estimate=cost(slots, 4),
        name="middle_products",
    )(lists, total, *near, far, *before, first)
    half = jax.ShapeDtypeStruct((share, size, size), jnp.float32)
    _, mine, other = pl.pallas_call(
        functools.partial(last_kernel, plan, bounds),
        out_shape=(running, half, half),
        in_specs=[scalars] + [vmem] * (2 + len(rest)),
        out_specs=(vmem, vmem, vmem),
        input_output_aliases={1: 0},
        compiler_params=compiler_params,
        cost_estimate=cost(slots // 2, 4),
        name="last_products",
    )(lists, total, left_last, *rest)
    received = lax.ppermute(other, "layer", [(0, 1), (1, 0)])
    return (mine + received).astype(jnp.bfloat16)[None, None]


def solution(mesh):
    plan = Plan(mesh)

    def body(*args):
        return on_device(plan, *args)

    in_specs = (P("col", "row", None, None, None), P(), P())
    out_specs = P("col", "row", "layer", None, None)
    return jax.shard_map(
        body, mesh=mesh, in_specs=in_specs, out_specs=out_specs, check_vma=False
    )
```

```python
import functools

import jax
import jax.numpy as jnp
from jax import lax
from jax.experimental import pallas as pl
from jax.experimental.pallas import tpu as pltpu
from jax.sharding import PartitionSpec as P

TB = 28
GROUP = 8
LANES = 128
GRANT = 16 << 20
CHUNKS = 2


class Plan:
    def __init__(self, mesh):
        self.grid = mesh.shape["row"]
        self.half = min(6, self.grid) // 2
        self.whole = 2 * self.half == self.grid
        self.stages = self.grid - 1 if self.whole else self.half

    def shift(self, a, l):
        if self.whole:
            return l - a
        mid = self.grid // 2
        k = (l - a + mid) % self.grid - mid
        return k if -self.half <= k < self.half else None

    def hop_pairs(self, stage):
        pairs = []
        for source in range(self.grid):
            for layer, step in ((0, 1), (1, -1)):
                target = source + step
                origin = target - step * stage
                if self.whole and not (0 <= target < self.grid and 0 <= origin < self.grid):
                    continue
                target %= self.grid
                if self.shift(target, origin % self.grid) == -step * stage:
                    pairs.append((source * 2 + layer, target * 2 + layer))
        return pairs

    def row_pairs(self, bys):
        pairs = []
        for r in range(self.grid):
            for a in range(self.grid):
                if self.shift(a, r) is not None:
                    for layer, by in enumerate(bys):
                        pairs.append(
                            tuple(
                                (p * self.grid + a) * 2 + layer for p in (r, r ^ by)
                            )
                        )
        return pairs

    def taken(self, a, layer, stage):
        l = jnp.where(layer == 0, a - stage, a + stage)
        if self.whole:
            valid = (l >= 0) & (l < self.grid)
        else:
            valid = jnp.where(layer == 0, stage <= self.half, stage < self.half)
        if stage == 0:
            valid = valid & (layer == 0)
        l = jnp.where(l < 0, l + self.grid, l)
        return jnp.where(l >= self.grid, l - self.grid, l), valid


def place():
    return tuple(lax.axis_index(n) for n in ("col", "row", "layer"))


def list_kernel(plan, bounds, slot_keys, pairs, keys, codes):
    slots = slot_keys.shape[2]
    stages = plan.stages + 1
    a, b, layer = place()
    lane = lax.broadcasted_iota(jnp.int32, (1, LANES), 1)
    down = lax.broadcasted_iota(jnp.int32, (LANES, LANES), 0)
    across = lax.broadcasted_iota(jnp.int32, (LANES, LANES), 1)

    keys[...] = jnp.full_like(keys, -1)
    taken = []
    for stage in range(stages):
        l, valid = plan.taken(a, layer, stage)
        taken.append(valid)
        l = jnp.clip(l, 0, plan.grid - 1)
        keys[pl.ds(stage, 1), 0:slots] = slot_keys[a, pl.ds(l, 1), :]
        keys[pl.ds(stages + stage, 1), 0:slots] = slot_keys[l, pl.ds(b, 1), :]
    keys[pl.ds(2 * stages, 1), 0:slots] = slot_keys[a, pl.ds(b, 1), :]
    out = keys[pl.ds(2 * stages, 1), :]
    out = jnp.where(lane < LANES // 2, out, pltpu.roll(out, LANES // 2, 1))
    slot = lane % (LANES // 2)
    r, d = out // 2, out % 2
    after = jnp.where(r + 1 == TB, 0, r + 1)
    second = lane >= LANES // 2
    left_key = jnp.where(second, 2 * r + 1, 2 * r)
    right_key = jnp.where(second, jnp.where(d == 1, 2 * after, -2), out)
    wanted = slot < slots
    left_key = jnp.where(wanted, left_key, -2)
    right_key = jnp.where(wanted, right_key, -2)
    columns = keys[...].T

    def find(column, key):
        hit = columns[:, column : column + 1] == key
        return jnp.sum(jnp.where(hit, down + 1, 0), axis=0, keepdims=True)

    codes[...] = jnp.zeros_like(codes)
    for stage in range(stages):
        left, right = find(stage, left_key), find(stages + stage, right_key)
        good = (left > 0) & (right > 0) & taken[stage]
        code = jnp.where(good, ((left - 1) * 64 + (right - 1)) * 64 + slot + 1, 0)
        if stage < plan.stages:
            codes[pl.ds(stage, 1), :] = code
        else:
            for j, (low, high) in enumerate(zip(bounds[:-1], bounds[1:])):
                here = (right > low) & (right <= high)
                codes[pl.ds(stage + j, 1), :] = jnp.where(here, code, 0)
    found = codes[...] > 0
    ahead = jnp.dot(
        found.astype(jnp.float32),
        (down < across).astype(jnp.float32),
        preferred_element_type=jnp.float32,
    ).astype(jnp.int32)
    order = jnp.where(found, ahead, -1).T
    entries = codes[...].T
    for stage in range(pairs.shape[0]):
        hit = order[:, stage : stage + 1] == across
        entry = jnp.where(hit, entries[:, stage : stage + 1], 0)
        entry = jnp.sum(entry, axis=0, keepdims=True)
        count = jnp.sum(
            found[stage : stage + 1].astype(jnp.int32), axis=1, keepdims=True
        )
        entry = jnp.where(lane < count, entry - 1, slots)
        pairs[pl.ds(stage, 1), :] = jnp.where(lane == LANES - 1, count, entry)


def add_products(count, pairs, row, left, right, acc, low=0):
    def step(i, carry):
        codes = [pairs[row, i * GROUP + j] for j in range(GROUP)]
        products = [
            jnp.dot(
                left[code // 4096],
                right[jnp.maximum((code // 64) % 64 - low, 0)],
                preferred_element_type=jnp.float32,
            )
            for code in codes
        ]
        for code, product in zip(codes, products):
            acc[code % 64] += product
        return carry

    lax.fori_loop(0, (count + GROUP - 1) // GROUP, step, 0)


def fetch(copies, buffer, sem):
    at = 0
    for j, ref in enumerate(copies):
        pltpu.make_async_copy(
            ref, buffer.at[pl.ds(at, ref.shape[0])], sem.at[j]
        ).start()
        at += ref.shape[0]


def fetched(copies, buffer, sem):
    at = 0
    for j, ref in enumerate(copies):
        pltpu.make_async_copy(
            ref, buffer.at[pl.ds(at, ref.shape[0])], sem.at[j]
        ).wait()
        at += ref.shape[0]


def fetch_left(lefts, by, layer, buffer, sem):
    own, near, swapped = lefts
    at = 2 * by + layer

    @pl.when(by == 0)
    def _():
        pltpu.make_async_copy(own, buffer, sem).start()

    for k in range(len(near)):

        @pl.when((at == 4 * k + 2) | (at == 4 * k + 5))
        def _(k=k):
            pltpu.make_async_copy(near[k], buffer, sem).start()

        @pl.when((at == 4 * k + 3) | (at == 4 * k + 4))
        def _(k=k):
            pltpu.make_async_copy(swapped[k], buffer, sem).start()


def split_lefts(plan, refs):
    near = plan.grid // 2 - 1
    return (refs[0], refs[1 : 1 + near], refs[1 + near : 1 + 2 * near]), refs[
        1 + 2 * near :
    ]


def early_kernel(plan, parts, pairs, *refs):
    far = plan.grid - 1
    lefts, refs = split_lefts(plan, refs)
    rights = []
    for n in parts:
        rights.append(refs[:n])
        refs = refs[n:]
    acc, left, right, left_sem, right_sem = refs
    a, b, layer = place()
    last = pairs.shape[1] - 1
    jobs = []
    for stage in range(plan.stages):
        l, _ = plan.taken(a, layer, stage)
        by = b ^ l
        count = jnp.where(by == far, 0, pairs[stage, last])
        jobs.append((stage, by, count))

        @pl.when(count > 0)
        def _(stage=stage, by=by):
            fetch(rights[stage], right.at[stage], right_sem.at[stage])
            fetch_left(lefts, by, layer, left.at[stage], left_sem.at[stage])

    acc[...] = jnp.zeros_like(acc)
    for stage, by, count in jobs:

        @pl.when(count > 0)
        def _(stage=stage, count=count):
            pltpu.make_async_copy(
                lefts[0], left.at[stage], left_sem.at[stage]
            ).wait()
            fetched(rights[stage], right.at[stage], right_sem.at[stage])
            add_products(
                count, pairs, stage, left.at[stage], right.at[stage], acc
            )


def middle_kernel(plan, parts, pairs, total, *refs):
    del total
    lefts, refs = split_lefts(plan, refs)
    halves, refs = refs[:2], refs[2:]
    rights = []
    for n in parts[:-1]:
        rights.append(refs[:n])
        refs = refs[n:]
    first, acc, left_last, left, right, left_sem, far_sem, right_sem = refs
    far, end, last = plan.grid - 1, plan.stages, pairs.shape[1] - 1
    a, b, layer = place()
    share = halves[0].shape[0]

    def far_copies(buffer):
        return [
            pltpu.make_async_copy(
                half, buffer.at[pl.ds(jnp.abs(layer - j) * share, share)], far_sem.at[j]
            )
            for j, half in enumerate(halves)
        ]

    l, _ = plan.taken(a, layer, end)
    end_by = b ^ l
    fetch_left(lefts, end_by, layer, left_last, left_sem)

    @pl.when(end_by == far)
    def _():
        for copy in far_copies(left_last):
            copy.start()

    counts = []
    for stage in range(end):
        l, _ = plan.taken(a, layer, stage)
        count = jnp.where(b ^ l == far, pairs[stage, last], 0)
        counts.append(count)

        @pl.when(count > 0)
        def _(stage=stage):
            fetch(rights[stage], right, right_sem)
            for copy in far_copies(left):
                copy.start()

    @pl.when(end_by == far)
    def _():
        for copy in far_copies(left_last):
            copy.wait()

    @pl.when(end_by != far)
    def _():
        pltpu.make_async_copy(lefts[0], left_last, left_sem).wait()

    add_products(pairs[end, last], pairs, end, left_last, first, acc)
    for stage, count in enumerate(counts):

        @pl.when(count > 0)
        def _(stage=stage, count=count):
            fetched(rights[stage], right, right_sem)
            for copy in far_copies(left):
                copy.wait()
            add_products(count, pairs, stage, left, right, acc)


def last_kernel(plan, bounds, pairs, total, left_last, *refs):
    del total
    refs, (acc, mine, other) = refs[:-3], refs[-3:]
    last = pairs.shape[1] - 1
    for j, part in enumerate(refs):
        row = plan.stages + 1 + j
        add_products(pairs[row, last], pairs, row, left_last, part, acc, bounds[1 + j])
    layer = lax.axis_index("layer")
    share = mine.shape[0]
    mine[...] = acc[pl.ds(layer * share, share)]
    other[...] = acc[pl.ds((1 - layer) * share, share)]


def on_device(plan, x_blocks, slot_rows, slot_cols):
    own = x_blocks[0, 0]
    slots, size = own.shape[0], own.shape[1]
    share = slots // 2
    bounds = [slots * i // CHUNKS for i in range(CHUNKS + 1)]
    held = [
        (lax.optimization_barrier(own) if i else own)[i:j]
        for i, j in zip(bounds[:-1], bounds[1:])
    ]
    anywhere = pl.BlockSpec(memory_space=pl.ANY)
    scalars = pl.BlockSpec(memory_space=pltpu.SMEM)
    vmem = pl.BlockSpec(memory_space=pltpu.VMEM)
    compiler_params = pltpu.CompilerParams(vmem_limit_bytes=GRANT)
    tile_bytes = own.size * 2

    def cost(products, tiles):
        return pl.CostEstimate(
            flops=2 * size**3 * products,
            bytes_accessed=tiles * tile_bytes,
            transcendentals=0,
        )

    lists = pl.pallas_call(
        functools.partial(list_kernel, plan, bounds),
        out_shape=jax.ShapeDtypeStruct((plan.stages + CHUNKS, LANES), jnp.int32),
        in_specs=[vmem],
        out_specs=vmem,
        scratch_shapes=[pltpu.VMEM((LANES, LANES), jnp.int32)] * 2,
        compiler_params=compiler_params,
        cost_estimate=cost(0, 2),
        name="list_products",
    )(2 * slot_rows + (slot_cols != slot_rows))
    halves = list(held)
    rights = [[own]]
    for stage in range(1, plan.stages + 1):
        pairs = plan.hop_pairs(stage)
        arrived = []
        for part in held:
            arrived.append(lax.ppermute(part, ("col", "layer"), pairs))
        rights.append(arrived)
        held = list(arrived)
    everywhere = ("row", "col", "layer")
    swap = [(0, 1), (1, 0)]
    far = plan.grid - 1
    near, swapped = [], []
    for k in range(plan.grid // 2 - 1):
        bys = (2 * k + 1, 2 * k + 2)
        near.append(lax.ppermute(own, everywhere, plan.row_pairs(bys)))
        swapped.append(lax.ppermute(near[-1], "layer", swap))
    sent = jnp.where(
        lax.axis_index("layer") == 0, *lax.optimization_barrier(halves)
    )
    far_half = lax.ppermute(sent, everywhere, plan.row_pairs((far, far)))
    far_swapped = lax.ppermute(far_half, "layer", swap)
    lefts = [own, *near, *swapped]
    parts = [len(r) for r in rights]
    running = jax.ShapeDtypeStruct((slots + 1, size, size), jnp.float32)
    before = [part for stage in rights[:-1] for part in stage]
    total = pl.pallas_call(
        functools.partial(early_kernel, plan, parts[:-1]),
        out_shape=running,
        in_specs=[scalars] + [anywhere] * (len(lefts) + len(before)),
        out_specs=vmem,
        scratch_shapes=[
            pltpu.VMEM((plan.stages, *own.shape), own.dtype),
            pltpu.VMEM((plan.stages, *own.shape), own.dtype),
            pltpu.SemaphoreType.DMA((plan.stages,)),
            pltpu.SemaphoreType.DMA((plan.stages, CHUNKS)),
        ],
        compiler_params=compiler_params,
        cost_estimate=cost(slots * plan.stages, 2 * plan.stages),
        name="early_products",
    )(lists, *lefts, *before)
    first, *rest = rights[-1]
    total, left_last = pl.pallas_call(
        functools.partial(middle_kernel, plan, parts),
        out_shape=(running, jax.ShapeDtypeStruct(own.shape, own.dtype)),
        in_specs=[scalars, vmem]
        + [anywhere] * (len(lefts) + 2 + len(before))
        + [vmem],
        out_specs=(vmem, vmem),
        input_output_aliases={1: 0},
        scratch_shapes=[
            pltpu.VMEM(own.shape, own.dtype),
            pltpu.VMEM(own.shape, own.dtype),
            pltpu.SemaphoreType.DMA,
            pltpu.SemaphoreType.DMA((2,)),
            pltpu.SemaphoreType.DMA((CHUNKS,)),
        ],
        compiler_params=compiler_params,
        cost_estimate=cost(slots, 4),
        name="middle_products",
    )(lists, total, *lefts, far_half, far_swapped, *before, first)
    half = jax.ShapeDtypeStruct((share, size, size), jnp.float32)
    _, mine, other = pl.pallas_call(
        functools.partial(last_kernel, plan, bounds),
        out_shape=(running, half, half),
        in_specs=[scalars] + [vmem] * (2 + len(rest)),
        out_specs=(vmem, vmem, vmem),
        input_output_aliases={1: 0},
        compiler_params=compiler_params,
        cost_estimate=cost(slots // 2, 4),
        name="last_products",
    )(lists, total, left_last, *rest)
    received = lax.ppermute(other, "layer", swap)
    return (mine + received).astype(jnp.bfloat16)[None, None]


def solution(mesh):
    plan = Plan(mesh)

    def body(*args):
        return on_device(plan, *args)

    in_specs = (P("col", "row", None, None, None), P(), P())
    out_specs = P("col", "row", "layer", None, None)
    return jax.shard_map(
        body, mesh=mesh, in_specs=in_specs, out_specs=out_specs, check_vma=False
    )
```

```python
import functools

import jax
import jax.numpy as jnp
from jax import lax
from jax.experimental import pallas as pl
from jax.experimental.pallas import tpu as pltpu
from jax.sharding import PartitionSpec as P

TB = 28
GROUP = 8
LANES = 128
GRANT = 16 << 20
CHUNKS = 2


class Plan:
    def __init__(self, mesh):
        self.grid = mesh.shape["row"]
        self.half = min(6, self.grid) // 2
        self.whole = 2 * self.half == self.grid
        self.stages = self.grid - 1 if self.whole else self.half

    def shift(self, a, l):
        if self.whole:
            return l - a
        mid = self.grid // 2
        k = (l - a + mid) % self.grid - mid
        return k if -self.half <= k < self.half else None

    def hop_pairs(self, stage):
        pairs = []
        for source in range(self.grid):
            for layer, step in ((0, 1), (1, -1)):
                target = source + step
                origin = target - step * stage
                if self.whole and not (0 <= target < self.grid and 0 <= origin < self.grid):
                    continue
                target %= self.grid
                if self.shift(target, origin % self.grid) == -step * stage:
                    pairs.append((source * 2 + layer, target * 2 + layer))
        return pairs

    def near_pairs(self, bys):
        pairs = []
        for r in range(self.grid):
            for a in range(self.grid):
                if self.shift(a, r) is not None:
                    for layer, by in enumerate(bys):
                        pairs.append(
                            tuple(
                                (p * self.grid + a) * 2 + layer for p in (r, r ^ by)
                            )
                        )
        return pairs

    def far_pairs(self):
        pairs = []
        for r in range(self.grid):
            for a in range(self.grid):
                k = self.shift(a, r)
                if k is not None:
                    pairs.append(
                        tuple(
                            (p * self.grid + a) * 2 + int(k > 0)
                            for p in (r, r ^ (self.grid - 1))
                        )
                    )
        return pairs

    def taken(self, a, layer, stage):
        l = jnp.where(layer == 0, a - stage, a + stage)
        if self.whole:
            valid = (l >= 0) & (l < self.grid)
        else:
            valid = jnp.where(layer == 0, stage <= self.half, stage < self.half)
        if stage == 0:
            valid = valid & (layer == 0)
        l = jnp.where(l < 0, l + self.grid, l)
        return jnp.where(l >= self.grid, l - self.grid, l), valid


def place():
    return tuple(lax.axis_index(n) for n in ("col", "row", "layer"))


def list_kernel(plan, bounds, slot_keys, pairs, keys, codes):
    slots = slot_keys.shape[2]
    stages = plan.stages + 1
    a, b, layer = place()
    lane = lax.broadcasted_iota(jnp.int32, (1, LANES), 1)
    down = lax.broadcasted_iota(jnp.int32, (LANES, LANES), 0)
    across = lax.broadcasted_iota(jnp.int32, (LANES, LANES), 1)

    keys[...] = jnp.full_like(keys, -1)
    taken = []
    for stage in range(stages):
        l, valid = plan.taken(a, layer, stage)
        taken.append(valid)
        l = jnp.clip(l, 0, plan.grid - 1)
        keys[pl.ds(stage, 1), 0:slots] = slot_keys[a, pl.ds(l, 1), :]
        keys[pl.ds(stages + stage, 1), 0:slots] = slot_keys[l, pl.ds(b, 1), :]
    keys[pl.ds(2 * stages, 1), 0:slots] = slot_keys[a, pl.ds(b, 1), :]
    out = keys[pl.ds(2 * stages, 1), :]
    out = jnp.where(lane < LANES // 2, out, pltpu.roll(out, LANES // 2, 1))
    slot = lane % (LANES // 2)
    r, d = out // 2, out % 2
    after = jnp.where(r + 1 == TB, 0, r + 1)
    second = lane >= LANES // 2
    left_key = jnp.where(second, 2 * r + 1, 2 * r)
    right_key = jnp.where(second, jnp.where(d == 1, 2 * after, -2), out)
    wanted = slot < slots
    left_key = jnp.where(wanted, left_key, -2)
    right_key = jnp.where(wanted, right_key, -2)
    columns = keys[...].T

    def find(column, key):
        hit = columns[:, column : column + 1] == key
        return jnp.sum(jnp.where(hit, down + 1, 0), axis=0, keepdims=True)

    codes[...] = jnp.zeros_like(codes)
    for stage in range(stages):
        left, right = find(stage, left_key), find(stages + stage, right_key)
        good = (left > 0) & (right > 0) & taken[stage]
        code = jnp.where(good, ((left - 1) * 64 + (right - 1)) * 64 + slot + 1, 0)
        if stage < plan.stages:
            codes[pl.ds(stage, 1), :] = code
        else:
            for j, (low, high) in enumerate(zip(bounds[:-1], bounds[1:])):
                here = (right > low) & (right <= high)
                codes[pl.ds(stage + j, 1), :] = jnp.where(here, code, 0)
    found = codes[...] > 0
    ahead = jnp.dot(
        found.astype(jnp.float32),
        (down < across).astype(jnp.float32),
        preferred_element_type=jnp.float32,
    ).astype(jnp.int32)
    order = jnp.where(found, ahead, -1).T
    entries = codes[...].T
    for stage in range(pairs.shape[0]):
        hit = order[:, stage : stage + 1] == across
        entry = jnp.where(hit, entries[:, stage : stage + 1], 0)
        entry = jnp.sum(entry, axis=0, keepdims=True)
        count = jnp.sum(
            found[stage : stage + 1].astype(jnp.int32), axis=1, keepdims=True
        )
        entry = jnp.where(lane < count, entry - 1, slots)
        pairs[pl.ds(stage, 1), :] = jnp.where(lane == LANES - 1, count, entry)


def add_products(count, pairs, row, left, right, acc, low=0):
    def step(i, carry):
        codes = [pairs[row, i * GROUP + j] for j in range(GROUP)]
        products = [
            jnp.dot(
                left[code // 4096],
                right[jnp.maximum((code // 64) % 64 - low, 0)],
                preferred_element_type=jnp.float32,
            )
            for code in codes
        ]
        for code, product in zip(codes, products):
            acc[code % 64] += product
        return carry

    lax.fori_loop(0, (count + GROUP - 1) // GROUP, step, 0)


def fetch(copies, buffer, sem):
    at = 0
    for j, ref in enumerate(copies):
        pltpu.make_async_copy(
            ref, buffer.at[pl.ds(at, ref.shape[0])], sem.at[j]
        ).start()
        at += ref.shape[0]


def fetched(copies, buffer, sem):
    at = 0
    for j, ref in enumerate(copies):
        pltpu.make_async_copy(
            ref, buffer.at[pl.ds(at, ref.shape[0])], sem.at[j]
        ).wait()
        at += ref.shape[0]


def fetch_left(lefts, by, layer, buffer, sem):
    own, near, swapped = lefts
    at = 2 * by + layer

    @pl.when(by == 0)
    def _():
        pltpu.make_async_copy(own, buffer, sem).start()

    for k in range(len(near)):

        @pl.when((at == 4 * k + 2) | (at == 4 * k + 5))
        def _(k=k):
            pltpu.make_async_copy(near[k], buffer, sem).start()

        @pl.when((at == 4 * k + 3) | (at == 4 * k + 4))
        def _(k=k):
            pltpu.make_async_copy(swapped[k], buffer, sem).start()


def split_lefts(plan, refs):
    near = plan.grid // 2 - 1
    return (refs[0], refs[1 : 1 + near], refs[1 + near : 1 + 2 * near]), refs[
        1 + 2 * near :
    ]


def early_kernel(plan, parts, pairs, *refs):
    far = plan.grid - 1
    lefts, refs = split_lefts(plan, refs)
    rights = []
    for n in parts:
        rights.append(refs[:n])
        refs = refs[n:]
    acc, left, right, left_sem, right_sem = refs
    a, b, layer = place()
    last = pairs.shape[1] - 1
    jobs = []
    for stage in range(plan.stages):
        l, _ = plan.taken(a, layer, stage)
        by = b ^ l
        count = jnp.where(by == far, 0, pairs[stage, last])
        jobs.append((stage, by, count))

        @pl.when(count > 0)
        def _(stage=stage, by=by):
            fetch(rights[stage], right.at[stage], right_sem.at[stage])
            fetch_left(lefts, by, layer, left.at[stage], left_sem.at[stage])

    acc[...] = jnp.zeros_like(acc)
    for stage, by, count in jobs:

        @pl.when(count > 0)
        def _(stage=stage, count=count):
            pltpu.make_async_copy(
                lefts[0], left.at[stage], left_sem.at[stage]
            ).wait()
            fetched(rights[stage], right.at[stage], right_sem.at[stage])
            add_products(
                count, pairs, stage, left.at[stage], right.at[stage], acc
            )


def middle_kernel(plan, parts, pairs, total, *refs):
    del total
    lefts, refs = split_lefts(plan, refs)
    far_tile, *refs = refs
    rights = []
    for n in parts[:-1]:
        rights.append(refs[:n])
        refs = refs[n:]
    first, acc, left_last, right, left_sem, right_sem = refs
    far, end, last = plan.grid - 1, plan.stages, pairs.shape[1] - 1
    a, b, layer = place()
    l, _ = plan.taken(a, layer, end)
    end_by = b ^ l
    fetch_left(lefts, end_by, layer, left_last, left_sem)

    @pl.when(end_by == far)
    def _():
        pltpu.make_async_copy(far_tile, left_last, left_sem).start()

    counts = []
    for stage in range(end):
        l, _ = plan.taken(a, layer, stage)
        count = jnp.where(b ^ l == far, pairs[stage, last], 0)
        counts.append(count)

        @pl.when(count > 0)
        def _(stage=stage):
            fetch(rights[stage], right, right_sem)

    pltpu.make_async_copy(far_tile, left_last, left_sem).wait()
    add_products(pairs[end, last], pairs, end, left_last, first, acc)
    for stage, count in enumerate(counts):

        @pl.when(count > 0)
        def _(stage=stage, count=count):
            fetched(rights[stage], right, right_sem)
            add_products(count, pairs, stage, far_tile, right, acc)


def last_kernel(plan, bounds, pairs, total, left_last, *refs):
    del total
    refs, (acc, mine, other) = refs[:-3], refs[-3:]
    last = pairs.shape[1] - 1
    for j, part in enumerate(refs):
        row = plan.stages + 1 + j
        add_products(pairs[row, last], pairs, row, left_last, part, acc, bounds[1 + j])
    layer = lax.axis_index("layer")
    share = mine.shape[0]
    mine[...] = acc[pl.ds(layer * share, share)]
    other[...] = acc[pl.ds((1 - layer) * share, share)]


def on_device(plan, x_blocks, slot_rows, slot_cols):
    own = x_blocks[0, 0]
    slots, size = own.shape[0], own.shape[1]
    share = slots // 2
    bounds = [slots * i // CHUNKS for i in range(CHUNKS + 1)]
    held = [
        (lax.optimization_barrier(own) if i else own)[i:j]
        for i, j in zip(bounds[:-1], bounds[1:])
    ]
    anywhere = pl.BlockSpec(memory_space=pl.ANY)
    scalars = pl.BlockSpec(memory_space=pltpu.SMEM)
    vmem = pl.BlockSpec(memory_space=pltpu.VMEM)
    compiler_params = pltpu.CompilerParams(vmem_limit_bytes=GRANT)
    tile_bytes = own.size * 2

    def cost(products, tiles):
        return pl.CostEstimate(
            flops=2 * size**3 * products,
            bytes_accessed=tiles * tile_bytes,
            transcendentals=0,
        )

    lists = pl.pallas_call(
        functools.partial(list_kernel, plan, bounds),
        out_shape=jax.ShapeDtypeStruct((plan.stages + CHUNKS, LANES), jnp.int32),
        in_specs=[vmem],
        out_specs=vmem,
        scratch_shapes=[pltpu.VMEM((LANES, LANES), jnp.int32)] * 2,
        compiler_params=compiler_params,
        cost_estimate=cost(0, 2),
        name="list_products",
    )(2 * slot_rows + (slot_cols != slot_rows))
    rights = [[own]]
    for stage in range(1, plan.stages + 1):
        pairs = plan.hop_pairs(stage)
        arrived = []
        for part in held:
            arrived.append(lax.ppermute(part, ("col", "layer"), pairs))
        rights.append(arrived)
        held = list(arrived)
    everywhere = ("row", "col", "layer")
    swap = [(0, 1), (1, 0)]
    near, swapped = [], []
    for k in range(plan.grid // 2 - 1):
        bys = (2 * k + 1, 2 * k + 2)
        near.append(lax.ppermute(own, everywhere, plan.near_pairs(bys)))
        swapped.append(lax.ppermute(near[-1], "layer", swap))
    far = lax.ppermute(own, everywhere, plan.far_pairs())
    lefts = [own, *near, *swapped]
    parts = [len(r) for r in rights]
    running = jax.ShapeDtypeStruct((slots + 1, size, size), jnp.float32)
    before = [part for stage in rights[:-1] for part in stage]
    total = pl.pallas_call(
        functools.partial(early_kernel, plan, parts[:-1]),
        out_shape=running,
        in_specs=[scalars] + [anywhere] * (len(lefts) + len(before)),
        out_specs=vmem,
        scratch_shapes=[
            pltpu.VMEM((plan.stages, *own.shape), own.dtype),
            pltpu.VMEM((plan.stages, *own.shape), own.dtype),
            pltpu.SemaphoreType.DMA((plan.stages,)),
            pltpu.SemaphoreType.DMA((plan.stages, CHUNKS)),
        ],
        compiler_params=compiler_params,
        cost_estimate=cost(slots * plan.stages, 2 * plan.stages),
        name="early_products",
    )(lists, *lefts, *before)
    first, *rest = rights[-1]
    total, left_last = pl.pallas_call(
        functools.partial(middle_kernel, plan, parts),
        out_shape=(running, jax.ShapeDtypeStruct(own.shape, own.dtype)),
        in_specs=[scalars, vmem]
        + [anywhere] * len(lefts)
        + [vmem]
        + [anywhere] * len(before)
        + [vmem],
        out_specs=(vmem, vmem),
        input_output_aliases={1: 0},
        scratch_shapes=[
            pltpu.VMEM(own.shape, own.dtype),
            pltpu.SemaphoreType.DMA,
            pltpu.SemaphoreType.DMA((CHUNKS,)),
        ],
        compiler_params=compiler_params,
        cost_estimate=cost(slots, 4),
        name="middle_products",
    )(lists, total, *lefts, far, *before, first)
    half = jax.ShapeDtypeStruct((share, size, size), jnp.float32)
    _, mine, other = pl.pallas_call(
        functools.partial(last_kernel, plan, bounds),
        out_shape=(running, half, half),
        in_specs=[scalars] + [vmem] * (2 + len(rest)),
        out_specs=(vmem, vmem, vmem),
        input_output_aliases={1: 0},
        compiler_params=compiler_params,
        cost_estimate=cost(slots // 2, 4),
        name="last_products",
    )(lists, total, left_last, *rest)
    received = lax.ppermute(other, "layer", swap)
    return (mine + received).astype(jnp.bfloat16)[None, None]


def solution(mesh):
    plan = Plan(mesh)

    def body(*args):
        return on_device(plan, *args)

    in_specs = (P("col", "row", None, None, None), P(), P())
    out_specs = P("col", "row", "layer", None, None)
    return jax.shard_map(
        body, mesh=mesh, in_specs=in_specs, out_specs=out_specs, check_vma=False
    )
```

```python
import functools

import jax
import jax.numpy as jnp
from jax import lax
from jax.experimental import pallas as pl
from jax.experimental.pallas import tpu as pltpu
from jax.sharding import PartitionSpec as P

TB = 28
GROUP = 8
LANES = 128
GRANT = 8 << 20
CHUNKS = 2


class Plan:
    def __init__(self, mesh):
        self.grid = mesh.shape["row"]
        self.half = min(6, self.grid) // 2
        self.whole = 2 * self.half == self.grid
        self.stages = self.grid - 1 if self.whole else self.half

    def shift(self, a, l):
        if self.whole:
            return l - a
        mid = self.grid // 2
        k = (l - a + mid) % self.grid - mid
        return k if -self.half <= k < self.half else None

    def hop_pairs(self, stage):
        pairs = []
        for source in range(self.grid):
            for layer, step in ((0, 1), (1, -1)):
                target = source + step
                origin = target - step * stage
                if self.whole and not (0 <= target < self.grid and 0 <= origin < self.grid):
                    continue
                target %= self.grid
                if self.shift(target, origin % self.grid) == -step * stage:
                    pairs.append((source * 2 + layer, target * 2 + layer))
        return pairs

    def near_pairs(self, bys):
        pairs = []
        for r in range(self.grid):
            for a in range(self.grid):
                if self.shift(a, r) is not None:
                    for layer, by in enumerate(bys):
                        pairs.append(
                            tuple(
                                (p * self.grid + a) * 2 + layer for p in (r, r ^ by)
                            )
                        )
        return pairs

    def far_pairs(self):
        far = self.grid - 1
        pairs = []
        for r in range(self.grid):
            for a in range(self.grid):
                if self.shift(a, r) is not None:
                    for layer, by in enumerate((1, 2)):
                        pairs.append(
                            tuple(
                                (p * self.grid + a) * 2 + layer
                                for p in (r ^ by, r ^ far)
                            )
                        )
        return pairs

    def taken(self, a, layer, stage):
        l = jnp.where(layer == 0, a - stage, a + stage)
        if self.whole:
            valid = (l >= 0) & (l < self.grid)
        else:
            valid = jnp.where(layer == 0, stage <= self.half, stage < self.half)
        if stage == 0:
            valid = valid & (layer == 0)
        l = jnp.where(l < 0, l + self.grid, l)
        return jnp.where(l >= self.grid, l - self.grid, l), valid


def place():
    return tuple(lax.axis_index(n) for n in ("col", "row", "layer"))


def list_kernel(plan, bounds, slot_keys, pairs, keys, codes):
    slots = slot_keys.shape[2]
    stages = plan.stages + 1
    a, b, layer = place()
    lane = lax.broadcasted_iota(jnp.int32, (1, LANES), 1)
    down = lax.broadcasted_iota(jnp.int32, (LANES, LANES), 0)
    across = lax.broadcasted_iota(jnp.int32, (LANES, LANES), 1)

    keys[...] = jnp.full_like(keys, -1)
    taken = []
    for stage in range(stages):
        l, valid = plan.taken(a, layer, stage)
        taken.append(valid)
        l = jnp.clip(l, 0, plan.grid - 1)
        keys[pl.ds(stage, 1), 0:slots] = slot_keys[a, pl.ds(l, 1), :]
        keys[pl.ds(stages + stage, 1), 0:slots] = slot_keys[l, pl.ds(b, 1), :]
    keys[pl.ds(2 * stages, 1), 0:slots] = slot_keys[a, pl.ds(b, 1), :]
    out = keys[pl.ds(2 * stages, 1), :]
    out = jnp.where(lane < LANES // 2, out, pltpu.roll(out, LANES // 2, 1))
    slot = lane % (LANES // 2)
    r, d = out // 2, out % 2
    after = jnp.where(r + 1 == TB, 0, r + 1)
    second = lane >= LANES // 2
    left_key = jnp.where(second, 2 * r + 1, 2 * r)
    right_key = jnp.where(second, jnp.where(d == 1, 2 * after, -2), out)
    wanted = slot < slots
    left_key = jnp.where(wanted, left_key, -2)
    right_key = jnp.where(wanted, right_key, -2)
    columns = keys[...].T

    def find(column, key):
        hit = columns[:, column : column + 1] == key
        return jnp.sum(jnp.where(hit, down + 1, 0), axis=0, keepdims=True)

    codes[...] = jnp.zeros_like(codes)
    for stage in range(stages):
        left, right = find(stage, left_key), find(stages + stage, right_key)
        good = (left > 0) & (right > 0) & taken[stage]
        code = jnp.where(good, ((left - 1) * 64 + (right - 1)) * 64 + slot + 1, 0)
        if stage < plan.stages:
            codes[pl.ds(stage, 1), :] = code
        else:
            for j, (low, high) in enumerate(zip(bounds[:-1], bounds[1:])):
                here = (right > low) & (right <= high)
                codes[pl.ds(stage + j, 1), :] = jnp.where(here, code, 0)
    found = codes[...] > 0
    ahead = jnp.dot(
        found.astype(jnp.float32),
        (down < across).astype(jnp.float32),
        preferred_element_type=jnp.float32,
    ).astype(jnp.int32)
    order = jnp.where(found, ahead, -1).T
    entries = codes[...].T
    for stage in range(pairs.shape[0]):
        hit = order[:, stage : stage + 1] == across
        entry = jnp.where(hit, entries[:, stage : stage + 1], 0)
        entry = jnp.sum(entry, axis=0, keepdims=True)
        count = jnp.sum(
            found[stage : stage + 1].astype(jnp.int32), axis=1, keepdims=True
        )
        entry = jnp.where(lane < count, entry - 1, slots)
        pairs[pl.ds(stage, 1), :] = jnp.where(lane == LANES - 1, count, entry)


def add_products(count, pairs, row, left, right, acc, low=0):
    def step(i, carry):
        codes = [pairs[row, i * GROUP + j] for j in range(GROUP)]
        products = [
            jnp.dot(
                left[code // 4096],
                right[jnp.maximum((code // 64) % 64 - low, 0)],
                preferred_element_type=jnp.float32,
            )
            for code in codes
        ]
        for code, product in zip(codes, products):
            acc[code % 64] += product
        return carry

    lax.fori_loop(0, (count + GROUP - 1) // GROUP, step, 0)


def fetch(copies, buffer, sem):
    at = 0
    for j, ref in enumerate(copies):
        pltpu.make_async_copy(
            ref, buffer.at[pl.ds(at, ref.shape[0])], sem.at[j]
        ).start()
        at += ref.shape[0]


def fetched(copies, buffer, sem):
    at = 0
    for j, ref in enumerate(copies):
        pltpu.make_async_copy(
            ref, buffer.at[pl.ds(at, ref.shape[0])], sem.at[j]
        ).wait()
        at += ref.shape[0]


class Lefts:
    def __init__(self, plan, refs, late):
        near = plan.grid // 2 - 1
        self.far = plan.grid - 1
        self.own, self.near = refs[0], refs[1 : 1 + near]
        self.late = late
        if late:
            self.swapped = refs[1 + near : 1 + 2 * near]
            self.halves = refs[1 + 2 * near : 3 + 2 * near]

    @staticmethod
    def number(plan, late):
        near = plan.grid // 2 - 1
        return 3 + 2 * near if late else 1 + near

    def direct(self, by, layer):
        found = by == 0
        for k in range(len(self.near)):
            found |= by == 2 * k + 1 + layer
        return found & (by != self.far)

    def fetch(self, by, layer, buffer, sem):
        @pl.when(by == 0)
        def _():
            pltpu.make_async_copy(self.own, buffer, sem).start()

        for k in range(len(self.near)):

            @pl.when(by == 2 * k + 1 + layer)
            def _(k=k):
                pltpu.make_async_copy(self.near[k], buffer, sem).start()

            if self.late:

                @pl.when(by == 2 * k + 2 - layer)
                def _(k=k):
                    pltpu.make_async_copy(self.swapped[k], buffer, sem).start()

        if self.late:

            @pl.when(by == self.far)
            def _():
                share = self.halves[0].shape[0]
                for j, half in enumerate(self.halves):
                    at = jnp.abs(layer - j) * share
                    pltpu.make_async_copy(
                        half, buffer.at[pl.ds(at, share)], sem
                    ).start()

    def fetched(self, buffer, sem):
        pltpu.make_async_copy(self.own, buffer, sem).wait()


def stages_of(parts, refs):
    rights = []
    for n in parts[:-1]:
        rights.append(refs[:n])
        refs = refs[n:]
    return rights, refs


def start_jobs(plan, lefts, rights, pairs, left, right, left_sem, right_sem, late):
    a, b, layer = place()
    counts = []
    for stage in range(plan.stages):
        l, _ = plan.taken(a, layer, stage)
        by = b ^ l
        here = lefts.direct(by, layer) != late
        count = jnp.where(here, pairs[stage, pairs.shape[1] - 1], 0)
        counts.append(count)

        @pl.when(count > 0)
        def _(stage=stage, by=by):
            fetch(rights[stage], right.at[stage], right_sem.at[stage])
            lefts.fetch(by, layer, left.at[stage], left_sem.at[stage])

    return counts


def finish_jobs(counts, lefts, rights, pairs, left, right, left_sem, right_sem, acc):
    for stage, count in enumerate(counts):

        @pl.when(count > 0)
        def _(stage=stage, count=count):
            lefts.fetched(left.at[stage], left_sem.at[stage])
            fetched(rights[stage], right.at[stage], right_sem.at[stage])
            add_products(count, pairs, stage, left.at[stage], right.at[stage], acc)


def early_kernel(plan, parts, pairs, *refs):
    n = Lefts.number(plan, False)
    lefts = Lefts(plan, refs[:n], False)
    rights, refs = stages_of(parts, refs[n:])
    acc, *buffers = refs
    counts = start_jobs(plan, lefts, rights, pairs, *buffers, False)
    acc[...] = jnp.zeros_like(acc)
    finish_jobs(counts, lefts, rights, pairs, *buffers, acc)


def middle_kernel(plan, parts, pairs, total, *refs):
    del total
    n = Lefts.number(plan, True)
    lefts = Lefts(plan, refs[:n], True)
    rights, refs = stages_of(parts, refs[n:])
    first, acc, left_last, *buffers, last_sem = refs
    end = plan.stages
    a, b, layer = place()
    l, _ = plan.taken(a, layer, end)
    counts = start_jobs(plan, lefts, rights, pairs, *buffers, True)
    lefts.fetch(b ^ l, layer, left_last, last_sem)
    finish_jobs(counts, lefts, rights, pairs, *buffers, acc)
    lefts.fetched(left_last, last_sem)
    add_products(pairs[end, pairs.shape[1] - 1], pairs, end, left_last, first, acc)


def last_kernel(plan, bounds, pairs, total, left_last, *refs):
    del total
    refs, (acc, mine, other) = refs[:-3], refs[-3:]
    last = pairs.shape[1] - 1
    for j, part in enumerate(refs):
        row = plan.stages + 1 + j
        add_products(pairs[row, last], pairs, row, left_last, part, acc, bounds[1 + j])
    layer = lax.axis_index("layer")
    share = mine.shape[0]
    mine[...] = acc[pl.ds(layer * share, share)]
    other[...] = acc[pl.ds((1 - layer) * share, share)]


def on_device(plan, x_blocks, slot_rows, slot_cols):
    own = x_blocks[0, 0]
    slots, size = own.shape[0], own.shape[1]
    share = slots // 2
    bounds = [slots * i // CHUNKS for i in range(CHUNKS + 1)]
    held = [
        (lax.optimization_barrier(own) if i else own)[i:j]
        for i, j in zip(bounds[:-1], bounds[1:])
    ]
    anywhere = pl.BlockSpec(memory_space=pl.ANY)
    scalars = pl.BlockSpec(memory_space=pltpu.SMEM)
    vmem = pl.BlockSpec(memory_space=pltpu.VMEM)
    compiler_params = pltpu.CompilerParams(vmem_limit_bytes=GRANT)
    tile_bytes = own.size * 2

    def cost(products, tiles):
        return pl.CostEstimate(
            flops=2 * size**3 * products,
            bytes_accessed=tiles * tile_bytes,
            transcendentals=0,
        )

    lists = pl.pallas_call(
        functools.partial(list_kernel, plan, bounds),
        out_shape=jax.ShapeDtypeStruct((plan.stages + CHUNKS, LANES), jnp.int32),
        in_specs=[vmem],
        out_specs=vmem,
        scratch_shapes=[pltpu.VMEM((LANES, LANES), jnp.int32)] * 2,
        compiler_params=compiler_params,
        cost_estimate=cost(0, 2),
        name="list_products",
    )(2 * slot_rows + (slot_cols != slot_rows))
    rights = [[own]]
    for stage in range(1, plan.stages + 1):
        pairs = plan.hop_pairs(stage)
        arrived = []
        for part in held:
            arrived.append(lax.ppermute(part, ("col", "layer"), pairs))
        rights.append(arrived)
        held = list(arrived)
    everywhere = ("row", "col", "layer")
    swap = [(0, 1), (1, 0)]
    near, swapped = [], []
    for k in range(plan.grid // 2 - 1):
        bys = (2 * k + 1, 2 * k + 2)
        near.append(lax.ppermute(own, everywhere, plan.near_pairs(bys)))
        swapped.append(lax.ppermute(near[-1], "layer", swap))
    sent = jnp.where(
        lax.axis_index("layer") == 0, near[0][:share], near[0][share:]
    )
    far = lax.ppermute(sent, everywhere, plan.far_pairs())
    far_swapped = lax.ppermute(far, "layer", swap)
    direct = [own, *near]
    lefts = [*direct, *swapped, far, far_swapped]
    parts = [len(r) for r in rights]
    running = jax.ShapeDtypeStruct((slots + 1, size, size), jnp.float32)
    before = [part for stage in rights[:-1] for part in stage]
    buffers = [
        pltpu.VMEM((plan.stages, *own.shape), own.dtype),
        pltpu.VMEM((plan.stages, *own.shape), own.dtype),
        pltpu.SemaphoreType.DMA((plan.stages,)),
        pltpu.SemaphoreType.DMA((plan.stages, CHUNKS)),
    ]
    total = pl.pallas_call(
        functools.partial(early_kernel, plan, parts),
        out_shape=running,
        in_specs=[scalars] + [anywhere] * (len(direct) + len(before)),
        out_specs=vmem,
        scratch_shapes=buffers,
        compiler_params=compiler_params,
        cost_estimate=cost(slots * plan.stages, 2 * plan.stages),
        name="early_products",
    )(lists, *direct, *before)
    first, *rest = rights[-1]
    total, left_last = pl.pallas_call(
        functools.partial(middle_kernel, plan, parts),
        out_shape=(running, jax.ShapeDtypeStruct(own.shape, own.dtype)),
        in_specs=[scalars, vmem]
        + [anywhere] * (len(lefts) + len(before))
        + [vmem],
        out_specs=(vmem, vmem),
        input_output_aliases={1: 0},
        scratch_shapes=buffers + [pltpu.SemaphoreType.DMA],
        compiler_params=compiler_params,
        cost_estimate=cost(slots * plan.stages, 2 * plan.stages),
        name="middle_products",
    )(lists, total, *lefts, *before, first)
    half = jax.ShapeDtypeStruct((share, size, size), jnp.float32)
    _, mine, other = pl.pallas_call(
        functools.partial(last_kernel, plan, bounds),
        out_shape=(running, half, half),
        in_specs=[scalars] + [vmem] * (2 + len(rest)),
        out_specs=(vmem, vmem, vmem),
        input_output_aliases={1: 0},
        compiler_params=compiler_params,
        cost_estimate=cost(slots // 2, 4),
        name="last_products",
    )(lists, total, left_last, *rest)
    received = lax.ppermute(other, "layer", swap)
    return (mine + received).astype(jnp.bfloat16)[None, None]


def solution(mesh):
    plan = Plan(mesh)

    def body(*args):
        return on_device(plan, *args)

    in_specs = (P("col", "row", None, None, None), P(), P())
    out_specs = P("col", "row", "layer", None, None)
    return jax.shard_map(
        body, mesh=mesh, in_specs=in_specs, out_specs=out_specs, check_vma=False
    )
```

```python
import functools

import jax
import jax.numpy as jnp
from jax import lax
from jax.experimental import pallas as pl
from jax.experimental.pallas import tpu as pltpu
from jax.sharding import PartitionSpec as P

TB = 28
GROUP = 8
LANES = 128
GRANT = 8 << 20
CHUNKS = 2


class Plan:
    def __init__(self, mesh):
        self.grid = mesh.shape["row"]
        self.half = min(6, self.grid) // 2
        self.whole = 2 * self.half == self.grid
        self.stages = self.grid - 1 if self.whole else self.half

    def shift(self, a, l):
        if self.whole:
            return l - a
        mid = self.grid // 2
        k = (l - a + mid) % self.grid - mid
        return k if -self.half <= k < self.half else None

    def hop_pairs(self, stage):
        pairs = []
        for source in range(self.grid):
            for layer, step in ((0, 1), (1, -1)):
                target = source + step
                origin = target - step * stage
                if self.whole and not (0 <= target < self.grid and 0 <= origin < self.grid):
                    continue
                target %= self.grid
                if self.shift(target, origin % self.grid) == -step * stage:
                    pairs.append((source * 2 + layer, target * 2 + layer))
        return pairs

    def near_pairs(self, bys):
        pairs = []
        for r in range(self.grid):
            for a in range(self.grid):
                if self.shift(a, r) is not None:
                    for layer, by in enumerate(bys):
                        pairs.append(
                            tuple(
                                (p * self.grid + a) * 2 + layer for p in (r, r ^ by)
                            )
                        )
        return pairs

    def far_pairs(self):
        far = self.grid - 1
        pairs = []
        for r in range(self.grid):
            for a in range(self.grid):
                if self.shift(a, r) is not None:
                    for layer, by in enumerate((1, 2)):
                        pairs.append(
                            tuple(
                                (p * self.grid + a) * 2 + layer
                                for p in (r ^ by, r ^ far)
                            )
                        )
        return pairs

    def taken(self, a, layer, stage):
        l = jnp.where(layer == 0, a - stage, a + stage)
        if self.whole:
            valid = (l >= 0) & (l < self.grid)
        else:
            valid = jnp.where(layer == 0, stage <= self.half, stage < self.half)
        if stage == 0:
            valid = valid & (layer == 0)
        l = jnp.where(l < 0, l + self.grid, l)
        return jnp.where(l >= self.grid, l - self.grid, l), valid


def place():
    return tuple(lax.axis_index(n) for n in ("col", "row", "layer"))


def list_kernel(plan, bounds, slot_keys, pairs, keys, codes):
    slots = slot_keys.shape[2]
    stages = plan.stages + 1
    a, b, layer = place()
    lane = lax.broadcasted_iota(jnp.int32, (1, LANES), 1)
    down = lax.broadcasted_iota(jnp.int32, (LANES, LANES), 0)
    across = lax.broadcasted_iota(jnp.int32, (LANES, LANES), 1)

    keys[...] = jnp.full_like(keys, -1)
    taken = []
    for stage in range(stages):
        l, valid = plan.taken(a, layer, stage)
        taken.append(valid)
        l = jnp.clip(l, 0, plan.grid - 1)
        keys[pl.ds(stage, 1), 0:slots] = slot_keys[a, pl.ds(l, 1), :]
        keys[pl.ds(stages + stage, 1), 0:slots] = slot_keys[l, pl.ds(b, 1), :]
    keys[pl.ds(2 * stages, 1), 0:slots] = slot_keys[a, pl.ds(b, 1), :]
    out = keys[pl.ds(2 * stages, 1), :]
    out = jnp.where(lane < LANES // 2, out, pltpu.roll(out, LANES // 2, 1))
    slot = lane % (LANES // 2)
    r, d = out // 2, out % 2
    after = jnp.where(r + 1 == TB, 0, r + 1)
    second = lane >= LANES // 2
    left_key = jnp.where(second, 2 * r + 1, 2 * r)
    right_key = jnp.where(second, jnp.where(d == 1, 2 * after, -2), out)
    wanted = slot < slots
    left_key = jnp.where(wanted, left_key, -2)
    right_key = jnp.where(wanted, right_key, -2)
    columns = keys[...].T

    def find(column, key):
        hit = columns[:, column : column + 1] == key
        return jnp.sum(jnp.where(hit, down + 1, 0), axis=0, keepdims=True)

    codes[...] = jnp.zeros_like(codes)
    for stage in range(stages):
        left, right = find(stage, left_key), find(stages + stage, right_key)
        good = (left > 0) & (right > 0) & taken[stage]
        code = jnp.where(good, ((left - 1) * 64 + (right - 1)) * 64 + slot + 1, 0)
        if stage < plan.stages:
            codes[pl.ds(stage, 1), :] = code
        else:
            for j, (low, high) in enumerate(zip(bounds[:-1], bounds[1:])):
                here = (right > low) & (right <= high)
                codes[pl.ds(stage + j, 1), :] = jnp.where(here, code, 0)
    found = codes[...] > 0
    ahead = jnp.dot(
        found.astype(jnp.float32),
        (down < across).astype(jnp.float32),
        preferred_element_type=jnp.float32,
    ).astype(jnp.int32)
    order = jnp.where(found, ahead, -1).T
    entries = codes[...].T
    for stage in range(pairs.shape[0]):
        hit = order[:, stage : stage + 1] == across
        entry = jnp.where(hit, entries[:, stage : stage + 1], 0)
        entry = jnp.sum(entry, axis=0, keepdims=True)
        count = jnp.sum(
            found[stage : stage + 1].astype(jnp.int32), axis=1, keepdims=True
        )
        entry = jnp.where(lane < count, entry - 1, slots)
        pairs[pl.ds(stage, 1), :] = jnp.where(lane == LANES - 1, count, entry)


def add_products(count, pairs, row, left, right, acc):
    def step(i, carry):
        codes = [pairs[row, i * GROUP + j] for j in range(GROUP)]
        products = [
            jnp.dot(
                left(code // 4096),
                right((code // 64) % 64),
                preferred_element_type=jnp.float32,
            )
            for code in codes
        ]
        for code, product in zip(codes, products):
            acc[code % 64] += product
        return carry

    lax.fori_loop(0, (count + GROUP - 1) // GROUP, step, 0)


def blocks_of(parts):
    if len(parts) == 1:
        return lambda slot: parts[0][slot]
    first, second = parts
    size = first.shape[0]

    def block(slot):
        return lax.select(
            slot < size,
            first[jnp.minimum(slot, size - 1)],
            second[jnp.maximum(slot - size, 0)],
        )

    return block


class Lefts:
    def __init__(self, plan, refs, late):
        near = plan.grid // 2 - 1
        self.far = plan.grid - 1
        self.own, self.near = refs[0], refs[1 : 1 + near]
        self.swapped = self.halves = ()
        if late:
            self.swapped = refs[1 + near : 1 + 2 * near]
            self.halves = refs[1 + 2 * near : 3 + 2 * near]

    @staticmethod
    def number(plan, late):
        near = plan.grid // 2 - 1
        return 3 + 2 * near if late else 1 + near

    def direct(self, by, layer):
        yield by == 0, blocks_of([self.own])
        for k, tile in enumerate(self.near):
            yield by == 2 * k + 1 + layer, blocks_of([tile])

    def indirect(self, by, layer):
        for k, tile in enumerate(self.swapped):
            yield by == 2 * k + 2 - layer, blocks_of([tile])
        mine, other = self.halves
        share = mine.shape[0]

        def block(slot):
            second = (slot >= share).astype(jnp.int32)
            slot = slot - second * share
            return lax.select(second == layer, mine[slot], other[slot])

        yield by == self.far, block


def run_jobs(cases, count, pairs, row, right, acc):
    for here, left in cases:

        @pl.when(here & (count > 0))
        def _(left=left):
            add_products(count, pairs, row, left, right, acc)


def stages_of(parts, refs):
    rights = []
    for n in parts:
        rights.append(refs[:n])
        refs = refs[n:]
    return rights, refs


def early_kernel(plan, parts, pairs, *refs):
    n = Lefts.number(plan, False)
    lefts = Lefts(plan, refs[:n], False)
    rights, (acc,) = stages_of(parts[:-1], refs[n:])
    a, b, layer = place()
    acc[...] = jnp.zeros_like(acc)
    for stage, right in enumerate(rights):
        by = b ^ plan.taken(a, layer, stage)[0]
        count = pairs[stage, pairs.shape[1] - 1]
        cases = lefts.direct(by, layer)
        run_jobs(cases, count, pairs, stage, blocks_of(right), acc)


def middle_kernel(plan, parts, pairs, total, *refs):
    del total
    n = Lefts.number(plan, True)
    lefts = Lefts(plan, refs[:n], True)
    rights, (first, acc) = stages_of(parts[:-1], refs[n:])
    a, b, layer = place()
    last = pairs.shape[1] - 1
    for stage, right in enumerate([*rights, [first]]):
        by = b ^ plan.taken(a, layer, stage)[0]
        cases = list(lefts.indirect(by, layer))
        if stage == plan.stages:
            cases += lefts.direct(by, layer)
        run_jobs(cases, pairs[stage, last], pairs, stage, blocks_of(right), acc)


def last_kernel(plan, bounds, pairs, total, *refs):
    del total
    n = Lefts.number(plan, True)
    lefts = Lefts(plan, refs[:n], True)
    refs, (acc, mine, other) = refs[n:-3], refs[-3:]
    a, b, layer = place()
    by = b ^ plan.taken(a, layer, plan.stages)[0]
    for j, part in enumerate(refs):
        row, low = plan.stages + 1 + j, bounds[1 + j]
        cases = [*lefts.direct(by, layer), *lefts.indirect(by, layer)]

        def right(slot, part=part, low=low):
            return part[jnp.maximum(slot - low, 0)]

        run_jobs(cases, pairs[row, pairs.shape[1] - 1], pairs, row, right, acc)
    share = mine.shape[0]
    mine[...] = acc[pl.ds(layer * share, share)]
    other[...] = acc[pl.ds((1 - layer) * share, share)]


def on_device(plan, x_blocks, slot_rows, slot_cols):
    own = x_blocks[0, 0]
    slots, size = own.shape[0], own.shape[1]
    share = slots // 2
    bounds = [slots * i // CHUNKS for i in range(CHUNKS + 1)]
    held = [
        (lax.optimization_barrier(own) if i else own)[i:j]
        for i, j in zip(bounds[:-1], bounds[1:])
    ]
    scalars = pl.BlockSpec(memory_space=pltpu.SMEM)
    vmem = pl.BlockSpec(memory_space=pltpu.VMEM)
    compiler_params = pltpu.CompilerParams(vmem_limit_bytes=GRANT)
    tile_bytes = own.size * 2

    def cost(products, tiles):
        return pl.CostEstimate(
            flops=2 * size**3 * products,
            bytes_accessed=tiles * tile_bytes,
            transcendentals=0,
        )

    lists = pl.pallas_call(
        functools.partial(list_kernel, plan, bounds),
        out_shape=jax.ShapeDtypeStruct((plan.stages + CHUNKS, LANES), jnp.int32),
        in_specs=[vmem],
        out_specs=vmem,
        scratch_shapes=[pltpu.VMEM((LANES, LANES), jnp.int32)] * 2,
        compiler_params=compiler_params,
        cost_estimate=cost(0, 2),
        name="list_products",
    )(2 * slot_rows + (slot_cols != slot_rows))
    rights = [[own]]
    for stage in range(1, plan.stages + 1):
        pairs = plan.hop_pairs(stage)
        arrived = []
        for part in held:
            arrived.append(lax.ppermute(part, ("col", "layer"), pairs))
        rights.append(arrived)
        held = list(arrived)
    everywhere = ("row", "col", "layer")
    swap = [(0, 1), (1, 0)]
    near, swapped = [], []
    for k in range(plan.grid // 2 - 1):
        bys = (2 * k + 1, 2 * k + 2)
        near.append(lax.ppermute(own, everywhere, plan.near_pairs(bys)))
        swapped.append(lax.ppermute(near[-1], "layer", swap))
    sent = jnp.where(
        lax.axis_index("layer") == 0, near[0][:share], near[0][share:]
    )
    far = lax.ppermute(sent, everywhere, plan.far_pairs())
    far_swapped = lax.ppermute(far, "layer", swap)
    direct = [own, *near]
    lefts = [*direct, *swapped, far, far_swapped]
    parts = [len(r) for r in rights]
    running = jax.ShapeDtypeStruct((slots + 1, size, size), jnp.float32)
    before = [part for stage in rights[:-1] for part in stage]
    total = pl.pallas_call(
        functools.partial(early_kernel, plan, parts),
        out_shape=running,
        in_specs=[scalars] + [vmem] * (len(direct) + len(before)),
        out_specs=vmem,
        compiler_params=compiler_params,
        cost_estimate=cost(slots * plan.stages, 2 * plan.stages),
        name="early_products",
    )(lists, *direct, *before)
    first, *rest = rights[-1]
    total = pl.pallas_call(
        functools.partial(middle_kernel, plan, parts),
        out_shape=running,
        in_specs=[scalars] + [vmem] * (2 + len(lefts) + len(before)),
        out_specs=vmem,
        input_output_aliases={1: 0},
        compiler_params=compiler_params,
        cost_estimate=cost(slots * plan.stages, 2 * plan.stages),
        name="middle_products",
    )(lists, total, *lefts, *before, first)
    half = jax.ShapeDtypeStruct((share, size, size), jnp.float32)
    _, mine, other = pl.pallas_call(
        functools.partial(last_kernel, plan, bounds),
        out_shape=(running, half, half),
        in_specs=[scalars] + [vmem] * (1 + len(lefts) + len(rest)),
        out_specs=(vmem, vmem, vmem),
        input_output_aliases={1: 0},
        compiler_params=compiler_params,
        cost_estimate=cost(slots // 2, 4),
        name="last_products",
    )(lists, total, *lefts, *rest)
    received = lax.ppermute(other, "layer", swap)
    return (mine + received).astype(jnp.bfloat16)[None, None]


def solution(mesh):
    plan = Plan(mesh)

    def body(*args):
        return on_device(plan, *args)

    in_specs = (P("col", "row", None, None, None), P(), P())
    out_specs = P("col", "row", "layer", None, None)
    return jax.shard_map(
        body, mesh=mesh, in_specs=in_specs, out_specs=out_specs, check_vma=False
    )
```

```python
import functools

import jax
import jax.numpy as jnp
from jax import lax
from jax.experimental import pallas as pl
from jax.experimental.pallas import tpu as pltpu
from jax.sharding import PartitionSpec as P

TB = 28
GROUP = 8
LANES = 128
GRANT = 8 << 20
CHUNKS = 2


class Plan:
    def __init__(self, mesh):
        self.grid = mesh.shape["row"]
        self.half = min(6, self.grid) // 2
        self.whole = 2 * self.half == self.grid
        self.stages = self.grid - 1 if self.whole else self.half

    def shift(self, a, l):
        if self.whole:
            return l - a
        mid = self.grid // 2
        k = (l - a + mid) % self.grid - mid
        return k if -self.half <= k < self.half else None

    def hop_pairs(self, stage):
        pairs = []
        for source in range(self.grid):
            for layer, step in ((0, 1), (1, -1)):
                target = source + step
                origin = target - step * stage
                if self.whole and not (0 <= target < self.grid and 0 <= origin < self.grid):
                    continue
                target %= self.grid
                if self.shift(target, origin % self.grid) == -step * stage:
                    pairs.append((source * 2 + layer, target * 2 + layer))
        return pairs

    def near_pairs(self, bys):
        pairs = []
        for r in range(self.grid):
            for a in range(self.grid):
                if self.shift(a, r) is not None:
                    for layer, by in enumerate(bys):
                        pairs.append(
                            tuple(
                                (p * self.grid + a) * 2 + layer for p in (r, r ^ by)
                            )
                        )
        return pairs

    def far_pairs(self):
        far = self.grid - 1
        pairs = []
        for r in range(self.grid):
            for a in range(self.grid):
                if self.shift(a, r) is not None:
                    for layer, by in enumerate((1, 2)):
                        pairs.append(
                            tuple(
                                (p * self.grid + a) * 2 + layer
                                for p in (r ^ by, r ^ far)
                            )
                        )
        return pairs

    def taken(self, a, layer, stage):
        l = jnp.where(layer == 0, a - stage, a + stage)
        if self.whole:
            valid = (l >= 0) & (l < self.grid)
        else:
            valid = jnp.where(layer == 0, stage <= self.half, stage < self.half)
        if stage == 0:
            valid = valid & (layer == 0)
        l = jnp.where(l < 0, l + self.grid, l)
        return jnp.where(l >= self.grid, l - self.grid, l), valid


def late_core(plan, a):
    l, valid = plan.taken(a, jnp.int32(0), plan.stages)
    other_l, other_valid = plan.taken(a, jnp.int32(1), plan.stages)
    late = jnp.where(valid, 0, 1)
    return late, jnp.where(valid, l, other_l), valid | other_valid


def place():
    return tuple(lax.axis_index(n) for n in ("col", "row", "layer"))


def list_kernel(plan, bounds, slot_keys, pairs, keys, codes):
    slots = slot_keys.shape[2]
    stages = plan.stages + 2
    a, b, layer = place()
    lane = lax.broadcasted_iota(jnp.int32, (1, LANES), 1)
    down = lax.broadcasted_iota(jnp.int32, (LANES, LANES), 0)
    across = lax.broadcasted_iota(jnp.int32, (LANES, LANES), 1)

    keys[...] = jnp.full_like(keys, -1)
    jobs = [plan.taken(a, layer, stage) for stage in range(stages - 1)]
    jobs.append(late_core(plan, a)[1:])
    for stage, (l, valid) in enumerate(jobs):
        l = jnp.clip(l, 0, plan.grid - 1)
        keys[pl.ds(stage, 1), 0:slots] = slot_keys[a, pl.ds(l, 1), :]
        keys[pl.ds(stages + stage, 1), 0:slots] = slot_keys[l, pl.ds(b, 1), :]
    keys[pl.ds(2 * stages, 1), 0:slots] = slot_keys[a, pl.ds(b, 1), :]
    out = keys[pl.ds(2 * stages, 1), :]
    out = jnp.where(lane < LANES // 2, out, pltpu.roll(out, LANES // 2, 1))
    slot = lane % (LANES // 2)
    r, d = out // 2, out % 2
    after = jnp.where(r + 1 == TB, 0, r + 1)
    second = lane >= LANES // 2
    left_key = jnp.where(second, 2 * r + 1, 2 * r)
    right_key = jnp.where(second, jnp.where(d == 1, 2 * after, -2), out)
    wanted = slot < slots
    left_key = jnp.where(wanted, left_key, -2)
    right_key = jnp.where(wanted, right_key, -2)
    columns = keys[...].T

    def find(column, key):
        hit = columns[:, column : column + 1] == key
        return jnp.sum(jnp.where(hit, down + 1, 0), axis=0, keepdims=True)

    codes[...] = jnp.zeros_like(codes)
    share = slots // 2
    for stage, (_, valid) in enumerate(jobs):
        left, right = find(stage, left_key), find(stages + stage, right_key)
        good = (left > 0) & (right > 0) & valid
        if stage == plan.stages:
            good = good & (right <= bounds[1])
        if stage > plan.stages:
            low = layer * share
            good = good & (right > bounds[1]) & (slot >= low) & (slot < low + share)
        code = ((left - 1) * 64 + (right - 1)) * 64 + slot + 1
        codes[pl.ds(stage, 1), :] = jnp.where(good, code, 0)
    found = codes[...] > 0
    ahead = jnp.dot(
        found.astype(jnp.float32),
        (down < across).astype(jnp.float32),
        preferred_element_type=jnp.float32,
    ).astype(jnp.int32)
    order = jnp.where(found, ahead, -1).T
    entries = codes[...].T
    for stage in range(pairs.shape[0]):
        hit = order[:, stage : stage + 1] == across
        entry = jnp.where(hit, entries[:, stage : stage + 1], 0)
        entry = jnp.sum(entry, axis=0, keepdims=True)
        count = jnp.sum(
            found[stage : stage + 1].astype(jnp.int32), axis=1, keepdims=True
        )
        entry = jnp.where(lane < count, entry - 1, slots)
        pairs[pl.ds(stage, 1), :] = jnp.where(lane == LANES - 1, count, entry)


def add_products(count, pairs, row, left, right, acc, at):
    def step(i, carry):
        codes = [pairs[row, i * GROUP + j] for j in range(GROUP)]
        products = [
            jnp.dot(
                left(code // 4096),
                right((code // 64) % 64),
                preferred_element_type=jnp.float32,
            )
            for code in codes
        ]
        for code, product in zip(codes, products):
            acc[at(code % 64)] += product
        return carry

    lax.fori_loop(0, (count + GROUP - 1) // GROUP, step, 0)


def blocks_of(parts):
    if len(parts) == 1:
        return lambda slot: parts[0][slot]
    first, second = parts
    size = first.shape[0]

    def block(slot):
        return lax.select(
            slot < size,
            first[jnp.minimum(slot, size - 1)],
            second[jnp.maximum(slot - size, 0)],
        )

    return block


class Lefts:
    def __init__(self, plan, refs, late):
        near = plan.grid // 2 - 1
        self.far = plan.grid - 1
        self.own, self.near = refs[0], refs[1 : 1 + near]
        self.swapped = self.halves = ()
        if late:
            self.swapped = refs[1 + near : 1 + 2 * near]
            self.halves = refs[1 + 2 * near : 3 + 2 * near]

    @staticmethod
    def number(plan, late):
        near = plan.grid // 2 - 1
        return 3 + 2 * near if late else 1 + near

    def direct(self, by, layer):
        yield by == 0, blocks_of([self.own])
        for k, tile in enumerate(self.near):
            yield by == 2 * k + 1 + layer, blocks_of([tile])

    def indirect(self, by, layer):
        for k, tile in enumerate(self.swapped):
            yield by == 2 * k + 2 - layer, blocks_of([tile])
        mine, other = self.halves
        share = mine.shape[0]

        def block(slot):
            second = (slot >= share).astype(jnp.int32)
            slot = slot - second * share
            return lax.select(second == layer, mine[slot], other[slot])

        yield by == self.far, block


def run_jobs(cases, count, pairs, row, right, acc, at=lambda slot: slot):
    for here, left in cases:

        @pl.when(here & (count > 0))
        def _(left=left):
            add_products(count, pairs, row, left, right, acc, at)


def stages_of(parts, refs):
    rights = []
    for n in parts:
        rights.append(refs[:n])
        refs = refs[n:]
    return rights, refs


def early_kernel(plan, parts, pairs, *refs):
    n = Lefts.number(plan, False)
    lefts = Lefts(plan, refs[:n], False)
    rights, (acc,) = stages_of(parts[:-1], refs[n:])
    a, b, layer = place()
    acc[...] = jnp.zeros_like(acc)
    for stage, right in enumerate(rights):
        by = b ^ plan.taken(a, layer, stage)[0]
        count = pairs[stage, pairs.shape[1] - 1]
        cases = lefts.direct(by, layer)
        run_jobs(cases, count, pairs, stage, blocks_of(right), acc)


def middle_kernel(plan, parts, pairs, total, *refs):
    del total
    n = Lefts.number(plan, True)
    lefts = Lefts(plan, refs[:n], True)
    rights, (first, acc, mine, other) = stages_of(parts[:-1], refs[n:])
    a, b, layer = place()
    last = pairs.shape[1] - 1
    for stage, right in enumerate([*rights, [first]]):
        by = b ^ plan.taken(a, layer, stage)[0]
        cases = list(lefts.indirect(by, layer))
        if stage == plan.stages:
            cases += lefts.direct(by, layer)
        run_jobs(cases, pairs[stage, last], pairs, stage, blocks_of(right), acc)
    share = other.shape[0]
    mine[...] = acc[pl.ds(layer * share, share)]
    other[...] = acc[pl.ds((1 - layer) * share, share)]


def last_kernel(plan, low, pairs, mine, received, *refs):
    n = Lefts.number(plan, True)
    lefts = Lefts(plan, refs[:n], True)
    part, part_swapped, out, acc, rounded, sem = refs[n:]
    a, b, layer = place()
    share = out.shape[0]
    acc[pl.ds(0, share)] = mine[...] + received[...]
    late, l, _ = late_core(plan, a)
    by = b ^ l
    row = plan.stages + 1
    cases = [*lefts.direct(by, layer), *lefts.indirect(by, layer)]

    def right(slot):
        slot = jnp.maximum(slot - low, 0)
        return lax.select(late == layer, part[slot], part_swapped[slot])

    count = pairs[row, pairs.shape[1] - 1]
    run_jobs(
        cases,
        count,
        pairs,
        row,
        right,
        acc,
        lambda slot: jnp.minimum(slot - layer * share, share),
    )
    copies = []
    for j, (start, end) in enumerate(((0, share // 2), (share // 2, share))):
        here = pl.ds(start, end - start)
        rounded[here] = acc[here].astype(rounded.dtype)
        copies.append(pltpu.make_async_copy(rounded.at[here], out.at[here], sem.at[j]))
        copies[-1].start()
    for copy in copies:
        copy.wait()


def on_device(plan, x_blocks, slot_rows, slot_cols):
    own = x_blocks[0, 0]
    slots, size = own.shape[0], own.shape[1]
    share = slots // 2
    bounds = [slots * i // CHUNKS for i in range(CHUNKS + 1)]
    held = [
        (lax.optimization_barrier(own) if i else own)[i:j]
        for i, j in zip(bounds[:-1], bounds[1:])
    ]
    scalars = pl.BlockSpec(memory_space=pltpu.SMEM)
    vmem = pl.BlockSpec(memory_space=pltpu.VMEM)
    compiler_params = pltpu.CompilerParams(vmem_limit_bytes=GRANT)
    tile_bytes = own.size * 2

    def cost(products, tiles):
        return pl.CostEstimate(
            flops=2 * size**3 * products,
            bytes_accessed=tiles * tile_bytes,
            transcendentals=0,
        )

    lists = pl.pallas_call(
        functools.partial(list_kernel, plan, bounds),
        out_shape=jax.ShapeDtypeStruct((plan.stages + CHUNKS, LANES), jnp.int32),
        in_specs=[vmem],
        out_specs=vmem,
        scratch_shapes=[pltpu.VMEM((LANES, LANES), jnp.int32)] * 2,
        compiler_params=compiler_params,
        cost_estimate=cost(0, 2),
        name="list_products",
    )(2 * slot_rows + (slot_cols != slot_rows))
    rights = [[own]]
    for stage in range(1, plan.stages + 1):
        pairs = plan.hop_pairs(stage)
        arrived = []
        for part in held:
            arrived.append(lax.ppermute(part, ("col", "layer"), pairs))
        rights.append(arrived)
        held = list(arrived)
    everywhere = ("row", "col", "layer")
    swap = [(0, 1), (1, 0)]
    near, swapped = [], []
    for k in range(plan.grid // 2 - 1):
        bys = (2 * k + 1, 2 * k + 2)
        near.append(lax.ppermute(own, everywhere, plan.near_pairs(bys)))
        swapped.append(lax.ppermute(near[-1], "layer", swap))
    sent = jnp.where(
        lax.axis_index("layer") == 0, near[0][:share], near[0][share:]
    )
    far = lax.ppermute(sent, everywhere, plan.far_pairs())
    far_swapped = lax.ppermute(far, "layer", swap)
    direct = [own, *near]
    lefts = [*direct, *swapped, far, far_swapped]
    parts = [len(r) for r in rights]
    running = jax.ShapeDtypeStruct((slots + 1, size, size), jnp.float32)
    before = [part for stage in rights[:-1] for part in stage]
    total = pl.pallas_call(
        functools.partial(early_kernel, plan, parts),
        out_shape=running,
        in_specs=[scalars] + [vmem] * (len(direct) + len(before)),
        out_specs=vmem,
        compiler_params=compiler_params,
        cost_estimate=cost(slots * plan.stages, 2 * plan.stages),
        name="early_products",
    )(lists, *direct, *before)
    first, second = rights[-1]
    half = jax.ShapeDtypeStruct((share, size, size), jnp.float32)
    _, mine, other = pl.pallas_call(
        functools.partial(middle_kernel, plan, parts),
        out_shape=(running, half, half),
        in_specs=[scalars] + [vmem] * (2 + len(lefts) + len(before)),
        out_specs=(vmem, vmem, vmem),
        input_output_aliases={1: 0},
        compiler_params=compiler_params,
        cost_estimate=cost(slots * plan.stages, 2 * plan.stages),
        name="middle_products",
    )(lists, total, *lefts, *before, first)
    received = lax.ppermute(other, "layer", swap)
    second_swapped = lax.ppermute(second, "layer", swap)
    square = pl.pallas_call(
        functools.partial(last_kernel, plan, bounds[1]),
        out_shape=jax.ShapeDtypeStruct((share, size, size), jnp.bfloat16),
        in_specs=[scalars] + [vmem] * (4 + len(lefts)),
        out_specs=pl.BlockSpec(memory_space=pl.ANY),
        scratch_shapes=[
            pltpu.VMEM((share + 1, size, size), jnp.float32),
            pltpu.VMEM((share, size, size), jnp.bfloat16),
            pltpu.SemaphoreType.DMA((2,)),
        ],
        compiler_params=compiler_params,
        cost_estimate=cost(slots // 2, 4),
        name="last_products",
    )(lists, mine, received, *lefts, second, second_swapped)
    return square[None, None]


def solution(mesh):
    plan = Plan(mesh)

    def body(*args):
        return on_device(plan, *args)

    in_specs = (P("col", "row", None, None, None), P(), P())
    out_specs = P("col", "row", "layer", None, None)
    return jax.shard_map(
        body, mesh=mesh, in_specs=in_specs, out_specs=out_specs, check_vma=False
    )
```

```python
import functools

import jax
import jax.numpy as jnp
from jax import lax
from jax.experimental import pallas as pl
from jax.experimental.pallas import tpu as pltpu
from jax.sharding import PartitionSpec as P

TB = 28
GROUP = 8
LANES = 128
GRANT = 8 << 20
CHUNKS = 2


class Plan:
    def __init__(self, mesh):
        self.grid = mesh.shape["row"]
        self.half = min(6, self.grid) // 2
        self.whole = 2 * self.half == self.grid
        self.stages = self.grid - 1 if self.whole else self.half

    def shift(self, a, l):
        if self.whole:
            return l - a
        mid = self.grid // 2
        k = (l - a + mid) % self.grid - mid
        return k if -self.half <= k < self.half else None

    def hop_pairs(self, stage):
        pairs = []
        for source in range(self.grid):
            for layer, step in ((0, 1), (1, -1)):
                target = source + step
                origin = target - step * stage
                if self.whole and not (0 <= target < self.grid and 0 <= origin < self.grid):
                    continue
                target %= self.grid
                if self.shift(target, origin % self.grid) == -step * stage:
                    pairs.append((source * 2 + layer, target * 2 + layer))
        return pairs

    def near_pairs(self, bys):
        pairs = []
        for r in range(self.grid):
            for a in range(self.grid):
                if self.shift(a, r) is not None:
                    for layer, by in enumerate(bys):
                        pairs.append(
                            tuple(
                                (p * self.grid + a) * 2 + layer for p in (r, r ^ by)
                            )
                        )
        return pairs

    def far_pairs(self):
        far = self.grid - 1
        pairs = []
        for r in range(self.grid):
            for a in range(self.grid):
                if self.shift(a, r) is not None:
                    for layer, by in enumerate((1, 2)):
                        pairs.append(
                            tuple(
                                (p * self.grid + a) * 2 + layer
                                for p in (r ^ by, r ^ far)
                            )
                        )
        return pairs

    def taken(self, a, layer, stage):
        l = jnp.where(layer == 0, a - stage, a + stage)
        if self.whole:
            valid = (l >= 0) & (l < self.grid)
        else:
            valid = jnp.where(layer == 0, stage <= self.half, stage < self.half)
        if stage == 0:
            valid = valid & (layer == 0)
        l = jnp.where(l < 0, l + self.grid, l)
        return jnp.where(l >= self.grid, l - self.grid, l), valid


def late_core(plan, a):
    l, valid = plan.taken(a, jnp.int32(0), plan.stages)
    other_l, other_valid = plan.taken(a, jnp.int32(1), plan.stages)
    late = jnp.where(valid, 0, 1)
    return late, jnp.where(valid, l, other_l), valid | other_valid


def place():
    return tuple(lax.axis_index(n) for n in ("col", "row", "layer"))


def list_kernel(plan, bounds, slot_keys, pairs, keys, codes):
    slots = slot_keys.shape[2]
    stages = plan.stages + 2
    a, b, layer = place()
    lane = lax.broadcasted_iota(jnp.int32, (1, LANES), 1)
    down = lax.broadcasted_iota(jnp.int32, (LANES, LANES), 0)
    across = lax.broadcasted_iota(jnp.int32, (LANES, LANES), 1)

    keys[...] = jnp.full_like(keys, -1)
    jobs = [plan.taken(a, layer, stage) for stage in range(stages - 1)]
    jobs.append(late_core(plan, a)[1:])
    for stage, (l, valid) in enumerate(jobs):
        l = jnp.clip(l, 0, plan.grid - 1)
        keys[pl.ds(stage, 1), 0:slots] = slot_keys[a, pl.ds(l, 1), :]
        keys[pl.ds(stages + stage, 1), 0:slots] = slot_keys[l, pl.ds(b, 1), :]
    keys[pl.ds(2 * stages, 1), 0:slots] = slot_keys[a, pl.ds(b, 1), :]
    out = keys[pl.ds(2 * stages, 1), :]
    out = jnp.where(lane < LANES // 2, out, pltpu.roll(out, LANES // 2, 1))
    slot = lane % (LANES // 2)
    r, d = out // 2, out % 2
    after = jnp.where(r + 1 == TB, 0, r + 1)
    second = lane >= LANES // 2
    left_key = jnp.where(second, 2 * r + 1, 2 * r)
    right_key = jnp.where(second, jnp.where(d == 1, 2 * after, -2), out)
    wanted = slot < slots
    left_key = jnp.where(wanted, left_key, -2)
    right_key = jnp.where(wanted, right_key, -2)
    columns = keys[...].T

    def find(column, key):
        hit = columns[:, column : column + 1] == key
        return jnp.sum(jnp.where(hit, down + 1, 0), axis=0, keepdims=True)

    codes[...] = jnp.zeros_like(codes)
    share = slots // 2
    for stage, (_, valid) in enumerate(jobs):
        left, right = find(stage, left_key), find(stages + stage, right_key)
        good = (left > 0) & (right > 0) & valid
        if stage == plan.stages:
            good = good & (right <= bounds[1])
        if stage > plan.stages:
            low = layer * share
            good = good & (right > bounds[1]) & (slot >= low) & (slot < low + share)
        code = ((left - 1) * 64 + (right - 1)) * 64 + slot + 1
        codes[pl.ds(stage, 1), :] = jnp.where(good, code, 0)
    found = codes[...] > 0
    ahead = jnp.dot(
        found.astype(jnp.float32),
        (down < across).astype(jnp.float32),
        preferred_element_type=jnp.float32,
    ).astype(jnp.int32)
    order = jnp.where(found, ahead, -1).T
    entries = codes[...].T
    for stage in range(pairs.shape[0]):
        hit = order[:, stage : stage + 1] == across
        entry = jnp.where(hit, entries[:, stage : stage + 1], 0)
        entry = jnp.sum(entry, axis=0, keepdims=True)
        count = jnp.sum(
            found[stage : stage + 1].astype(jnp.int32), axis=1, keepdims=True
        )
        entry = jnp.where(lane < count, entry - 1, slots)
        pairs[pl.ds(stage, 1), :] = jnp.where(lane == LANES - 1, count, entry)


def add_products(count, pairs, row, left, right, acc, at):
    def step(i, carry):
        codes = [pairs[row, i * GROUP + j] for j in range(GROUP)]
        products = [
            jnp.dot(
                left(code // 4096),
                right((code // 64) % 64),
                preferred_element_type=jnp.float32,
            )
            for code in codes
        ]
        for code, product in zip(codes, products):
            acc[at(code % 64)] += product
        return carry

    lax.fori_loop(0, (count + GROUP - 1) // GROUP, step, 0)


def blocks_of(parts):
    if len(parts) == 1:
        return lambda slot: parts[0][slot]
    first, second = parts
    size = first.shape[0]

    def block(slot):
        return lax.select(
            slot < size,
            first[jnp.minimum(slot, size - 1)],
            second[jnp.maximum(slot - size, 0)],
        )

    return block


class Lefts:
    def __init__(self, plan, refs):
        near = plan.grid // 2 - 1
        self.far = plan.grid - 1
        self.own, self.near = refs[0], refs[1 : 1 + near]
        self.swapped = refs[1 + near : 1 + 2 * near]
        self.halves = refs[1 + 2 * near :]

    def all(self, by, layer):
        yield from self.direct(by, layer)
        yield from self.indirect(by, layer)
        yield from self.opposite(by, layer)

    def direct(self, by, layer):
        yield by == 0, blocks_of([self.own])
        for k, tile in enumerate(self.near):
            yield by == 2 * k + 1 + layer, blocks_of([tile])

    def indirect(self, by, layer):
        for k, tile in enumerate(self.swapped):
            yield by == 2 * k + 2 - layer, blocks_of([tile])

    def opposite(self, by, layer):
        mine, other = self.halves
        share = mine.shape[0]

        def block(slot):
            second = (slot >= share).astype(jnp.int32)
            slot = slot - second * share
            return lax.select(second == layer, mine[slot], other[slot])

        yield by == self.far, block


def run_jobs(cases, count, pairs, row, right, acc, at=lambda slot: slot):
    for here, left in cases:

        @pl.when(here & (count > 0))
        def _(left=left):
            add_products(count, pairs, row, left, right, acc, at)


def stages_of(parts, refs):
    rights = []
    for n in parts:
        rights.append(refs[:n])
        refs = refs[n:]
    return rights, refs


def early_kernel(plan, n, parts, pairs, *refs):
    lefts = Lefts(plan, refs[:n])
    rights, (acc,) = stages_of(parts[:-1], refs[n:])
    a, b, layer = place()
    acc[...] = jnp.zeros_like(acc)
    for stage, right in enumerate(rights):
        by = b ^ plan.taken(a, layer, stage)[0]
        count = pairs[stage, pairs.shape[1] - 1]
        cases = lefts.direct(by, layer)
        run_jobs(cases, count, pairs, stage, blocks_of(right), acc)


def second_kernel(plan, n, parts, pairs, total, *refs):
    del total
    lefts = Lefts(plan, refs[:n])
    rights, (acc,) = stages_of(parts[:-1], refs[n:])
    a, b, layer = place()
    for stage, right in enumerate(rights):
        by = b ^ plan.taken(a, layer, stage)[0]
        count = pairs[stage, pairs.shape[1] - 1]
        cases = lefts.indirect(by, layer)
        run_jobs(cases, count, pairs, stage, blocks_of(right), acc)


def pick_kernel(tile, half):
    share = half.shape[0]
    half[...] = tile[pl.ds(lax.axis_index("layer") * share, share)]


def middle_kernel(plan, n, parts, pairs, total, *refs):
    del total
    lefts = Lefts(plan, refs[:n])
    rights, (first, acc, mine, other) = stages_of(parts[:-1], refs[n:])
    a, b, layer = place()
    last = pairs.shape[1] - 1
    for stage, right in enumerate([*rights, [first]]):
        by = b ^ plan.taken(a, layer, stage)[0]
        cases = (lefts.all if stage == plan.stages else lefts.opposite)(by, layer)
        run_jobs(cases, pairs[stage, last], pairs, stage, blocks_of(right), acc)
    share = other.shape[0]
    mine[...] = acc[pl.ds(layer * share, share)]
    other[...] = acc[pl.ds((1 - layer) * share, share)]


def last_kernel(plan, n, low, pairs, mine, received, *refs):
    lefts = Lefts(plan, refs[:n])
    part, part_swapped, out, acc, rounded, sem = refs[n:]
    a, b, layer = place()
    share = out.shape[0]
    acc[pl.ds(0, share)] = mine[...] + received[...]
    late, l, _ = late_core(plan, a)
    by = b ^ l
    row = plan.stages + 1
    cases = lefts.all(by, layer)

    def right(slot):
        slot = jnp.maximum(slot - low, 0)
        return lax.select(late == layer, part[slot], part_swapped[slot])

    count = pairs[row, pairs.shape[1] - 1]
    run_jobs(
        cases,
        count,
        pairs,
        row,
        right,
        acc,
        lambda slot: jnp.minimum(slot - layer * share, share),
    )
    copies = []
    for j, (start, end) in enumerate(((0, share // 2), (share // 2, share))):
        here = pl.ds(start, end - start)
        rounded[here] = acc[here].astype(rounded.dtype)
        copies.append(pltpu.make_async_copy(rounded.at[here], out.at[here], sem.at[j]))
        copies[-1].start()
    for copy in copies:
        copy.wait()


def on_device(plan, x_blocks, slot_rows, slot_cols):
    own = x_blocks[0, 0]
    slots, size = own.shape[0], own.shape[1]
    share = slots // 2
    bounds = [slots * i // CHUNKS for i in range(CHUNKS + 1)]
    held = [
        (lax.optimization_barrier(own) if i else own)[i:j]
        for i, j in zip(bounds[:-1], bounds[1:])
    ]
    scalars = pl.BlockSpec(memory_space=pltpu.SMEM)
    vmem = pl.BlockSpec(memory_space=pltpu.VMEM)
    compiler_params = pltpu.CompilerParams(vmem_limit_bytes=GRANT)
    tile_bytes = own.size * 2

    def cost(products, tiles):
        return pl.CostEstimate(
            flops=2 * size**3 * products,
            bytes_accessed=tiles * tile_bytes,
            transcendentals=0,
        )

    lists = pl.pallas_call(
        functools.partial(list_kernel, plan, bounds),
        out_shape=jax.ShapeDtypeStruct((plan.stages + CHUNKS, LANES), jnp.int32),
        in_specs=[vmem],
        out_specs=vmem,
        scratch_shapes=[pltpu.VMEM((LANES, LANES), jnp.int32)] * 2,
        compiler_params=compiler_params,
        cost_estimate=cost(0, 2),
        name="list_products",
    )(2 * slot_rows + (slot_cols != slot_rows))
    rights = [[own]]
    for stage in range(1, plan.stages + 1):
        pairs = plan.hop_pairs(stage)
        arrived = []
        for part in held:
            arrived.append(lax.ppermute(part, ("col", "layer"), pairs))
        rights.append(arrived)
        held = list(arrived)
    everywhere = ("row", "col", "layer")
    swap = [(0, 1), (1, 0)]
    near, swapped = [], []
    for k in range(plan.grid // 2 - 1):
        bys = (2 * k + 1, 2 * k + 2)
        near.append(lax.ppermute(own, everywhere, plan.near_pairs(bys)))
        swapped.append(lax.ppermute(near[-1], "layer", swap))
    sent = pl.pallas_call(
        pick_kernel,
        out_shape=jax.ShapeDtypeStruct((share, size, size), own.dtype),
        in_specs=[vmem],
        out_specs=vmem,
        compiler_params=compiler_params,
        cost_estimate=cost(0, 1),
        name="pick_half",
    )(near[0])
    far = lax.ppermute(sent, everywhere, plan.far_pairs())
    far_swapped = lax.ppermute(far, "layer", swap)
    direct = [own, *near]
    lefts = [*direct, *swapped, far, far_swapped]
    parts = [len(r) for r in rights]
    running = jax.ShapeDtypeStruct((slots + 1, size, size), jnp.float32)
    before = [part for stage in rights[:-1] for part in stage]
    total = pl.pallas_call(
        functools.partial(early_kernel, plan, len(direct), parts),
        out_shape=running,
        in_specs=[scalars] + [vmem] * (len(direct) + len(before)),
        out_specs=vmem,
        compiler_params=compiler_params,
        cost_estimate=cost(slots * plan.stages, 2 * plan.stages),
        name="early_products",
    )(lists, *direct, *before)
    total = pl.pallas_call(
        functools.partial(second_kernel, plan, len(direct) + len(swapped), parts),
        out_shape=running,
        in_specs=[scalars]
        + [vmem] * (1 + len(direct) + len(swapped) + len(before)),
        out_specs=vmem,
        input_output_aliases={1: 0},
        compiler_params=compiler_params,
        cost_estimate=cost(slots, 2),
        name="second_products",
    )(lists, total, *direct, *swapped, *before)
    first, second = rights[-1]
    half = jax.ShapeDtypeStruct((share, size, size), jnp.float32)
    _, mine, other = pl.pallas_call(
        functools.partial(middle_kernel, plan, len(lefts), parts),
        out_shape=(running, half, half),
        in_specs=[scalars] + [vmem] * (2 + len(lefts) + len(before)),
        out_specs=(vmem, vmem, vmem),
        input_output_aliases={1: 0},
        compiler_params=compiler_params,
        cost_estimate=cost(slots * plan.stages, 2 * plan.stages),
        name="middle_products",
    )(lists, total, *lefts, *before, first)
    received = lax.ppermute(other, "layer", swap)
    second_swapped = lax.ppermute(second, "layer", swap)
    square = pl.pallas_call(
        functools.partial(last_kernel, plan, len(lefts), bounds[1]),
        out_shape=jax.ShapeDtypeStruct((share, size, size), jnp.bfloat16),
        in_specs=[scalars] + [vmem] * (4 + len(lefts)),
        out_specs=pl.BlockSpec(memory_space=pl.ANY),
        scratch_shapes=[
            pltpu.VMEM((share + 1, size, size), jnp.float32),
            pltpu.VMEM((share, size, size), jnp.bfloat16),
            pltpu.SemaphoreType.DMA((2,)),
        ],
        compiler_params=compiler_params,
        cost_estimate=cost(slots // 2, 4),
        name="last_products",
    )(lists, mine, received, *lefts, second, second_swapped)
    return square[None, None]


def solution(mesh):
    plan = Plan(mesh)

    def body(*args):
        return on_device(plan, *args)

    in_specs = (P("col", "row", None, None, None), P(), P())
    out_specs = P("col", "row", "layer", None, None)
    return jax.shard_map(
        body, mesh=mesh, in_specs=in_specs, out_specs=out_specs, check_vma=False
    )
```

```python
import functools

import jax
import jax.numpy as jnp
from jax import lax
from jax.experimental import pallas as pl
from jax.experimental.pallas import tpu as pltpu
from jax.sharding import PartitionSpec as P

TB = 28
GROUP = 8
LANES = 128
GRANT = 8 << 20
CHUNKS = 2


class Plan:
    def __init__(self, mesh):
        self.grid = mesh.shape["row"]
        self.half = min(6, self.grid) // 2
        self.whole = 2 * self.half == self.grid
        self.stages = self.grid - 1 if self.whole else self.half

    def shift(self, a, l):
        if self.whole:
            return l - a
        mid = self.grid // 2
        k = (l - a + mid) % self.grid - mid
        return k if -self.half <= k < self.half else None

    def hop_pairs(self, stage):
        pairs = []
        for source in range(self.grid):
            for layer, step in ((0, 1), (1, -1)):
                target = source + step
                origin = target - step * stage
                if self.whole and not (0 <= target < self.grid and 0 <= origin < self.grid):
                    continue
                target %= self.grid
                if self.shift(target, origin % self.grid) == -step * stage:
                    pairs.append((source * 2 + layer, target * 2 + layer))
        return pairs

    def near_pairs(self, bys):
        pairs = []
        for r in range(self.grid):
            for a in range(self.grid):
                if self.shift(a, r) is not None:
                    for layer, by in enumerate(bys):
                        pairs.append(
                            tuple(
                                (p * self.grid + a) * 2 + layer for p in (r, r ^ by)
                            )
                        )
        return pairs

    def far_pairs(self):
        far = self.grid - 1
        pairs = []
        for r in range(self.grid):
            for a in range(self.grid):
                if self.shift(a, r) is not None:
                    for layer, by in enumerate((1, 2)):
                        pairs.append(
                            tuple(
                                (p * self.grid + a) * 2 + layer
                                for p in (r ^ by, r ^ far)
                            )
                        )
        return pairs

    def last_pairs(self):
        pairs = []
        for a in range(self.grid):
            for l in (a - self.stages, a + self.stages):
                if self.whole and not 0 <= l < self.grid:
                    continue
                if self.shift(a, l % self.grid) == l - a:
                    pairs += [(a * 2, a * 2 + 1), (a * 2 + 1, a * 2)]
        return pairs

    def taken(self, a, layer, stage):
        l = jnp.where(layer == 0, a - stage, a + stage)
        if self.whole:
            valid = (l >= 0) & (l < self.grid)
        else:
            valid = jnp.where(layer == 0, stage <= self.half, stage < self.half)
        if stage == 0:
            valid = valid & (layer == 0)
        l = jnp.where(l < 0, l + self.grid, l)
        return jnp.where(l >= self.grid, l - self.grid, l), valid


def late_core(plan, a):
    l, valid = plan.taken(a, jnp.int32(0), plan.stages)
    other_l, other_valid = plan.taken(a, jnp.int32(1), plan.stages)
    late = jnp.where(valid, 0, 1)
    return late, jnp.where(valid, l, other_l), valid | other_valid


def place():
    return tuple(lax.axis_index(n) for n in ("col", "row", "layer"))


def list_kernel(plan, bounds, slot_keys, pairs, keys, codes):
    slots = slot_keys.shape[2]
    stages = plan.stages + 2
    a, b, layer = place()
    lane = lax.broadcasted_iota(jnp.int32, (1, LANES), 1)
    down = lax.broadcasted_iota(jnp.int32, (LANES, LANES), 0)
    across = lax.broadcasted_iota(jnp.int32, (LANES, LANES), 1)

    keys[...] = jnp.full_like(keys, -1)
    jobs = [plan.taken(a, layer, stage) for stage in range(stages - 1)]
    jobs.append(late_core(plan, a)[1:])
    for stage, (l, valid) in enumerate(jobs):
        l = jnp.clip(l, 0, plan.grid - 1)
        keys[pl.ds(stage, 1), 0:slots] = slot_keys[a, pl.ds(l, 1), :]
        keys[pl.ds(stages + stage, 1), 0:slots] = slot_keys[l, pl.ds(b, 1), :]
    keys[pl.ds(2 * stages, 1), 0:slots] = slot_keys[a, pl.ds(b, 1), :]
    out = keys[pl.ds(2 * stages, 1), :]
    out = jnp.where(lane < LANES // 2, out, pltpu.roll(out, LANES // 2, 1))
    slot = lane % (LANES // 2)
    r, d = out // 2, out % 2
    after = jnp.where(r + 1 == TB, 0, r + 1)
    second = lane >= LANES // 2
    left_key = jnp.where(second, 2 * r + 1, 2 * r)
    right_key = jnp.where(second, jnp.where(d == 1, 2 * after, -2), out)
    wanted = slot < slots
    left_key = jnp.where(wanted, left_key, -2)
    right_key = jnp.where(wanted, right_key, -2)
    columns = keys[...].T

    def find(column, key):
        hit = columns[:, column : column + 1] == key
        return jnp.sum(jnp.where(hit, down + 1, 0), axis=0, keepdims=True)

    codes[...] = jnp.zeros_like(codes)
    share = slots // 2
    for stage, (_, valid) in enumerate(jobs):
        left, right = find(stage, left_key), find(stages + stage, right_key)
        good = (left > 0) & (right > 0) & valid
        if stage == plan.stages:
            good = good & (right <= bounds[1])
        if stage > plan.stages:
            low = layer * share
            good = good & (right > bounds[1]) & (slot >= low) & (slot < low + share)
        code = ((left - 1) * 64 + (right - 1)) * 64 + slot + 1
        codes[pl.ds(stage, 1), :] = jnp.where(good, code, 0)
    found = codes[...] > 0
    ahead = jnp.dot(
        found.astype(jnp.float32),
        (down < across).astype(jnp.float32),
        preferred_element_type=jnp.float32,
    ).astype(jnp.int32)
    order = jnp.where(found, ahead, -1).T
    entries = codes[...].T
    for stage in range(pairs.shape[0]):
        hit = order[:, stage : stage + 1] == across
        entry = jnp.where(hit, entries[:, stage : stage + 1], 0)
        entry = jnp.sum(entry, axis=0, keepdims=True)
        count = jnp.sum(
            found[stage : stage + 1].astype(jnp.int32), axis=1, keepdims=True
        )
        entry = jnp.where(lane < count, entry - 1, slots)
        pairs[pl.ds(stage, 1), :] = jnp.where(lane == LANES - 1, count, entry)


def add_products(count, pairs, row, left, right, acc, at):
    def step(i, carry):
        codes = [pairs[row, i * GROUP + j] for j in range(GROUP)]
        products = [
            jnp.dot(
                left(code // 4096),
                right((code // 64) % 64),
                preferred_element_type=jnp.float32,
            )
            for code in codes
        ]
        for code, product in zip(codes, products):
            acc[at(code % 64)] += product
        return carry

    lax.fori_loop(0, (count + GROUP - 1) // GROUP, step, 0)


def blocks_of(parts):
    if len(parts) == 1:
        return lambda slot: parts[0][slot]
    first, second = parts
    size = first.shape[0]

    def block(slot):
        return lax.select(
            slot < size,
            first[jnp.minimum(slot, size - 1)],
            second[jnp.maximum(slot - size, 0)],
        )

    return block


class Lefts:
    def __init__(self, plan, refs):
        near = plan.grid // 2 - 1
        self.far = plan.grid - 1
        self.own, self.near = refs[0], refs[1 : 1 + near]
        self.swapped = refs[1 + near : 1 + 2 * near]
        self.halves = refs[1 + 2 * near :]

    def all(self, by, layer):
        yield from self.direct(by, layer)
        yield from self.indirect(by, layer)
        yield from self.opposite(by, layer)

    def direct(self, by, layer):
        yield by == 0, blocks_of([self.own])
        for k, tile in enumerate(self.near):
            yield by == 2 * k + 1 + layer, blocks_of([tile])

    def indirect(self, by, layer):
        for k, tile in enumerate(self.swapped):
            yield by == 2 * k + 2 - layer, blocks_of([tile])

    def opposite(self, by, layer):
        mine, other = self.halves
        share = mine.shape[0]

        def block(slot):
            second = (slot >= share).astype(jnp.int32)
            slot = slot - second * share
            return lax.select(second == layer, mine[slot], other[slot])

        yield by == self.far, block


def run_jobs(cases, count, pairs, row, right, acc, at=lambda slot: slot):
    for here, left in cases:

        @pl.when(here & (count > 0))
        def _(left=left):
            add_products(count, pairs, row, left, right, acc, at)


def stages_of(parts, refs):
    rights = []
    for n in parts:
        rights.append(refs[:n])
        refs = refs[n:]
    return rights, refs


def early_kernel(plan, n, parts, pairs, *refs):
    lefts = Lefts(plan, refs[:n])
    rights, (acc,) = stages_of(parts[:-1], refs[n:])
    a, b, layer = place()
    acc[...] = jnp.zeros_like(acc)
    for stage, right in enumerate(rights):
        by = b ^ plan.taken(a, layer, stage)[0]
        count = pairs[stage, pairs.shape[1] - 1]
        cases = lefts.direct(by, layer)
        run_jobs(cases, count, pairs, stage, blocks_of(right), acc)


def second_kernel(plan, n, parts, pairs, total, *refs):
    del total
    lefts = Lefts(plan, refs[:n])
    rights, (acc,) = stages_of(parts[:-1], refs[n:])
    a, b, layer = place()
    for stage, right in enumerate(rights):
        by = b ^ plan.taken(a, layer, stage)[0]
        count = pairs[stage, pairs.shape[1] - 1]
        cases = lefts.indirect(by, layer)
        run_jobs(cases, count, pairs, stage, blocks_of(right), acc)


def pick_kernel(tile, half):
    share = half.shape[0]
    half[...] = tile[pl.ds(lax.axis_index("layer") * share, share)]


def middle_kernel(plan, n, parts, pairs, total, *refs):
    del total
    lefts = Lefts(plan, refs[:n])
    rights, (first, acc, mine, other) = stages_of(parts[:-1], refs[n:])
    a, b, layer = place()
    last = pairs.shape[1] - 1
    for stage, right in enumerate([*rights, [first]]):
        by = b ^ plan.taken(a, layer, stage)[0]
        cases = (lefts.all if stage == plan.stages else lefts.opposite)(by, layer)
        run_jobs(cases, pairs[stage, last], pairs, stage, blocks_of(right), acc)
    share = other.shape[0]
    mine[...] = acc[pl.ds(layer * share, share)]
    other[...] = acc[pl.ds((1 - layer) * share, share)]


def last_kernel(plan, n, low, pairs, mine, received, *refs):
    lefts = Lefts(plan, refs[:n])
    part, part_swapped, out, acc, rounded, sem = refs[n:]
    a, b, layer = place()
    share = out.shape[0]
    acc[pl.ds(0, share)] = mine[...] + received[...]
    late, l, _ = late_core(plan, a)
    by = b ^ l
    row = plan.stages + 1
    cases = lefts.all(by, layer)

    def right(slot):
        slot = jnp.maximum(slot - low, 0)
        return lax.select(late == layer, part[slot], part_swapped[slot])

    count = pairs[row, pairs.shape[1] - 1]
    run_jobs(
        cases,
        count,
        pairs,
        row,
        right,
        acc,
        lambda slot: jnp.minimum(slot - layer * share, share),
    )
    copies = []
    for j, (start, end) in enumerate(((0, share // 2), (share // 2, share))):
        here = pl.ds(start, end - start)
        rounded[here] = acc[here].astype(rounded.dtype)
        copies.append(pltpu.make_async_copy(rounded.at[here], out.at[here], sem.at[j]))
        copies[-1].start()
    for copy in copies:
        copy.wait()


def on_device(plan, x_blocks, slot_rows, slot_cols):
    own = x_blocks[0, 0]
    slots, size = own.shape[0], own.shape[1]
    share = slots // 2
    bounds = [slots * i // CHUNKS for i in range(CHUNKS + 1)]
    held = [
        (lax.optimization_barrier(own) if i else own)[i:j]
        for i, j in zip(bounds[:-1], bounds[1:])
    ]
    scalars = pl.BlockSpec(memory_space=pltpu.SMEM)
    vmem = pl.BlockSpec(memory_space=pltpu.VMEM)
    compiler_params = pltpu.CompilerParams(vmem_limit_bytes=GRANT)
    tile_bytes = own.size * 2

    def cost(products, tiles):
        return pl.CostEstimate(
            flops=2 * size**3 * products,
            bytes_accessed=tiles * tile_bytes,
            transcendentals=0,
        )

    lists = pl.pallas_call(
        functools.partial(list_kernel, plan, bounds),
        out_shape=jax.ShapeDtypeStruct((plan.stages + CHUNKS, LANES), jnp.int32),
        in_specs=[vmem],
        out_specs=vmem,
        scratch_shapes=[pltpu.VMEM((LANES, LANES), jnp.int32)] * 2,
        compiler_params=compiler_params,
        cost_estimate=cost(0, 2),
        name="list_products",
    )(2 * slot_rows + (slot_cols != slot_rows))
    rights = [[own]]
    for stage in range(1, plan.stages + 1):
        pairs = plan.hop_pairs(stage)
        arrived = []
        for part in held:
            arrived.append(lax.ppermute(part, ("col", "layer"), pairs))
        rights.append(arrived)
        held = list(arrived)
    everywhere = ("row", "col", "layer")
    swap = [(0, 1), (1, 0)]
    near, swapped = [], []
    for k in range(plan.grid // 2 - 1):
        bys = (2 * k + 1, 2 * k + 2)
        near.append(lax.ppermute(own, everywhere, plan.near_pairs(bys)))
        swapped.append(lax.ppermute(near[-1], "layer", swap))
    sent = pl.pallas_call(
        pick_kernel,
        out_shape=jax.ShapeDtypeStruct((share, size, size), own.dtype),
        in_specs=[vmem],
        out_specs=vmem,
        compiler_params=compiler_params,
        cost_estimate=cost(0, 1),
        name="pick_half",
    )(near[0])
    far = lax.ppermute(sent, everywhere, plan.far_pairs())
    far_swapped = lax.ppermute(far, "layer", swap)
    direct = [own, *near]
    lefts = [*direct, *swapped, far, far_swapped]
    parts = [len(r) for r in rights]
    running = jax.ShapeDtypeStruct((slots + 1, size, size), jnp.float32)
    before = [part for stage in rights[:-1] for part in stage]
    total = pl.pallas_call(
        functools.partial(early_kernel, plan, len(direct), parts),
        out_shape=running,
        in_specs=[scalars] + [vmem] * (len(direct) + len(before)),
        out_specs=vmem,
        compiler_params=compiler_params,
        cost_estimate=cost(slots * plan.stages, 2 * plan.stages),
        name="early_products",
    )(lists, *direct, *before)
    total = pl.pallas_call(
        functools.partial(second_kernel, plan, len(direct) + len(swapped), parts),
        out_shape=running,
        in_specs=[scalars]
        + [vmem] * (1 + len(direct) + len(swapped) + len(before)),
        out_specs=vmem,
        input_output_aliases={1: 0},
        compiler_params=compiler_params,
        cost_estimate=cost(slots, 2),
        name="second_products",
    )(lists, total, *direct, *swapped, *before)
    first, second = rights[-1]
    half = jax.ShapeDtypeStruct((share, size, size), jnp.float32)
    _, mine, other = pl.pallas_call(
        functools.partial(middle_kernel, plan, len(lefts), parts),
        out_shape=(running, half, half),
        in_specs=[scalars] + [vmem] * (2 + len(lefts) + len(before)),
        out_specs=(vmem, vmem, vmem),
        input_output_aliases={1: 0},
        compiler_params=compiler_params,
        cost_estimate=cost(slots * plan.stages, 2 * plan.stages),
        name="middle_products",
    )(lists, total, *lefts, *before, first)
    received = lax.ppermute(other, "layer", swap)
    second_swapped = lax.ppermute(second, ("col", "layer"), plan.last_pairs())
    square = pl.pallas_call(
        functools.partial(last_kernel, plan, len(lefts), bounds[1]),
        out_shape=jax.ShapeDtypeStruct((share, size, size), jnp.bfloat16),
        in_specs=[scalars] + [vmem] * (4 + len(lefts)),
        out_specs=pl.BlockSpec(memory_space=pl.ANY),
        scratch_shapes=[
            pltpu.VMEM((share + 1, size, size), jnp.float32),
            pltpu.VMEM((share, size, size), jnp.bfloat16),
            pltpu.SemaphoreType.DMA((2,)),
        ],
        compiler_params=compiler_params,
        cost_estimate=cost(slots // 2, 4),
        name="last_products",
    )(lists, mine, received, *lefts, second, second_swapped)
    return square[None, None]


def solution(mesh):
    plan = Plan(mesh)

    def body(*args):
        return on_device(plan, *args)

    in_specs = (P("col", "row", None, None, None), P(), P())
    out_specs = P("col", "row", "layer", None, None)
    return jax.shard_map(
        body, mesh=mesh, in_specs=in_specs, out_specs=out_specs, check_vma=False
    )
```

```python
import functools

import jax
import jax.numpy as jnp
from jax import lax
from jax.experimental import pallas as pl
from jax.experimental.pallas import tpu as pltpu
from jax.sharding import PartitionSpec as P

TB = 28
GROUP = 8
LANES = 128
GRANT = 8 << 20
CHUNKS = 2


class Plan:
    def __init__(self, mesh):
        self.grid = mesh.shape["row"]
        self.half = min(6, self.grid) // 2
        self.whole = 2 * self.half == self.grid
        self.stages = self.grid - 1 if self.whole else self.half

    def shift(self, a, l):
        if self.whole:
            return l - a
        mid = self.grid // 2
        k = (l - a + mid) % self.grid - mid
        return k if -self.half <= k < self.half else None

    def hop_pairs(self, stage):
        pairs = []
        for source in range(self.grid):
            for layer, step in ((0, 1), (1, -1)):
                target = source + step
                origin = target - step * stage
                if self.whole and not (0 <= target < self.grid and 0 <= origin < self.grid):
                    continue
                target %= self.grid
                if self.shift(target, origin % self.grid) == -step * stage:
                    pairs.append((source * 2 + layer, target * 2 + layer))
        return pairs

    def near_pairs(self, bys):
        pairs = []
        for r in range(self.grid):
            for a in range(self.grid):
                if self.shift(a, r) is not None:
                    for layer, by in enumerate(bys):
                        pairs.append(
                            tuple(
                                (p * self.grid + a) * 2 + layer for p in (r, r ^ by)
                            )
                        )
        return pairs

    def far_pairs(self):
        far = self.grid - 1
        pairs = []
        for r in range(self.grid):
            for a in range(self.grid):
                if self.shift(a, r) is not None:
                    for layer, by in enumerate((1, 2)):
                        pairs.append(
                            tuple(
                                (p * self.grid + a) * 2 + layer
                                for p in (r ^ by, r ^ far)
                            )
                        )
        return pairs

    def taken(self, a, layer, stage):
        l = jnp.where(layer == 0, a - stage, a + stage)
        if self.whole:
            valid = (l >= 0) & (l < self.grid)
        else:
            valid = jnp.where(layer == 0, stage <= self.half, stage < self.half)
        if stage == 0:
            valid = valid & (layer == 0)
        l = jnp.where(l < 0, l + self.grid, l)
        return jnp.where(l >= self.grid, l - self.grid, l), valid


def late_core(plan, a):
    l, valid = plan.taken(a, jnp.int32(0), plan.stages)
    other_l, other_valid = plan.taken(a, jnp.int32(1), plan.stages)
    late = jnp.where(valid, 0, 1)
    return late, jnp.where(valid, l, other_l), valid | other_valid


def place():
    return tuple(lax.axis_index(n) for n in ("col", "row", "layer"))


def list_kernel(plan, bounds, slot_keys, pairs, keys, codes):
    slots = slot_keys.shape[2]
    stages = plan.stages + 2
    a, b, layer = place()
    lane = lax.broadcasted_iota(jnp.int32, (1, LANES), 1)
    down = lax.broadcasted_iota(jnp.int32, (LANES, LANES), 0)
    across = lax.broadcasted_iota(jnp.int32, (LANES, LANES), 1)

    keys[...] = jnp.full_like(keys, -1)
    jobs = [plan.taken(a, layer, stage) for stage in range(stages - 1)]
    jobs.append(late_core(plan, a)[1:])
    for stage, (l, valid) in enumerate(jobs):
        l = jnp.clip(l, 0, plan.grid - 1)
        keys[pl.ds(stage, 1), 0:slots] = slot_keys[a, pl.ds(l, 1), :]
        keys[pl.ds(stages + stage, 1), 0:slots] = slot_keys[l, pl.ds(b, 1), :]
    keys[pl.ds(2 * stages, 1), 0:slots] = slot_keys[a, pl.ds(b, 1), :]
    out = keys[pl.ds(2 * stages, 1), :]
    out = jnp.where(lane < LANES // 2, out, pltpu.roll(out, LANES // 2, 1))
    slot = lane % (LANES // 2)
    r, d = out // 2, out % 2
    after = jnp.where(r + 1 == TB, 0, r + 1)
    second = lane >= LANES // 2
    left_key = jnp.where(second, 2 * r + 1, 2 * r)
    right_key = jnp.where(second, jnp.where(d == 1, 2 * after, -2), out)
    wanted = slot < slots
    left_key = jnp.where(wanted, left_key, -2)
    right_key = jnp.where(wanted, right_key, -2)
    columns = keys[...].T

    def find(column, key):
        hit = columns[:, column : column + 1] == key
        return jnp.sum(jnp.where(hit, down + 1, 0), axis=0, keepdims=True)

    codes[...] = jnp.zeros_like(codes)
    share = slots // 2
    for stage, (_, valid) in enumerate(jobs):
        left, right = find(stage, left_key), find(stages + stage, right_key)
        good = (left > 0) & (right > 0) & valid
        if stage == plan.stages:
            good = good & (right <= bounds[1])
        if stage > plan.stages:
            low = layer * share
            good = good & (right > bounds[1]) & (slot >= low) & (slot < low + share)
        code = ((left - 1) * 64 + (right - 1)) * 64 + slot + 1
        codes[pl.ds(stage, 1), :] = jnp.where(good, code, 0)
    found = codes[...] > 0
    ahead = jnp.dot(
        found.astype(jnp.float32),
        (down < across).astype(jnp.float32),
        preferred_element_type=jnp.float32,
    ).astype(jnp.int32)
    order = jnp.where(found, ahead, -1).T
    entries = codes[...].T
    for stage in range(pairs.shape[0]):
        hit = order[:, stage : stage + 1] == across
        entry = jnp.where(hit, entries[:, stage : stage + 1], 0)
        entry = jnp.sum(entry, axis=0, keepdims=True)
        count = jnp.sum(
            found[stage : stage + 1].astype(jnp.int32), axis=1, keepdims=True
        )
        entry = jnp.where(lane < count, entry - 1, slots)
        pairs[pl.ds(stage, 1), :] = jnp.where(lane == LANES - 1, count, entry)


def add_products(count, pairs, row, left, right, acc, at):
    def step(i, carry):
        codes = [pairs[row, i * GROUP + j] for j in range(GROUP)]
        products = [
            jnp.dot(
                left(code // 4096),
                right((code // 64) % 64),
                preferred_element_type=jnp.float32,
            )
            for code in codes
        ]
        for code, product in zip(codes, products):
            acc[at(code % 64)] += product
        return carry

    lax.fori_loop(0, (count + GROUP - 1) // GROUP, step, 0)


def blocks_of(parts):
    if len(parts) == 1:
        return lambda slot: parts[0][slot]
    first, second = parts
    size = first.shape[0]

    def block(slot):
        return lax.select(
            slot < size,
            first[jnp.minimum(slot, size - 1)],
            second[jnp.maximum(slot - size, 0)],
        )

    return block


class Lefts:
    def __init__(self, plan, refs):
        near = plan.grid // 2 - 1
        self.far = plan.grid - 1
        self.own, refs = refs[:CHUNKS], refs[CHUNKS:]
        self.near, refs = refs[:near], refs[near:]
        self.swapped, self.halves = refs[:near], refs[near:]

    def all(self, by, layer):
        yield from self.direct(by, layer)
        yield from self.indirect(by, layer)
        yield from self.opposite(by, layer)

    def direct(self, by, layer):
        yield by == 0, blocks_of(self.own)
        for k, tile in enumerate(self.near):
            yield by == 2 * k + 1 + layer, blocks_of([tile])

    def indirect(self, by, layer):
        for k, tile in enumerate(self.swapped):
            yield by == 2 * k + 2 - layer, blocks_of([tile])

    def opposite(self, by, layer):
        mine, other = self.halves
        share = mine.shape[0]

        def block(slot):
            second = (slot >= share).astype(jnp.int32)
            slot = slot - second * share
            return lax.select(second == layer, mine[slot], other[slot])

        yield by == self.far, block


def run_jobs(cases, count, pairs, row, right, acc, at=lambda slot: slot):
    for here, left in cases:

        @pl.when(here & (count > 0))
        def _(left=left):
            add_products(count, pairs, row, left, right, acc, at)


def stages_of(parts, refs):
    rights = []
    for n in parts:
        rights.append(refs[:n])
        refs = refs[n:]
    return rights, refs


def early_kernel(plan, n, parts, pairs, *refs):
    lefts = Lefts(plan, refs[:n])
    rights, (acc,) = stages_of(parts[:-2], refs[n:])
    a, b, layer = place()
    acc[...] = jnp.zeros_like(acc)
    for stage, right in enumerate(rights):
        by = b ^ plan.taken(a, layer, stage)[0]
        count = pairs[stage, pairs.shape[1] - 1]
        cases = lefts.direct(by, layer)
        run_jobs(cases, count, pairs, stage, blocks_of(right), acc)


def second_kernel(plan, n, parts, pairs, total, *refs):
    del total
    lefts = Lefts(plan, refs[:n])
    rights, (acc,) = stages_of(parts[:-1], refs[n:])
    a, b, layer = place()
    for stage, right in enumerate(rights):
        by = b ^ plan.taken(a, layer, stage)[0]
        count = pairs[stage, pairs.shape[1] - 1]
        cases = list(lefts.indirect(by, layer))
        if stage == plan.stages - 1:
            cases += lefts.direct(by, layer)
        run_jobs(cases, count, pairs, stage, blocks_of(right), acc)


def split_kernel(tile, first, second, sem):
    size = first.shape[0]
    copies = [
        pltpu.make_async_copy(tile.at[pl.ds(0, size)], first, sem.at[0]),
        pltpu.make_async_copy(
            tile.at[pl.ds(size, second.shape[0])], second, sem.at[1]
        ),
    ]
    for copy in copies:
        copy.start()
    for copy in copies:
        copy.wait()


def pick_kernel(tile, half):
    share = half.shape[0]
    half[...] = tile[pl.ds(lax.axis_index("layer") * share, share)]


def middle_kernel(plan, n, parts, pairs, total, *refs):
    del total
    lefts = Lefts(plan, refs[:n])
    rights, (first, acc, mine, other) = stages_of(parts[:-1], refs[n:])
    a, b, layer = place()
    last = pairs.shape[1] - 1
    for stage, right in enumerate([*rights, [first]]):
        by = b ^ plan.taken(a, layer, stage)[0]
        cases = (lefts.all if stage == plan.stages else lefts.opposite)(by, layer)
        run_jobs(cases, pairs[stage, last], pairs, stage, blocks_of(right), acc)
    share = other.shape[0]
    mine[...] = acc[pl.ds(layer * share, share)]
    other[...] = acc[pl.ds((1 - layer) * share, share)]


def last_kernel(plan, n, low, pairs, mine, received, *refs):
    lefts = Lefts(plan, refs[:n])
    part, part_swapped, out, acc, rounded, sem = refs[n:]
    a, b, layer = place()
    share = out.shape[0]
    acc[pl.ds(0, share)] = mine[...] + received[...]
    late, l, _ = late_core(plan, a)
    by = b ^ l
    row = plan.stages + 1
    cases = lefts.all(by, layer)

    def right(slot):
        slot = jnp.maximum(slot - low, 0)
        return lax.select(late == layer, part[slot], part_swapped[slot])

    count = pairs[row, pairs.shape[1] - 1]
    run_jobs(
        cases,
        count,
        pairs,
        row,
        right,
        acc,
        lambda slot: jnp.minimum(slot - layer * share, share),
    )
    copies = []
    for j, (start, end) in enumerate(((0, share // 2), (share // 2, share))):
        here = pl.ds(start, end - start)
        rounded[here] = acc[here].astype(rounded.dtype)
        copies.append(pltpu.make_async_copy(rounded.at[here], out.at[here], sem.at[j]))
        copies[-1].start()
    for copy in copies:
        copy.wait()


def on_device(plan, x_blocks, slot_rows, slot_cols):
    own = x_blocks[0, 0]
    slots, size = own.shape[0], own.shape[1]
    share = slots // 2
    bounds = [slots * i // CHUNKS for i in range(CHUNKS + 1)]
    scalars = pl.BlockSpec(memory_space=pltpu.SMEM)
    vmem = pl.BlockSpec(memory_space=pltpu.VMEM)
    compiler_params = pltpu.CompilerParams(vmem_limit_bytes=GRANT)
    tile_bytes = own.size * 2

    def cost(products, tiles):
        return pl.CostEstimate(
            flops=2 * size**3 * products,
            bytes_accessed=tiles * tile_bytes,
            transcendentals=0,
        )

    held = pl.pallas_call(
        split_kernel,
        out_shape=[
            jax.ShapeDtypeStruct((j - i, size, size), own.dtype)
            for i, j in zip(bounds[:-1], bounds[1:])
        ],
        in_specs=[pl.BlockSpec(memory_space=pl.ANY)],
        out_specs=[vmem] * CHUNKS,
        scratch_shapes=[pltpu.SemaphoreType.DMA((CHUNKS,))],
        compiler_params=compiler_params,
        cost_estimate=cost(0, 2),
        name="split_tile",
    )(own)
    lists = pl.pallas_call(
        functools.partial(list_kernel, plan, bounds),
        out_shape=jax.ShapeDtypeStruct((plan.stages + CHUNKS, LANES), jnp.int32),
        in_specs=[vmem],
        out_specs=vmem,
        scratch_shapes=[pltpu.VMEM((LANES, LANES), jnp.int32)] * 2,
        compiler_params=compiler_params,
        cost_estimate=cost(0, 2),
        name="list_products",
    )(2 * slot_rows + (slot_cols != slot_rows))
    own_parts = list(held)
    rights = [own_parts]
    for stage in range(1, plan.stages + 1):
        pairs = plan.hop_pairs(stage)
        arrived = []
        for part in held:
            arrived.append(lax.ppermute(part, ("col", "layer"), pairs))
        rights.append(arrived)
        held = list(arrived)
    everywhere = ("row", "col", "layer")
    swap = [(0, 1), (1, 0)]
    near, swapped = [], []
    for k in range(plan.grid // 2 - 1):
        bys = (2 * k + 1, 2 * k + 2)
        near.append(lax.ppermute(own, everywhere, plan.near_pairs(bys)))
        swapped.append(lax.ppermute(near[-1], "layer", swap))
    sent = pl.pallas_call(
        pick_kernel,
        out_shape=jax.ShapeDtypeStruct((share, size, size), own.dtype),
        in_specs=[vmem],
        out_specs=vmem,
        compiler_params=compiler_params,
        cost_estimate=cost(0, 1),
        name="pick_half",
    )(near[0])
    far = lax.ppermute(sent, everywhere, plan.far_pairs())
    far_swapped = lax.ppermute(far, "layer", swap)
    direct = [*own_parts, *near]
    lefts = [*direct, *swapped, far, far_swapped]
    parts = [len(r) for r in rights]
    running = jax.ShapeDtypeStruct((slots + 1, size, size), jnp.float32)
    before = [part for stage in rights[:-1] for part in stage]
    total = pl.pallas_call(
        functools.partial(early_kernel, plan, len(direct), parts),
        out_shape=running,
        in_specs=[scalars] + [vmem] * (len(direct) + len(before) - parts[-2]),
        out_specs=vmem,
        compiler_params=compiler_params,
        cost_estimate=cost(slots * plan.stages, 2 * plan.stages),
        name="early_products",
    )(lists, *direct, *before[: -parts[-2]])
    total = pl.pallas_call(
        functools.partial(second_kernel, plan, len(direct) + len(swapped), parts),
        out_shape=running,
        in_specs=[scalars]
        + [vmem] * (1 + len(direct) + len(swapped) + len(before)),
        out_specs=vmem,
        input_output_aliases={1: 0},
        compiler_params=compiler_params,
        cost_estimate=cost(slots, 2),
        name="second_products",
    )(lists, total, *direct, *swapped, *before)
    first, second = rights[-1]
    half = jax.ShapeDtypeStruct((share, size, size), jnp.float32)
    _, mine, other = pl.pallas_call(
        functools.partial(middle_kernel, plan, len(lefts), parts),
        out_shape=(running, half, half),
        in_specs=[scalars] + [vmem] * (2 + len(lefts) + len(before)),
        out_specs=(vmem, vmem, vmem),
        input_output_aliases={1: 0},
        compiler_params=compiler_params,
        cost_estimate=cost(slots * plan.stages, 2 * plan.stages),
        name="middle_products",
    )(lists, total, *lefts, *before, first)
    received = lax.ppermute(other, "layer", swap)
    second_swapped = lax.ppermute(second, "layer", swap)
    square = pl.pallas_call(
        functools.partial(last_kernel, plan, len(lefts), bounds[1]),
        out_shape=jax.ShapeDtypeStruct((share, size, size), jnp.bfloat16),
        in_specs=[scalars] + [vmem] * (4 + len(lefts)),
        out_specs=pl.BlockSpec(memory_space=pl.ANY),
        scratch_shapes=[
            pltpu.VMEM((share + 1, size, size), jnp.float32),
            pltpu.VMEM((share, size, size), jnp.bfloat16),
            pltpu.SemaphoreType.DMA((2,)),
        ],
        compiler_params=compiler_params,
        cost_estimate=cost(slots // 2, 4),
        name="last_products",
    )(lists, mine, received, *lefts, second, second_swapped)
    return square[None, None]


def solution(mesh):
    plan = Plan(mesh)

    def body(*args):
        return on_device(plan, *args)

    in_specs = (P("col", "row", None, None, None), P(), P())
    out_specs = P("col", "row", "layer", None, None)
    return jax.shard_map(
        body, mesh=mesh, in_specs=in_specs, out_specs=out_specs, check_vma=False
    )
```

```python
import functools

import jax
import jax.numpy as jnp
from jax import lax
from jax.experimental import pallas as pl
from jax.experimental.pallas import tpu as pltpu
from jax.sharding import PartitionSpec as P

TB = 28
GROUP = 8
LANES = 128
WRITTEN = 2
GRANT = 8 << 20
CHUNKS = 2


class Plan:
    def __init__(self, mesh):
        self.grid = mesh.shape["row"]
        self.half = min(6, self.grid) // 2
        self.whole = 2 * self.half == self.grid
        self.stages = self.grid - 1 if self.whole else self.half

    def shift(self, a, l):
        if self.whole:
            return l - a
        mid = self.grid // 2
        k = (l - a + mid) % self.grid - mid
        return k if -self.half <= k < self.half else None

    def hop_pairs(self, stage):
        pairs = []
        for source in range(self.grid):
            for layer, step in ((0, 1), (1, -1)):
                target = source + step
                origin = target - step * stage
                if self.whole and not (0 <= target < self.grid and 0 <= origin < self.grid):
                    continue
                target %= self.grid
                if self.shift(target, origin % self.grid) == -step * stage:
                    pairs.append((source * 2 + layer, target * 2 + layer))
        return pairs

    def near_pairs(self, bys):
        pairs = []
        for r in range(self.grid):
            for a in range(self.grid):
                if self.shift(a, r) is not None:
                    for layer, by in enumerate(bys):
                        pairs.append(
                            tuple(
                                (p * self.grid + a) * 2 + layer for p in (r, r ^ by)
                            )
                        )
        return pairs

    def far_pairs(self):
        far = self.grid - 1
        pairs = []
        for r in range(self.grid):
            for a in range(self.grid):
                if self.shift(a, r) is not None:
                    for layer, by in enumerate((1, 2)):
                        pairs.append(
                            tuple(
                                (p * self.grid + a) * 2 + layer
                                for p in (r ^ by, r ^ far)
                            )
                        )
        return pairs

    def taken(self, a, layer, stage):
        l = jnp.where(layer == 0, a - stage, a + stage)
        if self.whole:
            valid = (l >= 0) & (l < self.grid)
        else:
            valid = jnp.where(layer == 0, stage <= self.half, stage < self.half)
        if stage == 0:
            valid = valid & (layer == 0)
        l = jnp.where(l < 0, l + self.grid, l)
        return jnp.where(l >= self.grid, l - self.grid, l), valid


def late_core(plan, a):
    l, valid = plan.taken(a, jnp.int32(0), plan.stages)
    other_l, other_valid = plan.taken(a, jnp.int32(1), plan.stages)
    late = jnp.where(valid, 0, 1)
    return late, jnp.where(valid, l, other_l), valid | other_valid


def place():
    return tuple(lax.axis_index(n) for n in ("col", "row", "layer"))


def list_kernel(plan, bounds, slot_keys, pairs, keys, codes):
    slots = slot_keys.shape[2]
    stages = plan.stages + 2
    a, b, layer = place()
    lane = lax.broadcasted_iota(jnp.int32, (1, LANES), 1)
    down = lax.broadcasted_iota(jnp.int32, (LANES, LANES), 0)
    across = lax.broadcasted_iota(jnp.int32, (LANES, LANES), 1)

    keys[...] = jnp.full_like(keys, -1)
    jobs = [plan.taken(a, layer, stage) for stage in range(stages - 1)]
    jobs.append(late_core(plan, a)[1:])
    for stage, (l, valid) in enumerate(jobs):
        l = jnp.clip(l, 0, plan.grid - 1)
        keys[pl.ds(stage, 1), 0:slots] = slot_keys[a, pl.ds(l, 1), :]
        keys[pl.ds(stages + stage, 1), 0:slots] = slot_keys[l, pl.ds(b, 1), :]
    keys[pl.ds(2 * stages, 1), 0:slots] = slot_keys[a, pl.ds(b, 1), :]
    out = keys[pl.ds(2 * stages, 1), :]
    out = jnp.where(lane < LANES // 2, out, pltpu.roll(out, LANES // 2, 1))
    slot = lane % (LANES // 2)
    r, d = out // 2, out % 2
    after = jnp.where(r + 1 == TB, 0, r + 1)
    second = lane >= LANES // 2
    left_key = jnp.where(second, 2 * r + 1, 2 * r)
    right_key = jnp.where(second, jnp.where(d == 1, 2 * after, -2), out)
    wanted = slot < slots
    left_key = jnp.where(wanted, left_key, -2)
    right_key = jnp.where(wanted, right_key, -2)
    columns = keys[...].T

    def find(column, key):
        hit = columns[:, column : column + 1] == key
        return jnp.sum(jnp.where(hit, down + 1, 0), axis=0, keepdims=True)

    codes[...] = jnp.zeros_like(codes)
    share = slots // 2
    for stage, (_, valid) in enumerate(jobs):
        left, right = find(stage, left_key), find(stages + stage, right_key)
        good = (left > 0) & (right > 0) & valid
        if stage == plan.stages:
            good = good & (right <= bounds[1])
        if stage > plan.stages:
            low = layer * share
            good = good & (right > bounds[1]) & (slot >= low) & (slot < low + share)
        code = ((left - 1) * 64 + (right - 1)) * 64 + slot + 1
        codes[pl.ds(stage, 1), :] = jnp.where(good, code, 0)
    found = codes[...] > 0
    ahead = jnp.dot(
        found.astype(jnp.float32),
        (down < across).astype(jnp.float32),
        preferred_element_type=jnp.float32,
    ).astype(jnp.int32)
    order = jnp.where(found, ahead, -1).T
    entries = codes[...].T
    for stage in range(pairs.shape[0]):
        hit = order[:, stage : stage + 1] == across
        entry = jnp.where(hit, entries[:, stage : stage + 1], 0)
        entry = jnp.sum(entry, axis=0, keepdims=True)
        count = jnp.sum(
            found[stage : stage + 1].astype(jnp.int32), axis=1, keepdims=True
        )
        entry = jnp.where(lane < count, entry - 1, slots)
        pairs[pl.ds(stage, 1), :] = jnp.where(lane == LANES - 1, count, entry)


def add_products(count, pairs, row, left, right, acc, at):
    def step(i, carry):
        codes = [pairs[row, i * GROUP + j] for j in range(GROUP)]
        products = [
            jnp.dot(
                left(code // 4096),
                right((code // 64) % 64),
                preferred_element_type=jnp.float32,
            )
            for code in codes
        ]
        for code, product in zip(codes, products):
            acc[at(code % 64)] += product
        return carry

    lax.fori_loop(0, (count + GROUP - 1) // GROUP, step, 0)


def blocks_of(parts):
    if len(parts) == 1:
        return lambda slot: parts[0][slot]
    first, second = parts
    size = first.shape[0]

    def block(slot):
        return lax.select(
            slot < size,
            first[jnp.minimum(slot, size - 1)],
            second[jnp.maximum(slot - size, 0)],
        )

    return block


class Lefts:
    def __init__(self, plan, refs):
        near = plan.grid // 2 - 1
        self.far = plan.grid - 1
        self.own, refs = refs[:CHUNKS], refs[CHUNKS:]
        self.near, refs = refs[:near], refs[near:]
        self.swapped, self.halves = refs[:near], refs[near:]

    def all(self, by, layer):
        yield from self.direct(by, layer)
        yield from self.indirect(by, layer)
        yield from self.opposite(by, layer)

    def direct(self, by, layer):
        yield by == 0, blocks_of(self.own)
        for k, tile in enumerate(self.near):
            yield by == 2 * k + 1 + layer, blocks_of([tile])

    def indirect(self, by, layer):
        for k, tile in enumerate(self.swapped):
            yield by == 2 * k + 2 - layer, blocks_of([tile])

    def opposite(self, by, layer):
        mine, other = self.halves
        share = mine.shape[0]

        def block(slot):
            second = (slot >= share).astype(jnp.int32)
            slot = slot - second * share
            return lax.select(second == layer, mine[slot], other[slot])

        yield by == self.far, block


def run_jobs(cases, count, pairs, row, right, acc, at=lambda slot: slot):
    for here, left in cases:

        @pl.when(here & (count > 0))
        def _(left=left):
            add_products(count, pairs, row, left, right, acc, at)


def stages_of(parts, refs):
    rights = []
    for n in parts:
        rights.append(refs[:n])
        refs = refs[n:]
    return rights, refs


def early_kernel(plan, n, parts, pairs, *refs):
    lefts = Lefts(plan, refs[:n])
    rights, (acc,) = stages_of(parts[:-2], refs[n:])
    a, b, layer = place()
    acc[...] = jnp.zeros_like(acc)
    for stage, right in enumerate(rights):
        by = b ^ plan.taken(a, layer, stage)[0]
        count = pairs[stage, pairs.shape[1] - 1]
        cases = lefts.direct(by, layer)
        run_jobs(cases, count, pairs, stage, blocks_of(right), acc)


def second_kernel(plan, n, parts, pairs, total, *refs):
    del total
    lefts = Lefts(plan, refs[:n])
    rights, (acc,) = stages_of(parts[:-1], refs[n:])
    a, b, layer = place()
    for stage, right in enumerate(rights):
        by = b ^ plan.taken(a, layer, stage)[0]
        count = pairs[stage, pairs.shape[1] - 1]
        cases = list(lefts.indirect(by, layer))
        if stage == plan.stages - 1:
            cases += lefts.direct(by, layer)
        run_jobs(cases, count, pairs, stage, blocks_of(right), acc)


def split_kernel(low, tile, part, sem):
    size = part.shape[0]
    copies = [
        pltpu.make_async_copy(
            tile.at[pl.ds(low + start, end - start)],
            part.at[pl.ds(start, end - start)],
            sem.at[j],
        )
        for j, (start, end) in enumerate(((0, size // 2), (size // 2, size)))
    ]
    for copy in copies:
        copy.start()
    for copy in copies:
        copy.wait()


def pick_kernel(tile, half):
    share = half.shape[0]
    half[...] = tile[pl.ds(lax.axis_index("layer") * share, share)]


def middle_kernel(plan, n, parts, pairs, total, *refs):
    del total
    lefts = Lefts(plan, refs[:n])
    rights, (first, acc, mine, other) = stages_of(parts[:-1], refs[n:])
    a, b, layer = place()
    last = pairs.shape[1] - 1
    for stage, right in enumerate([*rights, [first]]):
        by = b ^ plan.taken(a, layer, stage)[0]
        cases = (lefts.all if stage == plan.stages else lefts.opposite)(by, layer)
        run_jobs(cases, pairs[stage, last], pairs, stage, blocks_of(right), acc)
    share = other.shape[0]
    mine[...] = acc[pl.ds(layer * share, share)]
    other[...] = acc[pl.ds((1 - layer) * share, share)]


def last_kernel(plan, n, low, pairs, mine, received, *refs):
    lefts = Lefts(plan, refs[:n])
    part, part_swapped, out, acc, rounded, sem = refs[n:]
    a, b, layer = place()
    share = out.shape[0]
    acc[pl.ds(0, share)] = mine[...] + received[...]
    late, l, _ = late_core(plan, a)
    by = b ^ l
    row = plan.stages + 1
    cases = lefts.all(by, layer)

    def right(slot):
        slot = jnp.maximum(slot - low, 0)
        return lax.select(late == layer, part[slot], part_swapped[slot])

    count = pairs[row, pairs.shape[1] - 1]
    run_jobs(
        cases,
        count,
        pairs,
        row,
        right,
        acc,
        lambda slot: jnp.minimum(slot - layer * share, share),
    )
    copies = []
    for j, start in enumerate(range(0, share, WRITTEN)):
        here = pl.ds(start, min(WRITTEN, share - start))
        rounded[here] = acc[here].astype(rounded.dtype)
        copies.append(pltpu.make_async_copy(rounded.at[here], out.at[here], sem.at[j]))
        copies[-1].start()
    for copy in copies:
        copy.wait()


def on_device(plan, x_blocks, slot_rows, slot_cols):
    own = x_blocks[0, 0]
    slots, size = own.shape[0], own.shape[1]
    share = slots // 2
    bounds = [slots * i // CHUNKS for i in range(CHUNKS + 1)]
    scalars = pl.BlockSpec(memory_space=pltpu.SMEM)
    vmem = pl.BlockSpec(memory_space=pltpu.VMEM)
    compiler_params = pltpu.CompilerParams(vmem_limit_bytes=GRANT)
    tile_bytes = own.size * 2

    def cost(products, tiles):
        return pl.CostEstimate(
            flops=2 * size**3 * products,
            bytes_accessed=tiles * tile_bytes,
            transcendentals=0,
        )

    held = [
        pl.pallas_call(
            functools.partial(split_kernel, i),
            out_shape=jax.ShapeDtypeStruct((j - i, size, size), own.dtype),
            in_specs=[pl.BlockSpec(memory_space=pl.ANY)],
            out_specs=vmem,
            scratch_shapes=[pltpu.SemaphoreType.DMA((2,))],
            compiler_params=compiler_params,
            cost_estimate=cost(0, 1),
            name="split_tile",
        )(own)
        for i, j in zip(bounds[:-1], bounds[1:])
    ]
    lists = pl.pallas_call(
        functools.partial(list_kernel, plan, bounds),
        out_shape=jax.ShapeDtypeStruct((plan.stages + CHUNKS, LANES), jnp.int32),
        in_specs=[vmem],
        out_specs=vmem,
        scratch_shapes=[pltpu.VMEM((LANES, LANES), jnp.int32)] * 2,
        compiler_params=compiler_params,
        cost_estimate=cost(0, 2),
        name="list_products",
    )(2 * slot_rows + (slot_cols != slot_rows))
    own_parts = list(held)
    rights = [own_parts]
    for stage in range(1, plan.stages + 1):
        pairs = plan.hop_pairs(stage)
        arrived = []
        for part in held:
            arrived.append(lax.ppermute(part, ("col", "layer"), pairs))
        rights.append(arrived)
        held = list(arrived)
    everywhere = ("row", "col", "layer")
    swap = [(0, 1), (1, 0)]
    near, swapped = [], []
    for k in range(plan.grid // 2 - 1):
        bys = (2 * k + 1, 2 * k + 2)
        near.append(lax.ppermute(own, everywhere, plan.near_pairs(bys)))
        swapped.append(lax.ppermute(near[-1], "layer", swap))
    sent = pl.pallas_call(
        pick_kernel,
        out_shape=jax.ShapeDtypeStruct((share, size, size), own.dtype),
        in_specs=[vmem],
        out_specs=vmem,
        compiler_params=compiler_params,
        cost_estimate=cost(0, 1),
        name="pick_half",
    )(near[0])
    far = lax.ppermute(sent, everywhere, plan.far_pairs())
    far_swapped = lax.ppermute(far, "layer", swap)
    direct = [*own_parts, *near]
    lefts = [*direct, *swapped, far, far_swapped]
    parts = [len(r) for r in rights]
    running = jax.ShapeDtypeStruct((slots + 1, size, size), jnp.float32)
    before = [part for stage in rights[:-1] for part in stage]
    total = pl.pallas_call(
        functools.partial(early_kernel, plan, len(direct), parts),
        out_shape=running,
        in_specs=[scalars] + [vmem] * (len(direct) + len(before) - parts[-2]),
        out_specs=vmem,
        compiler_params=compiler_params,
        cost_estimate=cost(slots * plan.stages, 2 * plan.stages),
        name="early_products",
    )(lists, *direct, *before[: -parts[-2]])
    total = pl.pallas_call(
        functools.partial(second_kernel, plan, len(direct) + len(swapped), parts),
        out_shape=running,
        in_specs=[scalars]
        + [vmem] * (1 + len(direct) + len(swapped) + len(before)),
        out_specs=vmem,
        input_output_aliases={1: 0},
        compiler_params=compiler_params,
        cost_estimate=cost(slots, 2),
        name="second_products",
    )(lists, total, *direct, *swapped, *before)
    first, second = rights[-1]
    half = jax.ShapeDtypeStruct((share, size, size), jnp.float32)
    _, mine, other = pl.pallas_call(
        functools.partial(middle_kernel, plan, len(lefts), parts),
        out_shape=(running, half, half),
        in_specs=[scalars] + [vmem] * (2 + len(lefts) + len(before)),
        out_specs=(vmem, vmem, vmem),
        input_output_aliases={1: 0},
        compiler_params=compiler_params,
        cost_estimate=cost(slots * plan.stages, 2 * plan.stages),
        name="middle_products",
    )(lists, total, *lefts, *before, first)
    received = lax.ppermute(other, "layer", swap)
    second_swapped = lax.ppermute(second, "layer", swap)
    square = pl.pallas_call(
        functools.partial(last_kernel, plan, len(lefts), bounds[1]),
        out_shape=jax.ShapeDtypeStruct((share, size, size), jnp.bfloat16),
        in_specs=[scalars] + [vmem] * (4 + len(lefts)),
        out_specs=pl.BlockSpec(memory_space=pl.ANY),
        scratch_shapes=[
            pltpu.VMEM((share + 1, size, size), jnp.float32),
            pltpu.VMEM((share, size, size), jnp.bfloat16),
            pltpu.SemaphoreType.DMA((pl.cdiv(share, WRITTEN),)),
        ],
        compiler_params=compiler_params,
        cost_estimate=cost(slots // 2, 4),
        name="last_products",
    )(lists, mine, received, *lefts, second, second_swapped)
    return square[None, None]


def solution(mesh):
    plan = Plan(mesh)

    def body(*args):
        return on_device(plan, *args)

    in_specs = (P("col", "row", None, None, None), P(), P())
    out_specs = P("col", "row", "layer", None, None)
    return jax.shard_map(
        body, mesh=mesh, in_specs=in_specs, out_specs=out_specs, check_vma=False
    )
```

```python
import functools

import jax
import jax.numpy as jnp
from jax import lax
from jax.experimental import pallas as pl
from jax.experimental.pallas import tpu as pltpu
from jax.sharding import PartitionSpec as P

TB = 28
GROUP = 8
LANES = 128
GRANT = 8 << 20
CHUNKS = 2


class Plan:
    def __init__(self, mesh):
        self.grid = mesh.shape["row"]
        self.half = min(6, self.grid) // 2
        self.whole = 2 * self.half == self.grid
        self.stages = self.grid - 1 if self.whole else self.half

    def shift(self, a, l):
        if self.whole:
            return l - a
        mid = self.grid // 2
        k = (l - a + mid) % self.grid - mid
        return k if -self.half <= k < self.half else None

    def hop_pairs(self, stage):
        pairs = []
        for source in range(self.grid):
            for layer, step in ((0, 1), (1, -1)):
                target = source + step
                origin = target - step * stage
                if self.whole and not (0 <= target < self.grid and 0 <= origin < self.grid):
                    continue
                target %= self.grid
                if self.shift(target, origin % self.grid) == -step * stage:
                    pairs.append((source * 2 + layer, target * 2 + layer))
        return pairs

    def near_pairs(self, bys):
        pairs = []
        for r in range(self.grid):
            for a in range(self.grid):
                if self.shift(a, r) is not None:
                    for layer, by in enumerate(bys):
                        pairs.append(
                            tuple(
                                (p * self.grid + a) * 2 + layer for p in (r, r ^ by)
                            )
                        )
        return pairs

    def far_pairs(self):
        far = self.grid - 1
        pairs = []
        for r in range(self.grid):
            for a in range(self.grid):
                if self.shift(a, r) is not None:
                    for layer, by in enumerate((1, 2)):
                        pairs.append(
                            tuple(
                                (p * self.grid + a) * 2 + layer
                                for p in (r ^ by, r ^ far)
                            )
                        )
        return pairs

    def taken(self, a, layer, stage):
        l = jnp.where(layer == 0, a - stage, a + stage)
        if self.whole:
            valid = (l >= 0) & (l < self.grid)
        else:
            valid = jnp.where(layer == 0, stage <= self.half, stage < self.half)
        if stage == 0:
            valid = valid & (layer == 0)
        l = jnp.where(l < 0, l + self.grid, l)
        return jnp.where(l >= self.grid, l - self.grid, l), valid


def late_core(plan, a):
    l, valid = plan.taken(a, jnp.int32(0), plan.stages)
    other_l, other_valid = plan.taken(a, jnp.int32(1), plan.stages)
    late = jnp.where(valid, 0, 1)
    return late, jnp.where(valid, l, other_l), valid | other_valid


def place():
    return tuple(lax.axis_index(n) for n in ("col", "row", "layer"))


def list_kernel(plan, bounds, slot_keys, pairs, keys, codes):
    slots = slot_keys.shape[2]
    stages = plan.stages + 2
    a, b, layer = place()
    lane = lax.broadcasted_iota(jnp.int32, (1, LANES), 1)
    down = lax.broadcasted_iota(jnp.int32, (LANES, LANES), 0)
    across = lax.broadcasted_iota(jnp.int32, (LANES, LANES), 1)

    keys[...] = jnp.full_like(keys, -1)
    jobs = [plan.taken(a, layer, stage) for stage in range(stages - 1)]
    jobs.append(late_core(plan, a)[1:])
    for stage, (l, valid) in enumerate(jobs):
        l = jnp.clip(l, 0, plan.grid - 1)
        keys[pl.ds(stage, 1), 0:slots] = slot_keys[a, pl.ds(l, 1), :]
        keys[pl.ds(stages + stage, 1), 0:slots] = slot_keys[l, pl.ds(b, 1), :]
    keys[pl.ds(2 * stages, 1), 0:slots] = slot_keys[a, pl.ds(b, 1), :]
    out = keys[pl.ds(2 * stages, 1), :]
    out = jnp.where(lane < LANES // 2, out, pltpu.roll(out, LANES // 2, 1))
    slot = lane % (LANES // 2)
    r, d = out // 2, out % 2
    after = jnp.where(r + 1 == TB, 0, r + 1)
    second = lane >= LANES // 2
    left_key = jnp.where(second, 2 * r + 1, 2 * r)
    right_key = jnp.where(second, jnp.where(d == 1, 2 * after, -2), out)
    wanted = slot < slots
    left_key = jnp.where(wanted, left_key, -2)
    right_key = jnp.where(wanted, right_key, -2)
    columns = keys[...].T

    def find(column, key):
        hit = columns[:, column : column + 1] == key
        return jnp.sum(jnp.where(hit, down + 1, 0), axis=0, keepdims=True)

    codes[...] = jnp.zeros_like(codes)
    share = slots // 2
    for stage, (_, valid) in enumerate(jobs):
        left, right = find(stage, left_key), find(stages + stage, right_key)
        good = (left > 0) & (right > 0) & valid
        if stage == plan.stages:
            good = good & (right <= bounds[1])
        if stage > plan.stages:
            low = layer * share
            good = good & (right > bounds[1]) & (slot >= low) & (slot < low + share)
        code = ((left - 1) * 64 + (right - 1)) * 64 + slot + 1
        codes[pl.ds(stage, 1), :] = jnp.where(good, code, 0)
    found = codes[...] > 0
    ahead = jnp.dot(
        found.astype(jnp.float32),
        (down < across).astype(jnp.float32),
        preferred_element_type=jnp.float32,
    ).astype(jnp.int32)
    order = jnp.where(found, ahead, -1).T
    entries = codes[...].T
    for stage in range(pairs.shape[0]):
        hit = order[:, stage : stage + 1] == across
        entry = jnp.where(hit, entries[:, stage : stage + 1], 0)
        entry = jnp.sum(entry, axis=0, keepdims=True)
        count = jnp.sum(
            found[stage : stage + 1].astype(jnp.int32), axis=1, keepdims=True
        )
        entry = jnp.where(lane < count, entry - 1, slots)
        pairs[pl.ds(stage, 1), :] = jnp.where(lane == LANES - 1, count, entry)


def add_products(count, pairs, row, left, right, acc, at, group):
    def step(i, carry):
        codes = [pairs[row, i * group + j] for j in range(group)]
        products = [
            jnp.dot(
                left(code // 4096),
                right((code // 64) % 64),
                preferred_element_type=jnp.float32,
            )
            for code in codes
        ]
        for code, product in zip(codes, products):
            acc[at(code % 64)] += product
        return carry

    lax.fori_loop(0, (count + group - 1) // group, step, 0)


def blocks_of(parts):
    if len(parts) == 1:
        return lambda slot: parts[0][slot]
    first, second = parts
    size = first.shape[0]

    def block(slot):
        return lax.select(
            slot < size,
            first[jnp.minimum(slot, size - 1)],
            second[jnp.maximum(slot - size, 0)],
        )

    return block


class Lefts:
    def __init__(self, plan, refs):
        near = plan.grid // 2 - 1
        self.far = plan.grid - 1
        self.own, refs = refs[:CHUNKS], refs[CHUNKS:]
        self.near, refs = refs[:near], refs[near:]
        self.swapped, self.halves = refs[:near], refs[near:]

    def all(self, by, layer):
        yield from self.direct(by, layer)
        yield from self.indirect(by, layer)
        yield from self.opposite(by, layer)

    def direct(self, by, layer):
        yield by == 0, blocks_of(self.own)
        for k, tile in enumerate(self.near):
            yield by == 2 * k + 1 + layer, blocks_of([tile])

    def indirect(self, by, layer):
        for k, tile in enumerate(self.swapped):
            yield by == 2 * k + 2 - layer, blocks_of([tile])

    def opposite(self, by, layer):
        mine, other = self.halves
        share = mine.shape[0]

        def block(slot):
            second = (slot >= share).astype(jnp.int32)
            slot = slot - second * share
            return lax.select(second == layer, mine[slot], other[slot])

        yield by == self.far, block


def run_jobs(
    cases, count, pairs, row, right, acc, at=lambda slot: slot, group=GROUP
):
    for here, left in cases:

        @pl.when(here & (count > 0))
        def _(left=left):
            add_products(count, pairs, row, left, right, acc, at, group)


def stages_of(parts, refs):
    rights = []
    for n in parts:
        rights.append(refs[:n])
        refs = refs[n:]
    return rights, refs


def early_kernel(plan, n, parts, pairs, *refs):
    lefts = Lefts(plan, refs[:n])
    rights, (acc,) = stages_of(parts[:-2], refs[n:])
    a, b, layer = place()
    acc[...] = jnp.zeros_like(acc)
    for stage, right in enumerate(rights):
        by = b ^ plan.taken(a, layer, stage)[0]
        count = pairs[stage, pairs.shape[1] - 1]
        cases = lefts.direct(by, layer)
        run_jobs(cases, count, pairs, stage, blocks_of(right), acc)


def second_kernel(plan, n, parts, pairs, total, *refs):
    del total
    lefts = Lefts(plan, refs[:n])
    rights, (acc,) = stages_of(parts[:-1], refs[n:])
    a, b, layer = place()
    for stage, right in enumerate(rights):
        by = b ^ plan.taken(a, layer, stage)[0]
        count = pairs[stage, pairs.shape[1] - 1]
        cases = list(lefts.indirect(by, layer))
        if stage == plan.stages - 1:
            cases += lefts.direct(by, layer)
        run_jobs(cases, count, pairs, stage, blocks_of(right), acc)


def split_kernel(tile, first, second, sem):
    size = first.shape[0]
    copies = [
        pltpu.make_async_copy(tile.at[pl.ds(0, size)], first, sem.at[0]),
        pltpu.make_async_copy(
            tile.at[pl.ds(size, second.shape[0])], second, sem.at[1]
        ),
    ]
    for copy in copies:
        copy.start()
    for copy in copies:
        copy.wait()


def pick_kernel(tile, half):
    share = half.shape[0]
    half[...] = tile[pl.ds(lax.axis_index("layer") * share, share)]


def middle_kernel(plan, n, parts, pairs, total, *refs):
    del total
    lefts = Lefts(plan, refs[:n])
    rights, (first, acc, mine, other) = stages_of(parts[:-1], refs[n:])
    a, b, layer = place()
    last = pairs.shape[1] - 1
    for stage, right in enumerate([*rights, [first]]):
        by = b ^ plan.taken(a, layer, stage)[0]
        cases = (lefts.all if stage == plan.stages else lefts.opposite)(by, layer)
        run_jobs(cases, pairs[stage, last], pairs, stage, blocks_of(right), acc)
    share = other.shape[0]
    mine[...] = acc[pl.ds(layer * share, share)]
    other[...] = acc[pl.ds((1 - layer) * share, share)]


def last_kernel(plan, n, low, pairs, mine, received, *refs):
    lefts = Lefts(plan, refs[:n])
    part, part_swapped, out, acc, rounded, sem = refs[n:]
    a, b, layer = place()
    share = out.shape[0]
    acc[pl.ds(0, share)] = mine[...] + received[...]
    late, l, _ = late_core(plan, a)
    by = b ^ l
    row = plan.stages + 1
    cases = lefts.all(by, layer)

    def right(slot):
        slot = jnp.maximum(slot - low, 0)
        return lax.select(late == layer, part[slot], part_swapped[slot])

    count = pairs[row, pairs.shape[1] - 1]
    run_jobs(
        cases,
        count,
        pairs,
        row,
        right,
        acc,
        lambda slot: jnp.minimum(slot - layer * share, share),
        GROUP // 2,
    )
    copies = []
    for j, (start, end) in enumerate(((0, share // 2), (share // 2, share))):
        here = pl.ds(start, end - start)
        rounded[here] = acc[here].astype(rounded.dtype)
        copies.append(pltpu.make_async_copy(rounded.at[here], out.at[here], sem.at[j]))
        copies[-1].start()
    for copy in copies:
        copy.wait()


def on_device(plan, x_blocks, slot_rows, slot_cols):
    own = x_blocks[0, 0]
    slots, size = own.shape[0], own.shape[1]
    share = slots // 2
    bounds = [slots * i // CHUNKS for i in range(CHUNKS + 1)]
    scalars = pl.BlockSpec(memory_space=pltpu.SMEM)
    vmem = pl.BlockSpec(memory_space=pltpu.VMEM)
    compiler_params = pltpu.CompilerParams(vmem_limit_bytes=GRANT)
    tile_bytes = own.size * 2

    def cost(products, tiles):
        return pl.CostEstimate(
            flops=2 * size**3 * products,
            bytes_accessed=tiles * tile_bytes,
            transcendentals=0,
        )

    held = pl.pallas_call(
        split_kernel,
        out_shape=[
            jax.ShapeDtypeStruct((j - i, size, size), own.dtype)
            for i, j in zip(bounds[:-1], bounds[1:])
        ],
        in_specs=[pl.BlockSpec(memory_space=pl.ANY)],
        out_specs=[vmem] * CHUNKS,
        scratch_shapes=[pltpu.SemaphoreType.DMA((CHUNKS,))],
        compiler_params=compiler_params,
        cost_estimate=cost(0, 2),
        name="split_tile",
    )(own)
    lists = pl.pallas_call(
        functools.partial(list_kernel, plan, bounds),
        out_shape=jax.ShapeDtypeStruct((plan.stages + CHUNKS, LANES), jnp.int32),
        in_specs=[vmem],
        out_specs=vmem,
        scratch_shapes=[pltpu.VMEM((LANES, LANES), jnp.int32)] * 2,
        compiler_params=compiler_params,
        cost_estimate=cost(0, 2),
        name="list_products",
    )(2 * slot_rows + (slot_cols != slot_rows))
    own_parts = list(held)
    rights = [own_parts]
    for stage in range(1, plan.stages + 1):
        pairs = plan.hop_pairs(stage)
        arrived = []
        for part in held:
            arrived.append(lax.ppermute(part, ("col", "layer"), pairs))
        rights.append(arrived)
        held = list(arrived)
    everywhere = ("row", "col", "layer")
    swap = [(0, 1), (1, 0)]
    near, swapped = [], []
    for k in range(plan.grid // 2 - 1):
        bys = (2 * k + 1, 2 * k + 2)
        near.append(lax.ppermute(own, everywhere, plan.near_pairs(bys)))
        swapped.append(lax.ppermute(near[-1], "layer", swap))
    sent = pl.pallas_call(
        pick_kernel,
        out_shape=jax.ShapeDtypeStruct((share, size, size), own.dtype),
        in_specs=[vmem],
        out_specs=vmem,
        compiler_params=compiler_params,
        cost_estimate=cost(0, 1),
        name="pick_half",
    )(near[0])
    far = lax.ppermute(sent, everywhere, plan.far_pairs())
    far_swapped = lax.ppermute(far, "layer", swap)
    direct = [*own_parts, *near]
    lefts = [*direct, *swapped, far, far_swapped]
    parts = [len(r) for r in rights]
    running = jax.ShapeDtypeStruct((slots + 1, size, size), jnp.float32)
    before = [part for stage in rights[:-1] for part in stage]
    total = pl.pallas_call(
        functools.partial(early_kernel, plan, len(direct), parts),
        out_shape=running,
        in_specs=[scalars] + [vmem] * (len(direct) + len(before) - parts[-2]),
        out_specs=vmem,
        compiler_params=compiler_params,
        cost_estimate=cost(slots * plan.stages, 2 * plan.stages),
        name="early_products",
    )(lists, *direct, *before[: -parts[-2]])
    total = pl.pallas_call(
        functools.partial(second_kernel, plan, len(direct) + len(swapped), parts),
        out_shape=running,
        in_specs=[scalars]
        + [vmem] * (1 + len(direct) + len(swapped) + len(before)),
        out_specs=vmem,
        input_output_aliases={1: 0},
        compiler_params=compiler_params,
        cost_estimate=cost(slots, 2),
        name="second_products",
    )(lists, total, *direct, *swapped, *before)
    first, second = rights[-1]
    half = jax.ShapeDtypeStruct((share, size, size), jnp.float32)
    _, mine, other = pl.pallas_call(
        functools.partial(middle_kernel, plan, len(lefts), parts),
        out_shape=(running, half, half),
        in_specs=[scalars] + [vmem] * (2 + len(lefts) + len(before)),
        out_specs=(vmem, vmem, vmem),
        input_output_aliases={1: 0},
        compiler_params=compiler_params,
        cost_estimate=cost(slots * plan.stages, 2 * plan.stages),
        name="middle_products",
    )(lists, total, *lefts, *before, first)
    received = lax.ppermute(other, "layer", swap)
    second_swapped = lax.ppermute(second, "layer", swap)
    square = pl.pallas_call(
        functools.partial(last_kernel, plan, len(lefts), bounds[1]),
        out_shape=jax.ShapeDtypeStruct((share, size, size), jnp.bfloat16),
        in_specs=[scalars] + [vmem] * (4 + len(lefts)),
        out_specs=pl.BlockSpec(memory_space=pl.ANY),
        scratch_shapes=[
            pltpu.VMEM((share + 1, size, size), jnp.float32),
            pltpu.VMEM((share, size, size), jnp.bfloat16),
            pltpu.SemaphoreType.DMA((2,)),
        ],
        compiler_params=compiler_params,
        cost_estimate=cost(slots // 2, 4),
        name="last_products",
    )(lists, mine, received, *lefts, second, second_swapped)
    return square[None, None]


def solution(mesh):
    plan = Plan(mesh)

    def body(*args):
        return on_device(plan, *args)

    in_specs = (P("col", "row", None, None, None), P(), P())
    out_specs = P("col", "row", "layer", None, None)
    return jax.shard_map(
        body, mesh=mesh, in_specs=in_specs, out_specs=out_specs, check_vma=False
    )
```

```python
import functools

import jax
import jax.numpy as jnp
from jax import lax
from jax.experimental import pallas as pl
from jax.experimental.pallas import tpu as pltpu
from jax.sharding import PartitionSpec as P

TB = 28
GROUP = 8
LANES = 128
GRANT = 8 << 20
CHUNKS = 2


class Plan:
    def __init__(self, mesh):
        self.grid = mesh.shape["row"]
        self.half = min(6, self.grid) // 2
        self.whole = 2 * self.half == self.grid
        self.stages = self.grid - 1 if self.whole else self.half

    def shift(self, a, l):
        if self.whole:
            return l - a
        mid = self.grid // 2
        k = (l - a + mid) % self.grid - mid
        return k if -self.half <= k < self.half else None

    def hop_pairs(self, stage):
        pairs = []
        for source in range(self.grid):
            for layer, step in ((0, 1), (1, -1)):
                target = source + step
                origin = target - step * stage
                if self.whole and not (0 <= target < self.grid and 0 <= origin < self.grid):
                    continue
                target %= self.grid
                if self.shift(target, origin % self.grid) == -step * stage:
                    pairs.append((source * 2 + layer, target * 2 + layer))
        return pairs

    def near_pairs(self, bys):
        pairs = []
        for r in range(self.grid):
            for a in range(self.grid):
                if self.shift(a, r) is not None:
                    for layer, by in enumerate(bys):
                        pairs.append(
                            tuple(
                                (p * self.grid + a) * 2 + layer for p in (r, r ^ by)
                            )
                        )
        return pairs

    def far_pairs(self):
        far = self.grid - 1
        pairs = []
        for r in range(self.grid):
            for a in range(self.grid):
                if self.shift(a, r) is not None:
                    for layer, by in enumerate((1, 2)):
                        pairs.append(
                            tuple(
                                (p * self.grid + a) * 2 + layer
                                for p in (r ^ by, r ^ far)
                            )
                        )
        return pairs

    def taken(self, a, layer, stage):
        l = jnp.where(layer == 0, a - stage, a + stage)
        if self.whole:
            valid = (l >= 0) & (l < self.grid)
        else:
            valid = jnp.where(layer == 0, stage <= self.half, stage < self.half)
        if stage == 0:
            valid = valid & (layer == 0)
        l = jnp.where(l < 0, l + self.grid, l)
        return jnp.where(l >= self.grid, l - self.grid, l), valid


def late_core(plan, a):
    l, valid = plan.taken(a, jnp.int32(0), plan.stages)
    other_l, other_valid = plan.taken(a, jnp.int32(1), plan.stages)
    late = jnp.where(valid, 0, 1)
    return late, jnp.where(valid, l, other_l), valid | other_valid


def place():
    return tuple(lax.axis_index(n) for n in ("col", "row", "layer"))


def list_kernel(plan, bounds, slot_keys, pairs, keys, codes):
    slots = slot_keys.shape[2]
    stages = plan.stages + 2
    a, b, layer = place()
    lane = lax.broadcasted_iota(jnp.int32, (1, LANES), 1)
    down = lax.broadcasted_iota(jnp.int32, (LANES, LANES), 0)
    across = lax.broadcasted_iota(jnp.int32, (LANES, LANES), 1)

    keys[...] = jnp.full_like(keys, -1)
    jobs = [plan.taken(a, layer, stage) for stage in range(stages - 1)]
    jobs.append(late_core(plan, a)[1:])
    for stage, (l, valid) in enumerate(jobs):
        l = jnp.clip(l, 0, plan.grid - 1)
        keys[pl.ds(stage, 1), 0:slots] = slot_keys[a, pl.ds(l, 1), :]
        keys[pl.ds(stages + stage, 1), 0:slots] = slot_keys[l, pl.ds(b, 1), :]
    keys[pl.ds(2 * stages, 1), 0:slots] = slot_keys[a, pl.ds(b, 1), :]
    out = keys[pl.ds(2 * stages, 1), :]
    out = jnp.where(lane < LANES // 2, out, pltpu.roll(out, LANES // 2, 1))
    slot = lane % (LANES // 2)
    r, d = out // 2, out % 2
    after = jnp.where(r + 1 == TB, 0, r + 1)
    second = lane >= LANES // 2
    left_key = jnp.where(second, 2 * r + 1, 2 * r)
    right_key = jnp.where(second, jnp.where(d == 1, 2 * after, -2), out)
    wanted = slot < slots
    left_key = jnp.where(wanted, left_key, -2)
    right_key = jnp.where(wanted, right_key, -2)
    columns = keys[...].T

    def find(column, key):
        hit = columns[:, column : column + 1] == key
        return jnp.sum(jnp.where(hit, down + 1, 0), axis=0, keepdims=True)

    codes[...] = jnp.zeros_like(codes)
    share = slots // 2
    for stage, (_, valid) in enumerate(jobs):
        left, right = find(stage, left_key), find(stages + stage, right_key)
        good = (left > 0) & (right > 0) & valid
        if stage == plan.stages:
            good = good & (right <= bounds[1])
        if stage > plan.stages:
            low = layer * share
            good = good & (right > bounds[1]) & (slot >= low) & (slot < low + share)
        code = ((left - 1) * 64 + (right - 1)) * 64 + slot + 1
        codes[pl.ds(stage, 1), :] = jnp.where(good, code, 0)
    found = codes[...] > 0
    ahead = jnp.dot(
        found.astype(jnp.float32),
        (down < across).astype(jnp.float32),
        preferred_element_type=jnp.float32,
    ).astype(jnp.int32)
    order = jnp.where(found, ahead, -1).T
    entries = codes[...].T
    for stage in range(pairs.shape[0]):
        hit = order[:, stage : stage + 1] == across
        entry = jnp.where(hit, entries[:, stage : stage + 1], 0)
        entry = jnp.sum(entry, axis=0, keepdims=True)
        count = jnp.sum(
            found[stage : stage + 1].astype(jnp.int32), axis=1, keepdims=True
        )
        entry = jnp.where(lane < count, entry - 1, slots)
        pairs[pl.ds(stage, 1), :] = jnp.where(lane == LANES - 1, count, entry)


def add_products(count, pairs, row, left, right, acc, at, group):
    def step(i, carry):
        codes = [pairs[row, i * group + j] for j in range(group)]
        products = [
            jnp.dot(
                left(code // 4096),
                right((code // 64) % 64),
                preferred_element_type=jnp.float32,
            )
            for code in codes
        ]
        for code, product in zip(codes, products):
            acc[at(code % 64)] += product
        return carry

    lax.fori_loop(0, (count + group - 1) // group, step, 0)


def blocks_of(parts):
    if len(parts) == 1:
        return lambda slot: parts[0][slot]
    first, second = parts
    size = first.shape[0]

    def block(slot):
        return lax.select(
            slot < size,
            first[jnp.minimum(slot, size - 1)],
            second[jnp.maximum(slot - size, 0)],
        )

    return block


class Lefts:
    def __init__(self, plan, refs):
        near = plan.grid // 2 - 1
        self.far = plan.grid - 1
        self.own, refs = refs[:CHUNKS], refs[CHUNKS:]
        self.near, refs = refs[:near], refs[near:]
        self.swapped, self.halves = refs[:near], refs[near:]

    def all(self, by, layer):
        yield from self.direct(by, layer)
        yield from self.indirect(by, layer)
        yield from self.opposite(by, layer)

    def direct(self, by, layer):
        yield by == 0, blocks_of(self.own)
        for k, tile in enumerate(self.near):
            yield by == 2 * k + 1 + layer, blocks_of([tile])

    def indirect(self, by, layer):
        for k, tile in enumerate(self.swapped):
            yield by == 2 * k + 2 - layer, blocks_of([tile])

    def opposite(self, by, layer):
        mine, other = self.halves
        share = mine.shape[0]

        def block(slot):
            second = (slot >= share).astype(jnp.int32)
            slot = slot - second * share
            return lax.select(second == layer, mine[slot], other[slot])

        yield by == self.far, block


def run_jobs(
    cases, count, pairs, row, right, acc, at=lambda slot: slot, group=GROUP
):
    for here, left in cases:

        @pl.when(here & (count > 0))
        def _(left=left):
            add_products(count, pairs, row, left, right, acc, at, group)


def stages_of(parts, refs):
    rights = []
    for n in parts:
        rights.append(refs[:n])
        refs = refs[n:]
    return rights, refs


def early_kernel(plan, n, parts, pairs, *refs):
    lefts = Lefts(plan, refs[:n])
    rights, (acc,) = stages_of(parts[:-2], refs[n:])
    a, b, layer = place()
    acc[...] = jnp.zeros_like(acc)
    for stage, right in enumerate(rights):
        by = b ^ plan.taken(a, layer, stage)[0]
        count = pairs[stage, pairs.shape[1] - 1]
        cases = lefts.direct(by, layer)
        run_jobs(cases, count, pairs, stage, blocks_of(right), acc)


def second_kernel(plan, n, parts, pairs, total, *refs):
    del total
    lefts = Lefts(plan, refs[:n])
    rights, (acc,) = stages_of(parts[:-1], refs[n:])
    a, b, layer = place()
    for stage, right in enumerate(rights):
        by = b ^ plan.taken(a, layer, stage)[0]
        count = pairs[stage, pairs.shape[1] - 1]
        cases = list(lefts.indirect(by, layer))
        if stage == plan.stages - 1:
            cases += lefts.direct(by, layer)
        run_jobs(cases, count, pairs, stage, blocks_of(right), acc)


def split_kernel(tile, first, second, sem):
    size = first.shape[0]
    copies = [
        pltpu.make_async_copy(tile.at[pl.ds(0, size)], first, sem.at[0]),
        pltpu.make_async_copy(
            tile.at[pl.ds(size, second.shape[0])], second, sem.at[1]
        ),
    ]
    for copy in copies:
        copy.start()
    for copy in copies:
        copy.wait()


def pick_kernel(tile, half):
    share = half.shape[0]
    half[...] = tile[pl.ds(lax.axis_index("layer") * share, share)]


def middle_kernel(plan, n, parts, pairs, total, *refs):
    del total
    lefts = Lefts(plan, refs[:n])
    rights, (first, acc, mine, other) = stages_of(parts[:-1], refs[n:])
    a, b, layer = place()
    last = pairs.shape[1] - 1
    for stage, right in enumerate([*rights, [first]]):
        by = b ^ plan.taken(a, layer, stage)[0]
        cases = (lefts.all if stage == plan.stages else lefts.opposite)(by, layer)
        run_jobs(cases, pairs[stage, last], pairs, stage, blocks_of(right), acc)
    share = other.shape[0]
    mine[...] = acc[pl.ds(layer * share, share)]
    other[...] = acc[pl.ds((1 - layer) * share, share)]


def last_kernel(plan, n, low, pairs, mine, received, *refs):
    lefts = Lefts(plan, refs[:n])
    part, part_swapped, out, acc, rounded, sem = refs[n:]
    a, b, layer = place()
    share = out.shape[0]
    acc[pl.ds(0, share)] = mine[...] + received[...]
    late, l, _ = late_core(plan, a)
    by = b ^ l
    row = plan.stages + 1
    count = pairs[row, pairs.shape[1] - 1]
    for mine_is_late, source in ((True, part), (False, part_swapped)):

        def right(slot, source=source):
            return source[jnp.maximum(slot - low, 0)]

        run_jobs(
            lefts.all(by, layer),
            jnp.where((late == layer) == mine_is_late, count, 0),
            pairs,
            row,
            right,
            acc,
            lambda slot: jnp.minimum(slot - layer * share, share),
            GROUP // 2,
        )
    copies = []
    for j, (start, end) in enumerate(((0, share // 2), (share // 2, share))):
        here = pl.ds(start, end - start)
        rounded[here] = acc[here].astype(rounded.dtype)
        copies.append(pltpu.make_async_copy(rounded.at[here], out.at[here], sem.at[j]))
        copies[-1].start()
    for copy in copies:
        copy.wait()


def on_device(plan, x_blocks, slot_rows, slot_cols):
    own = x_blocks[0, 0]
    slots, size = own.shape[0], own.shape[1]
    share = slots // 2
    bounds = [slots * i // CHUNKS for i in range(CHUNKS + 1)]
    scalars = pl.BlockSpec(memory_space=pltpu.SMEM)
    vmem = pl.BlockSpec(memory_space=pltpu.VMEM)
    compiler_params = pltpu.CompilerParams(vmem_limit_bytes=GRANT)
    tile_bytes = own.size * 2

    def cost(products, tiles):
        return pl.CostEstimate(
            flops=2 * size**3 * products,
            bytes_accessed=tiles * tile_bytes,
            transcendentals=0,
        )

    held = pl.pallas_call(
        split_kernel,
        out_shape=[
            jax.ShapeDtypeStruct((j - i, size, size), own.dtype)
            for i, j in zip(bounds[:-1], bounds[1:])
        ],
        in_specs=[pl.BlockSpec(memory_space=pl.ANY)],
        out_specs=[vmem] * CHUNKS,
        scratch_shapes=[pltpu.SemaphoreType.DMA((CHUNKS,))],
        compiler_params=compiler_params,
        cost_estimate=cost(0, 2),
        name="split_tile",
    )(own)
    lists = pl.pallas_call(
        functools.partial(list_kernel, plan, bounds),
        out_shape=jax.ShapeDtypeStruct((plan.stages + CHUNKS, LANES), jnp.int32),
        in_specs=[vmem],
        out_specs=vmem,
        scratch_shapes=[pltpu.VMEM((LANES, LANES), jnp.int32)] * 2,
        compiler_params=compiler_params,
        cost_estimate=cost(0, 2),
        name="list_products",
    )(2 * slot_rows + (slot_cols != slot_rows))
    own_parts = list(held)
    rights = [own_parts]
    for stage in range(1, plan.stages + 1):
        pairs = plan.hop_pairs(stage)
        arrived = []
        for part in held:
            arrived.append(lax.ppermute(part, ("col", "layer"), pairs))
        rights.append(arrived)
        held = list(arrived)
    everywhere = ("row", "col", "layer")
    swap = [(0, 1), (1, 0)]
    near, swapped = [], []
    for k in range(plan.grid // 2 - 1):
        bys = (2 * k + 1, 2 * k + 2)
        near.append(lax.ppermute(own, everywhere, plan.near_pairs(bys)))
        swapped.append(lax.ppermute(near[-1], "layer", swap))
    sent = pl.pallas_call(
        pick_kernel,
        out_shape=jax.ShapeDtypeStruct((share, size, size), own.dtype),
        in_specs=[vmem],
        out_specs=vmem,
        compiler_params=compiler_params,
        cost_estimate=cost(0, 1),
        name="pick_half",
    )(near[0])
    far = lax.ppermute(sent, everywhere, plan.far_pairs())
    far_swapped = lax.ppermute(far, "layer", swap)
    direct = [*own_parts, *near]
    lefts = [*direct, *swapped, far, far_swapped]
    parts = [len(r) for r in rights]
    running = jax.ShapeDtypeStruct((slots + 1, size, size), jnp.float32)
    before = [part for stage in rights[:-1] for part in stage]
    total = pl.pallas_call(
        functools.partial(early_kernel, plan, len(direct), parts),
        out_shape=running,
        in_specs=[scalars] + [vmem] * (len(direct) + len(before) - parts[-2]),
        out_specs=vmem,
        compiler_params=compiler_params,
        cost_estimate=cost(slots * plan.stages, 2 * plan.stages),
        name="early_products",
    )(lists, *direct, *before[: -parts[-2]])
    total = pl.pallas_call(
        functools.partial(second_kernel, plan, len(direct) + len(swapped), parts),
        out_shape=running,
        in_specs=[scalars]
        + [vmem] * (1 + len(direct) + len(swapped) + len(before)),
        out_specs=vmem,
        input_output_aliases={1: 0},
        compiler_params=compiler_params,
        cost_estimate=cost(slots, 2),
        name="second_products",
    )(lists, total, *direct, *swapped, *before)
    first, second = rights[-1]
    half = jax.ShapeDtypeStruct((share, size, size), jnp.float32)
    _, mine, other = pl.pallas_call(
        functools.partial(middle_kernel, plan, len(lefts), parts),
        out_shape=(running, half, half),
        in_specs=[scalars] + [vmem] * (2 + len(lefts) + len(before)),
        out_specs=(vmem, vmem, vmem),
        input_output_aliases={1: 0},
        compiler_params=compiler_params,
        cost_estimate=cost(slots * plan.stages, 2 * plan.stages),
        name="middle_products",
    )(lists, total, *lefts, *before, first)
    received = lax.ppermute(other, "layer", swap)
    second_swapped = lax.ppermute(second, "layer", swap)
    square = pl.pallas_call(
        functools.partial(last_kernel, plan, len(lefts), bounds[1]),
        out_shape=jax.ShapeDtypeStruct((share, size, size), jnp.bfloat16),
        in_specs=[scalars] + [vmem] * (4 + len(lefts)),
        out_specs=pl.BlockSpec(memory_space=pl.ANY),
        scratch_shapes=[
            pltpu.VMEM((share + 1, size, size), jnp.float32),
            pltpu.VMEM((share, size, size), jnp.bfloat16),
            pltpu.SemaphoreType.DMA((2,)),
        ],
        compiler_params=compiler_params,
        cost_estimate=cost(slots // 2, 4),
        name="last_products",
    )(lists, mine, received, *lefts, second, second_swapped)
    return square[None, None]


def solution(mesh):
    plan = Plan(mesh)

    def body(*args):
        return on_device(plan, *args)

    in_specs = (P("col", "row", None, None, None), P(), P())
    out_specs = P("col", "row", "layer", None, None)
    return jax.shard_map(
        body, mesh=mesh, in_specs=in_specs, out_specs=out_specs, check_vma=False
    )
```
